32 devices in a mesh: fsdp: 8 (over z, x), seq: 4 (over y, core).
Axes of the slice: x: 2, y: 2, z: 4, core: 2. Of those that a mesh axis runs over, the one named last changes fastest.
Arguments:
- tokens: bfloat16 [32768, 1024], P(('fsdp', 'seq')), may hold values from -6 to 6
- cotangent: bfloat16 [32768, 1024], P(('fsdp', 'seq')), may hold values from -6 to 6
- query_weight: bfloat16 [1024, 1024], P('fsdp'), may hold values from -0.1875 to 0.1875
- key_weight: bfloat16 [1024, 1024], P('fsdp'), may hold values from -0.1875 to 0.1875
- value_weight: bfloat16 [1024, 1024], P('fsdp'), may hold values from -0.1875 to 0.1875
- output_weight: bfloat16 [1024, 1024], P('fsdp'), may hold values from -6 to 6
- gate_weight: bfloat16 [1024, 2816], P('fsdp'), may hold values from -0.1875 to 0.1875
- up_weight: bfloat16 [1024, 2816], P('fsdp'), may hold values from -0.1875 to 0.1875
- down_weight: bfloat16 [2816, 1024], P(None, 'fsdp'), may hold values from -0.109375 to 0.109375
- attention_gain: bfloat16 [1024], P('fsdp'), may hold values from 0.5 to 1.5
- feedforward_gain: bfloat16 [1024], P('fsdp'), may hold values from 0.5 to 1.5
- cache_keys: bfloat16 [8, 8, 2048, 128], P('fsdp', 'seq'), may hold values from -6 to 6
- cache_values: bfloat16 [8, 8, 2048, 128], P('fsdp', 'seq'), may hold values from -6 to 6
- memory_rows: int32 [8, 8, 32, 128], P('fsdp', 'seq'), may hold values from 0 to 2047
- memory_docs: int32 [8, 8, 32, 128], P('fsdp', 'seq'), may hold values from 0 to 1
Outputs:
- result: bfloat16 [32768, 1024], P(('fsdp', 'seq'))
- grad_tokens: bfloat16 [32768, 1024], P(('fsdp', 'seq'))
- grad_query_weight: float32 [1024, 1024], P('fsdp')
- grad_key_weight: float32 [1024, 1024], P('fsdp')
- grad_value_weight: float32 [1024, 1024], P('fsdp')
- grad_output_weight: float32 [1024, 1024], P('fsdp')
- grad_gate_weight: float32 [1024, 2816], P('fsdp')
- grad_up_weight: float32 [1024, 2816], P('fsdp')
- grad_down_weight: float32 [2816, 1024], P(None, 'fsdp')
- grad_attention_gain: float32 [1024], P('fsdp')
- grad_feedforward_gain: float32 [1024], P('fsdp')
The draws below stay inside these ranges and needn't reach their ends.
Inputs may be any that keep to these rules, and one draw needn't show every extreme that they name: `memory_rows`: a row of a cache of 2048 rows. `memory_docs`: 0 picks the sequence's own cache, 1 the cache of the sequence before it in the batch (the last sequence for the first).
All inputs are finite; a program needn't handle non-finite values.
Results may differ from the reference program's by a relative error of at most 0.018.
Values may be sent and summed in bfloat16 or wider, within the bound.
No kernel may reach another device: no remote copies, remote signals or barrier semaphores. Data moves between devices by JAX's collectives and lax.ppermute only.
A program may use at most 384 MiB of HBM per device.

```python
import jax
import jax.numpy as jnp
from jax import lax

D = 1024
HEADS = 8
HD = 128
FF = 2816
CROWS = 2048
MBLK = 128
MEM = 128
SEQ_LEN = 4096
SEQS = 8
TOKENS = 32768
NBLK = 32


def set_ends(drawn, rng, low, high):
    index_at = [jax.random.randint(jax.random.fold_in(rng, axis), (), 0, length) for axis, length in enumerate(drawn.shape)]
    widest = drawn.shape.index(max(drawn.shape))
    neighbour = index_at[:widest] + [(index_at[widest] + 1) % drawn.shape[widest]] + index_at[widest + 1:]
    return drawn.at[tuple(index_at)].set(low).at[tuple(neighbour)].set(high)


def with_spikes(entries, rng, source, target, parts, factor):
    def block_of(position):
        return (jnp.arange(entries.shape[position]) // (entries.shape[position] // parts)).reshape((-1,) + (1,) * (entries.ndim - 1 - position))

    near = jax.random.permutation(rng, parts)[block_of(target)]
    second = (block_of(target) + parts // 2) % parts
    return jnp.where((block_of(source) == near) | (block_of(source) == second), factor * entries, entries)


def shard_levels(key, dims, split, smallest, high):
    level, own = 1.0, jax.random.fold_in(key, 6)
    for position, blocks in split:
        draws = jnp.exp(jax.random.uniform(jax.random.fold_in(own, position), (blocks,), jnp.float32, smallest / len(split), high / len(split)))
        level = level * jnp.repeat(draws, dims[position] // blocks).reshape([-1 if axis == position else 1 for axis in range(len(dims))])
    return level


def normal_values(stream_key, extent, spread, limit, shards=(), kind=jnp.bfloat16):
    array = jax.random.normal(stream_key, extent, jnp.float32) * spread
    if len(shards) > 0:
        array = shard_levels(stream_key, extent, shards, -0.22, 0.18) * array
    return jnp.clip(array, min=-limit, max=limit).astype(kind)


def noise_with(own_key, shape, deviation, limit, shards, heavy, held_as=jnp.bfloat16):
    entries = deviation * jax.random.normal(own_key, shape, jnp.float32)
    if shards:
        entries = entries * shard_levels(own_key, shape, shards, -0.22, 0.18)
    return jnp.clip(with_spikes(entries, jax.random.fold_in(own_key, 3), *heavy), -limit, limit).astype(held_as)


def setup_inputs(seed: int = 0) -> dict:
    keys = jax.random.split(jax.random.key(seed), 16)
    tokens = normal_values(keys[0], (TOKENS, D), 1.0, 6.0, ((0, 32),))
    cotangent = noise_with(keys[1], (TOKENS, D), 1.0, 6.0, ((0, 32),), (0, 1, 32, 2.75))
    query_weight = normal_values(keys[2], (D, D), D ** -0.5, 0.1875, ((0, 8),))
    key_weight = normal_values(keys[3], (D, D), D ** -0.5, 0.1875, ((0, 8),))
    value_weight = normal_values(keys[4], (D, D), D ** -0.5, 0.1875, ((0, 8),))
    output_weight = normal_values(keys[5], (D, D), (max(1, 2 * D // SEQ_LEN)) ** -0.5, 6.0, ((0, 8),))
    gate_weight = normal_values(keys[6], (D, FF), D ** -0.5, 0.1875, ((0, 8),))
    up_weight = normal_values(keys[7], (D, FF), D ** -0.5, 0.1875, ((0, 8),))
    down_weight = normal_values(keys[8], (FF, D), FF ** -0.5, 0.109375, ((1, 8),))
    attention_gain = jnp.clip(1.0 + 0.1 * jax.random.normal(keys[9], (D,), jnp.float32), 0.5, 1.5).astype(jnp.bfloat16)
    feedforward_gain = jnp.clip(1.0 + 0.1 * jax.random.normal(keys[10], (D,), jnp.float32), 0.5, 1.5).astype(jnp.bfloat16)
    cache_keys = normal_values(keys[11], (SEQS, HEADS, CROWS, HD), 1.0, 6.0, ((0, 8), (1, 4)))
    cache_values = normal_values(keys[12], (SEQS, HEADS, CROWS, HD), 1.0, 6.0, ((0, 8), (1, 4)))
    memory_rows = set_ends(jax.random.randint(keys[13], (SEQS, HEADS, NBLK, MEM), 0, CROWS), jax.random.fold_in(keys[13], 1), 0, CROWS - 1).astype(jnp.int32)
    memory_docs = set_ends(jax.random.randint(keys[14], (SEQS, HEADS, NBLK, MEM), 0, 2), jax.random.fold_in(keys[14], 1), 0, 1).astype(jnp.int32)
    return {"tokens": tokens, "cotangent": cotangent, "query_weight": query_weight, "key_weight": key_weight, "value_weight": value_weight, "output_weight": output_weight, "gate_weight": gate_weight, "up_weight": up_weight, "down_weight": down_weight, "attention_gain": attention_gain, "feedforward_gain": feedforward_gain, "cache_keys": cache_keys, "cache_values": cache_values, "memory_rows": memory_rows, "memory_docs": memory_docs}


@jax.custom_vjp
def low(v):
    return lax.optimization_barrier(v.astype(jnp.bfloat16)).astype(jnp.float32)

@jax.custom_vjp
def low_back(v):
    return v

def low_keep(v):
    return (low(v), None)

def low_pass(kept, grad):
    return (grad,)

def back_keep(v):
    return (v, None)

def back_low(kept, grad):
    return (low(grad),)
low.defvjp(low_keep, low_pass)
low_back.defvjp(back_keep, back_low)
epsilon = 1e-06
highest = lax.Precision.HIGHEST

def rms_scale(values, gain_row):
    return values * lax.rsqrt(lax.optimization_barrier(jnp.mean(values * values, axis=-1, keepdims=True)) + epsilon) * gain_row

def rotate(tensor, positions, direction):
    half_dim = tensor.shape[-1] // 2
    frequency = 10000.0 ** (-2.0 * jnp.arange(half_dim, dtype=jnp.float32) / tensor.shape[-1])
    angles = positions.astype(jnp.float32)[:, None] * frequency[None, :]
    cosine = jnp.cos(angles)[:, None, :]
    sine_table = direction * jnp.sin(angles)[:, None, :]
    first_half = tensor[..., :half_dim]
    second_half = tensor[..., half_dim:]
    return jnp.concatenate([first_half * cosine - second_half * sine_table, second_half * cosine + first_half * sine_table], axis=-1)

def product(first_op, second_op):
    return jnp.dot(first_op, second_op, precision=highest)

def sequence_forward(inputs, weights, picked_keys, picked_values):
    query_weight, key_weight, value_weight, output_weight, gate_weight, up_weight, down_weight, attention_gain, feedforward_gain = weights
    positions = jnp.arange(SEQ_LEN, dtype=jnp.int32)
    normed_one = low(rms_scale(inputs, attention_gain))
    query_lin = low_back(product(normed_one, query_weight)).reshape(SEQ_LEN, HEADS, HD)
    key_lin = low_back(product(normed_one, key_weight)).reshape(SEQ_LEN, HEADS, HD)
    query_heads = low_back(low(rotate(query_lin, positions, 1.0)))
    key_heads = low_back(low(rotate(key_lin, positions, 1.0)))
    value_heads = low_back(low(product(normed_one, value_weight))).reshape(SEQ_LEN, HEADS, HD)
    block_rows = min(512, SEQ_LEN)
    group_count = block_rows // MBLK
    score_scale = HD ** (-0.5)

    def attend(block_index):
        row_start = block_index * block_rows
        query_slab = lax.dynamic_slice_in_dim(query_heads, row_start, block_rows, 0)
        local_scores = low_back(jnp.einsum('qhd,khd->hqk', query_slab, key_heads, precision=highest) * score_scale)
        query_positions = row_start + jnp.arange(block_rows, dtype=jnp.int32)
        causal = positions[None, :] <= query_positions[:, None]
        local_scores = jnp.where(causal[None], local_scores, -jnp.inf)
        memory_keys = lax.dynamic_slice_in_dim(picked_keys, block_index * group_count, group_count, 1)
        memory_values = lax.dynamic_slice_in_dim(picked_values, block_index * group_count, group_count, 1)
        grouped = query_slab.reshape(group_count, MBLK, HEADS, HD)
        memory_scores = low_back(jnp.einsum('bqhd,hbmd->hbqm', grouped, memory_keys, precision=highest) * score_scale)
        memory_scores = memory_scores.reshape(HEADS, block_rows, MEM)
        probabilities = low(jax.nn.softmax(jnp.concatenate([local_scores, memory_scores], axis=-1), axis=-1))
        local_part = jnp.einsum('hqk,khd->qhd', probabilities[..., :SEQ_LEN], value_heads, precision=highest)
        memory_probs = probabilities[..., SEQ_LEN:].reshape(HEADS, group_count, MBLK, MEM)
        memory_part = jnp.einsum('hbqm,hbmd->bqhd', memory_probs, memory_values, precision=highest).reshape(block_rows, HEADS, HD)
        return local_part + memory_part
    attended = lax.map(jax.checkpoint(attend), jnp.arange(SEQ_LEN // block_rows, dtype=jnp.int32))
    attended = attended.reshape(SEQ_LEN, HEADS * HD)
    mixed = low_back(low(attended))
    residual = inputs + low_back(product(mixed, output_weight))
    normed_two = low(rms_scale(residual, feedforward_gain))
    gate_lin = low_back(product(normed_two, gate_weight))
    up_lin = low_back(product(normed_two, up_weight))
    hidden = low(jax.nn.silu(gate_lin) * up_lin)
    return residual + product(hidden, down_weight)

def reference(tokens, cotangent, query_weight, key_weight, value_weight, output_weight, gate_weight, up_weight, down_weight, attention_gain, feedforward_gain, cache_keys, cache_values, memory_rows, memory_docs):
    float_weights = tuple((weight_item.astype(jnp.float32) for weight_item in (query_weight, key_weight, value_weight, output_weight, gate_weight, up_weight, down_weight, attention_gain, feedforward_gain)))
    key_table = jnp.concatenate([cache_keys, jnp.roll(cache_keys, 1, axis=0)], axis=2).astype(jnp.float32)
    value_table = jnp.concatenate([cache_values, jnp.roll(cache_values, 1, axis=0)], axis=2).astype(jnp.float32)
    chosen_rows = (memory_docs * CROWS + memory_rows).astype(jnp.int32)
    picker = jax.vmap(jax.vmap(lambda source, chosen: source[chosen]))
    picked_keys = picker(key_table, chosen_rows)
    picked_values = picker(value_table, chosen_rows)
    inputs = tokens.astype(jnp.float32).reshape(SEQS, SEQ_LEN, D)

    def whole_layer(layer_inputs, layer_weights):

        def per_sequence(bundle):
            return jax.checkpoint(sequence_forward)(bundle[0], layer_weights, bundle[1], bundle[2])
        return lax.map(per_sequence, (layer_inputs, picked_keys, picked_values))
    outputs, pullback = jax.vjp(whole_layer, inputs, float_weights)
    grad_inputs, grad_weights = pullback(cotangent.astype(jnp.float32).reshape(SEQS, SEQ_LEN, D))
    return (outputs.reshape(TOKENS, D).astype(jnp.bfloat16), grad_inputs.reshape(TOKENS, D).astype(jnp.bfloat16), grad_weights[0], grad_weights[1], grad_weights[2], grad_weights[3], grad_weights[4], grad_weights[5], grad_weights[6], grad_weights[7], grad_weights[8])
```

```python
import functools

import jax
import jax.numpy as jnp
from jax import lax
from jax.experimental import pallas as pl
from jax.experimental.pallas import tpu as pltpu
from jax.sharding import PartitionSpec as P

epsilon = 1e-06
log2e = 1.4426950408889634
f32 = jnp.float32
bf16 = jnp.bfloat16
VMEM_LIMIT = 60 * 1024 * 1024


def dot(a, b):
    return jnp.dot(a, b, preferred_element_type=f32)


def dot_nt(a, b):
    return lax.dot_general(a, b, (((1,), (1,)), ((), ())), preferred_element_type=f32)


def dot_tn(a, b):
    return lax.dot_general(a, b, (((0,), (0,)), ((), ())), preferred_element_type=f32)


def call(kernel, grid, in_specs, out_specs, out_shape, flops, bytes_accessed, scratch=(), prefetch=0):
    return pl.pallas_call(
        kernel,
        grid_spec=pltpu.PrefetchScalarGridSpec(
            num_scalar_prefetch=prefetch,
            grid=grid,
            in_specs=in_specs,
            out_specs=out_specs,
            scratch_shapes=list(scratch),
        ),
        out_shape=out_shape,
        compiler_params=pltpu.CompilerParams(
            dimension_semantics=("arbitrary",) * len(grid), vmem_limit_bytes=VMEM_LIMIT
        ),
        cost_estimate=pl.CostEstimate(
            flops=int(flops), bytes_accessed=int(bytes_accessed), transcendentals=0
        ),
    )


def resident(shape, index):
    return pl.BlockSpec(shape, lambda *_: index, pipeline_mode=pl.Buffered(1))


def struct(shape, dtype):
    return jax.ShapeDtypeStruct(shape, dtype)


def swap_seq(array, bit):
    count = lax.axis_size("seq")
    return lax.ppermute(array, "seq", [(i, i ^ bit) for i in range(count)])


def spread(array, axis):
    count = lax.axis_size(axis)
    copies = jnp.broadcast_to(array[None], (count,) + array.shape)
    return lax.all_to_all(copies, axis, split_axis=0, concat_axis=0, tiled=True)


def project(order, pieces, weights, gain_row, cosine, sine, head_local, head_dim):
    rows, width = pieces[0].shape
    count = len(pieces)
    block = min(256, rows)
    steps = rows // block
    length = rows * count
    cols = weights.shape[1]
    group = head_local * head_dim

    def kernel(order_ref, *refs):
        xs = refs[:count]
        w_ref, g_ref, c_ref, s_ref, q_ref, k_ref, v_ref, nt_ref = refs[count:]
        slot = pl.program_id(0)

        def run(x_ref):
            x = x_ref[...].astype(f32)
            scale = lax.rsqrt(jnp.mean(x * x, axis=-1, keepdims=True) + epsilon)
            normed = (x * scale * g_ref[...]).astype(bf16)
            nt_ref[...] = normed.T
            lin = dot(normed, w_ref[...])
            cos, sin = c_ref[...], s_ref[...]
            for head in range(head_local):
                for part, out in ((0, q_ref), (1, k_ref)):
                    start = part * group + head * head_dim
                    u = lin[:, start : start + head_dim]
                    out[head] = (u * cos + pltpu.roll(u, head_dim // 2, 1) * sin).astype(bf16)
                start = 2 * group + head * head_dim
                v_ref[head] = lin[:, start : start + head_dim].astype(bf16)

        for k in range(count):
            pl.when(slot == k)(functools.partial(run, xs[k]))

    def piece_spec(k):
        return pl.BlockSpec(
            (block, width),
            lambda slot, i, order_ref: (
                jnp.where(slot == k, i, jnp.where(slot < k, 0, steps - 1)),
                0,
            ),
        )

    def at_rows(slot, i, order_ref):
        return order_ref[slot] * steps + i

    head_spec = pl.BlockSpec((head_local, block, head_dim), lambda *a: (0, at_rows(*a), 0))
    table_spec = pl.BlockSpec((block, head_dim), lambda *a: (at_rows(*a), 0))
    heads = struct((head_local, length, head_dim), bf16)
    return call(
        kernel,
        (count, steps),
        [piece_spec(k) for k in range(count)]
        + [resident((width, cols), (0, 0)), resident((1, width), (0, 0)), table_spec, table_spec],
        [head_spec, head_spec, head_spec, pl.BlockSpec((width, block), lambda *a: (0, at_rows(*a)))],
        [heads, heads, heads, struct((width, length), bf16)],
        2 * length * width * cols,
        4 * length * width + 2 * length * cols + 8 * length * head_dim,
        prefetch=1,
    )(order, *pieces, weights, gain_row, cosine, sine)


def retrieve(chosen, keys, values, base, before=None):
    head_local, rows_cache, head_dim = keys.shape
    blocks, slots = chosen.shape[1:]
    per = min(4, blocks)
    total = blocks * slots

    def kernel(c_ref, k_ref, v_ref, *refs):
        if before is not None:
            bk_ref, bv_ref = refs[:2]
        ok_ref, ov_ref, table, mask = refs[-4:]

        @pl.when(pl.program_id(1) == 0)
        def _():
            table[:, :head_dim] = k_ref[0]
            table[:, head_dim:] = v_ref[0]

        for b in range(per):
            row = c_ref[0, 0, b : b + 1, :] - base
            column = jnp.broadcast_to(row, (slots, slots)).T
            lane = lax.broadcasted_iota(jnp.int32, (slots, slots), 1)
            for start in range(0, rows_cache, slots):
                mask[b * slots : (b + 1) * slots, start : start + slots] = jnp.where(
                    column == lane + start, 1.0, 0.0
                ).astype(bf16)
        picked = dot(mask[...], table[...])
        if before is not None:
            picked_keys = picked[:, :head_dim] + bk_ref[0].astype(f32)
            picked_values = picked[:, head_dim:] + bv_ref[0].astype(f32)
        else:
            picked_keys, picked_values = picked[:, :head_dim], picked[:, head_dim:]
        ok_ref[0] = picked_keys.astype(bf16)
        ov_ref[0] = picked_values.astype(bf16)

    out_spec = pl.BlockSpec((1, per * slots, head_dim), lambda h, i: (h, i, 0))
    table_spec = pl.BlockSpec((1, rows_cache, head_dim), lambda h, i: (h, 0, 0))
    extra = () if before is None else before
    out = struct((head_local, total, head_dim), bf16)
    return call(
        kernel,
        (head_local, blocks // per),
        [pl.BlockSpec((1, 1, per, slots), lambda h, i: (h, i, 0, 0)), table_spec, table_spec]
        + [out_spec] * len(extra),
        [out_spec, out_spec],
        [out, out],
        4 * head_local * total * rows_cache * head_dim,
        8 * head_local * total * head_dim,
        scratch=[
            pltpu.VMEM((rows_cache, 2 * head_dim), bf16),
            pltpu.VMEM((per * slots, rows_cache), bf16),
        ],
    )(chosen.reshape(head_local, blocks // per, per, slots), keys, values, *extra)


def attend(query, key, value, memory_keys, memory_values, mem_block, mem_count):
    head_local, length, head_dim = query.shape
    block = min(512, length)
    count = length // block
    groups = block // mem_block
    factor = head_dim ** (-0.5) * log2e

    def kernel(q_ref, k_ref, v_ref, mk_ref, mv_ref, o_ref, lse_ref):
        index = pl.program_id(0)
        row = lax.broadcasted_iota(jnp.int32, (block, block), 0)
        col = lax.broadcasted_iota(jnp.int32, (block, block), 1)

        def memory(head):
            parts = []
            for g in range(groups):
                q = q_ref[head, g * mem_block : (g + 1) * mem_block, :]
                parts.append(dot_nt(q, mk_ref[head, g * mem_count : (g + 1) * mem_count, :]))
            scores = jnp.concatenate(parts, axis=0) * factor
            top = jnp.max(scores, axis=-1, keepdims=True)
            weight = jnp.exp2(scores - top)
            total = jnp.sum(weight, axis=-1, keepdims=True)
            weight = weight.astype(bf16)
            mixed = jnp.concatenate(
                [
                    dot(
                        weight[g * mem_block : (g + 1) * mem_block],
                        mv_ref[head, g * mem_count : (g + 1) * mem_count, :],
                    )
                    for g in range(groups)
                ],
                axis=0,
            )
            return top, total, mixed

        def step(head, carry, start, masked):
            top, total, mixed = carry
            scores = dot_nt(q_ref[head], k_ref[head, pl.ds(start, block), :]) * factor
            if masked:
                scores = jnp.where(col <= row, scores, -jnp.inf)
            new_top = jnp.maximum(top, jnp.max(scores, axis=-1, keepdims=True))
            decay = jnp.exp2(top - new_top)
            weight = jnp.exp2(scores - new_top)
            total = total * decay + jnp.sum(weight, axis=-1, keepdims=True)
            mixed = mixed * decay + dot(weight.astype(bf16), v_ref[head, pl.ds(start, block), :])
            return new_top, total, mixed

        def both(carries, start, masked):
            return tuple(step(head, carries[head], start, masked) for head in range(head_local))

        carries = tuple(memory(head) for head in range(head_local))
        carries = lax.fori_loop(
            0, index, lambda j, c: both(c, pl.multiple_of(j * block, block), False), carries
        )
        carries = both(carries, pl.multiple_of(index * block, block), True)
        for head, (top, total, mixed) in enumerate(carries):
            o_ref[:, head * head_dim : (head + 1) * head_dim] = (mixed / total).astype(bf16)
            lse = jnp.broadcast_to(top + jnp.log2(total), (block, head_dim))
            lse_ref[0, head : head + 1, :] = lse.T[0:1, :]

    full = resident((head_local, length, head_dim), (0, 0, 0))
    rows = pl.BlockSpec((head_local, block, head_dim), lambda i: (0, i, 0))
    mem_rows = pl.BlockSpec((head_local, groups * mem_count, head_dim), lambda i: (0, i, 0))
    return call(
        kernel,
        (count,),
        [rows, full, full, mem_rows, mem_rows],
        [
            pl.BlockSpec((block, head_local * head_dim), lambda i: (i, 0)),
            pl.BlockSpec((1, 8, block), lambda i: (i, 0, 0)),
        ],
        [struct((length, head_local * head_dim), bf16), struct((count, 8, block), f32)],
        4 * head_local * length * length * head_dim,
        12 * head_local * length * head_dim,
    )(query, key, value, memory_keys, memory_values)


def attend_back(
    query, key, value, memory_keys, memory_values, mem_block, mem_count, grad, attended, lse, cosine, sine
):
    head_local, length, head_dim = query.shape
    count, _, block = lse.shape
    groups = block // mem_block
    scale = head_dim ** (-0.5)
    factor = scale * log2e

    def kernel(
        q_ref, k_ref, v_ref, mk_ref, mv_ref, do_ref, o_ref, lse_ref, c_ref, s_ref,
        dq_ref, dk_ref, dv_ref, dq_acc, delta,
    ):
        index = pl.program_id(0)

        def cols(head):
            return slice(head * head_dim, (head + 1) * head_dim)

        @pl.when(index == 0)
        def _():
            def prepare(i, _):
                start = pl.multiple_of(i * block, block)
                for head in range(head_local):
                    do = do_ref[pl.ds(start, block), cols(head)]
                    o = o_ref[pl.ds(start, block), cols(head)]
                    row = jnp.sum((do.astype(f32) * o.astype(f32)).T, axis=0, keepdims=True)
                    delta[i, head : head + 1, :] = row
                    lse_row = lse_ref[i, head : head + 1, :]
                    q = q_ref[head, pl.ds(start, block), :]
                    mem_start = pl.multiple_of(i * (groups * mem_count), groups * mem_count)
                    for g in range(groups):
                        lanes = slice(g * mem_block, (g + 1) * mem_block)
                        mk = mk_ref[head, pl.ds(mem_start + g * mem_count, mem_count), :]
                        mv = mv_ref[head, pl.ds(mem_start + g * mem_count, mem_count), :]
                        weight = jnp.exp2(dot_nt(mk, q[lanes]) * factor - lse_row[:, lanes])
                        dp = dot_nt(mv, do[lanes])
                        ds = (weight * (dp - row[:, lanes])).astype(bf16)
                        dq_acc[head, pl.ds(start + g * mem_block, mem_block), :] = dot_tn(ds, mk)
                return 0

            lax.fori_loop(0, count, prepare, 0)

        row_id = lax.broadcasted_iota(jnp.int32, (block, block), 0)
        col_id = lax.broadcasted_iota(jnp.int32, (block, block), 1)

        def step(head, carry, i, masked):
            dk, dv = carry
            start = pl.multiple_of(i * block, block)
            q = q_ref[head, pl.ds(start, block), :]
            do = do_ref[pl.ds(start, block), cols(head)]
            k, v = k_ref[head], v_ref[head]
            weight = jnp.exp2(dot_nt(k, q) * factor - lse_ref[i, head : head + 1, :])
            if masked:
                weight = jnp.where(row_id <= col_id, weight, 0.0)
            dp = dot_nt(v, do)
            ds = (weight * (dp - delta[i, head : head + 1, :])).astype(bf16)
            dv = dv + dot(weight.astype(bf16), do)
            dk = dk + dot(ds, q)
            dq_acc[head, pl.ds(start, block), :] += dot_tn(ds, k)
            return dk, dv

        def both(carries, i, masked):
            return tuple(step(head, carries[head], i, masked) for head in range(head_local))

        zero = jnp.zeros((block, head_dim), f32)
        carries = both(tuple((zero, zero) for _ in range(head_local)), index, True)
        carries = lax.fori_loop(index + 1, count, lambda i, c: both(c, i, False), carries)
        cos, sin = c_ref[...], s_ref[...]

        def unrotate(grad_rows):
            u = (grad_rows * scale).astype(bf16).astype(f32)
            return (u * cos - pltpu.roll(u, head_dim // 2, 1) * sin).astype(bf16)

        for head, (dk, dv) in enumerate(carries):
            start = pl.multiple_of(index * block, block)
            dq_ref[:, cols(head)] = unrotate(dq_acc[head, pl.ds(start, block), :])
            dk_ref[:, cols(head)] = unrotate(dk)
            dv_ref[:, cols(head)] = dv.astype(bf16)

    group = head_local * head_dim
    full = resident((head_local, length, head_dim), (0, 0, 0))
    mem_full = resident(memory_keys.shape, (0, 0, 0))
    flat = resident((length, group), (0, 0))
    rows = pl.BlockSpec((head_local, block, head_dim), lambda i: (0, i, 0))
    table = pl.BlockSpec((block, head_dim), lambda i: (i, 0))
    out_rows = pl.BlockSpec((block, group), lambda i: (i, 0))
    out = struct((length, group), bf16)
    return call(
        kernel,
        (count,),
        [full, rows, rows, mem_full, mem_full, flat, flat, resident(lse.shape, (0, 0, 0)), table, table],
        [out_rows, out_rows, out_rows],
        [out, out, out],
        10 * head_local * length * length * head_dim // 2,
        24 * head_local * length * head_dim,
        scratch=[
            pltpu.VMEM((head_local, length, head_dim), f32),
            pltpu.VMEM((count, 8, block), f32),
        ],
    )(query, key, value, memory_keys, memory_values, grad, attended, lse, cosine, sine)


def mix(attended, weights, tokens, gain_row):
    count, rows, group = attended.shape
    width = tokens.shape[1]
    block = min(256, rows)

    def kernel(a_ref, w_ref, x_ref, g_ref, res_ref, n_ref, nt_ref, at_ref):
        total = x_ref[...].astype(f32)
        mixed = dot(a_ref[0], w_ref[0:group, :])
        for k in range(1, count):
            mixed = mixed + dot(a_ref[k], w_ref[k * group : (k + 1) * group, :])
        for k in range(count):
            at_ref[k * group : (k + 1) * group, :] = a_ref[k].T
        residual = total + mixed
        scale = lax.rsqrt(jnp.mean(residual * residual, axis=-1, keepdims=True) + epsilon)
        normed = (residual * scale * g_ref[...]).astype(bf16)
        res_ref[...] = residual
        n_ref[...] = normed
        nt_ref[...] = normed.T

    rows_spec = pl.BlockSpec((block, width), lambda i: (i, 0))
    cols_spec = pl.BlockSpec((width, block), lambda i: (0, i))
    return call(
        kernel,
        (rows // block,),
        [
            pl.BlockSpec((count, block, group), lambda i: (0, i, 0)),
            resident((count * group, width), (0, 0)),
            rows_spec,
            resident((1, width), (0, 0)),
        ],
        [rows_spec, rows_spec, cols_spec, cols_spec],
        [struct((rows, width), f32), struct((rows, width), bf16)]
        + [struct((width, rows), bf16)] * 2,
        2 * rows * width * width,
        16 * rows * width,
    )(attended, weights, tokens, gain_row)


def gated(normed, cotangent, weights, first, hidden_cols):
    rows, width = normed.shape
    block = 256

    def kernel(n_ref, c_ref, wg_ref, wu_ref, wd_ref, h_ref, gg_ref, gu_ref):
        normed_block = n_ref[...]
        gate = dot(normed_block, wg_ref[...])
        up = dot(normed_block, wu_ref[...])
        grad = dot(c_ref[...], wd_ref[...])
        sg = 1.0 / (1.0 + jnp.exp(-gate))
        silu = gate * sg
        h_ref[...] = (silu * up).astype(bf16)
        gg_ref[...] = (grad * up * sg * (1.0 + gate * (1.0 - sg))).astype(bf16)
        gu_ref[...] = (grad * silu).astype(bf16)

    def weight_spec(k):
        offset = (first + k * hidden_cols) // block
        return pl.BlockSpec((width, block), lambda i: (0, i + offset))

    flat = resident((rows, width), (0, 0))
    out_spec = pl.BlockSpec((rows, block), lambda i: (0, i))
    return call(
        kernel,
        (hidden_cols // block,),
        [flat, flat] + [weight_spec(k) for k in range(3)],
        [out_spec] * 3,
        [struct((rows, hidden_cols), bf16)] * 3,
        6 * rows * width * hidden_cols,
        6 * (rows + width) * hidden_cols,
    )(normed, cotangent, weights, weights, weights)


def norm_back(grads, weight_arrays, parts, wo, residual, cotangent, gain_row, count):
    rows, width = residual.shape
    block = min(256, rows)
    steps = width // block
    row_steps = rows // block
    group = width // count
    n_grads = len(grads)

    def kernel(*refs):
        g_refs, w_refs = refs[:n_grads], refs[n_grads : 2 * n_grads]
        wo_ref, r_ref, c_ref, gain_ref, gres_ref, gb_ref, gm_ref, gg_ref, acc = refs[2 * n_grads :]
        step = pl.program_id(0)

        @pl.when(step < steps)
        def _():
            total = dot_nt(g_refs[0][...], w_refs[0][...])
            for k in range(1, n_grads):
                total = total + dot_nt(g_refs[k][...], w_refs[k][...])
            for d in range(steps):
                @pl.when(step == d)
                def _():
                    acc[:, d * block : (d + 1) * block] = total

        @pl.when(step >= steps)
        def _():
            start = pl.multiple_of((step - steps) * block, block)
            grad = acc[pl.ds(start, block), :]
            res = r_ref[...]
            scale = lax.rsqrt(jnp.mean(res * res, axis=-1, keepdims=True) + epsilon)
            unit = res * scale
            scaled = grad * gain_ref[...]
            inner = jnp.mean(scaled * unit, axis=-1, keepdims=True)
            gres = c_ref[...].astype(f32) + scale * (scaled - unit * inner)
            gres_ref[...] = gres
            branch = gres.astype(bf16)
            gb_ref[...] = branch
            for k in range(count):
                gm_ref[k] = dot_nt(branch, wo_ref[k * group : (k + 1) * group, :]).astype(bf16)
            partial = jnp.sum(grad * unit, axis=0, keepdims=True)

            @pl.when(step == steps)
            def _():
                gg_ref[...] = partial

            @pl.when(step > steps)
            def _():
                gg_ref[...] += partial

    def row(i):
        return jnp.maximum(i - steps, 0)

    rows_spec = pl.BlockSpec((block, width), lambda i: (row(i), 0))
    weight_specs = [
        pl.BlockSpec(
            (block, grads[k].shape[1]),
            functools.partial(lambda c, i: (jnp.minimum(i, steps - 1), c), parts[k][1]),
        )
        for k in range(n_grads)
    ]
    hidden_cols = sum(g.shape[1] for g in grads)
    return call(
        kernel,
        (steps + row_steps,),
        [resident(g.shape, (0, 0)) for g in grads]
        + weight_specs
        + [resident((width, width), (0, 0)), rows_spec, rows_spec, resident((1, width), (0, 0))],
        [
            rows_spec,
            rows_spec,
            pl.BlockSpec((count, block, group), lambda i: (0, row(i), 0)),
            pl.BlockSpec((1, width), lambda i: (0, 0)),
        ],
        [
            struct((rows, width), f32),
            struct((rows, width), bf16),
            struct((count, rows, group), bf16),
            struct((1, width), f32),
        ],
        2 * rows * width * hidden_cols + 2 * rows * width * width,
        2 * (rows + width) * hidden_cols + 16 * rows * width,
        scratch=[pltpu.VMEM((rows, width), f32)],
    )(*grads, *[weight_arrays[p[0]] for p in parts], wo, residual, cotangent, gain_row)


def products(lefts, rights, pairs, block=256):
    height = lefts[0].shape[0]
    sizes = [rights[r].shape[1] // block for _, r in pairs]
    firsts = [sum(sizes[:k]) for k in range(len(pairs))]

    def kernel(*refs):
        l_refs, r_refs, out = refs[: len(lefts)], refs[len(lefts) : -1], refs[-1]
        step = pl.program_id(0)
        for k, (l, _) in enumerate(pairs):
            @pl.when((step >= firsts[k]) & (step < firsts[k] + sizes[k]))
            def _():
                out[...] = dot(l_refs[l][...], r_refs[k][...]).astype(bf16)

    def right_spec(k):
        return pl.BlockSpec(
            (rights[pairs[k][1]].shape[0], block),
            lambda i: (0, jnp.clip(i - firsts[k], 0, sizes[k] - 1)),
        )

    width = block * sum(sizes)
    return call(
        kernel,
        (sum(sizes),),
        [resident(a.shape, (0, 0)) for a in lefts] + [right_spec(k) for k in range(len(pairs))],
        pl.BlockSpec((height, block), lambda i: (0, i)),
        struct((height, width), bf16),
        sum(2 * height * lefts[l].shape[1] * rights[r].shape[1] for l, r in pairs),
        2 * height * width,
    )(*lefts, *[rights[r] for _, r in pairs])


def project_back(order, slot, grads, weights):
    length, group = grads[0].shape
    width = weights.shape[0]
    rows = length // order.shape[0]
    block = min(256, rows)
    steps = rows // block

    def kernel(order_ref, a_ref, b_ref, c_ref, w_ref, out_ref):
        total = dot_nt(a_ref[...], w_ref[:, :group])
        total = total + dot_nt(b_ref[...], w_ref[:, group : 2 * group])
        total = total + dot_nt(c_ref[...], w_ref[:, 2 * group :])
        out_ref[...] = total.astype(bf16)

    rows_spec = pl.BlockSpec((block, group), lambda i, order_ref: (order_ref[slot] * steps + i, 0))
    return call(
        kernel,
        (steps,),
        [rows_spec] * 3 + [resident(weights.shape, (0, 0))],
        pl.BlockSpec((block, width), lambda i, order_ref: (i, 0)),
        struct((rows, width), bf16),
        6 * rows * width * group,
        2 * rows * (width + 3 * group),
        prefetch=1,
    )(order, *grads, weights)


def body(
    tokens, cotangent, query_weight, key_weight, value_weight, output_weight, gate_weight, up_weight,
    down_weight, attention_gain, feedforward_gain, cache_keys, cache_values, memory_rows, memory_docs,
):
    seq_count, fsdp_count = lax.axis_size("seq"), lax.axis_size("fsdp")
    here = lax.axis_index("seq")
    tok_rows, width = tokens.shape
    head_local, rows_cache, head_dim = cache_keys.shape[1:]
    group = head_local * head_dim
    length = tok_rows * seq_count
    mem_block = length // memory_rows.shape[2]
    mem_count = memory_rows.shape[3]
    shard = query_weight.shape[0]
    hidden_cols = gate_weight.shape[1]
    order = here ^ jnp.arange(seq_count, dtype=jnp.int32)

    gains = spread(jnp.stack([attention_gain, feedforward_gain]), "fsdp")
    gains = gains.transpose(1, 0, 2).reshape(2, width).astype(f32)
    gain_one, gain_two = gains[0:1], gains[1:2]
    own_cols = [
        lax.dynamic_slice_in_dim(w, here * group, group, axis=1)
        for w in (query_weight, key_weight, value_weight)
    ]
    qkv = spread(jnp.concatenate(own_cols, axis=1), "fsdp").reshape(width, 3 * group)

    pieces = [tokens, swap_seq(tokens, 1), swap_seq(tokens, 2)]
    pieces.append(swap_seq(pieces[2], 1))

    ring = [(i, (i + 1) % fsdp_count) for i in range(fsdp_count)]
    partner_keys = lax.ppermute(cache_keys[0], "fsdp", ring)
    partner_values = lax.ppermute(cache_values[0], "fsdp", ring)

    part = shard // seq_count
    split_a = 1024

    def own_rows(w):
        return lax.dynamic_slice_in_dim(w, here * part, part, axis=0)

    own_wo, own_wg, own_wu = own_rows(output_weight), own_rows(gate_weight), own_rows(up_weight)
    own_wd = lax.dynamic_slice_in_dim(down_weight, here * part, part, axis=1).T
    first_part = jnp.concatenate(
        [own_wo, own_wg[:, :split_a], own_wu[:, :split_a], own_wd[:, :split_a]], axis=1
    )
    second_part = jnp.concatenate(
        [own_wg[:, split_a:], own_wu[:, split_a:], own_wd[:, split_a:]], axis=1
    )
    both_axes = ("fsdp", "seq")
    big_a = lax.all_gather(first_part, both_axes, axis=0, tiled=True)
    big_b = lax.all_gather(second_part, both_axes, axis=0, tiled=True)
    rest = hidden_cols - split_a

    half = head_dim // 2
    frequency = 10000.0 ** (-2.0 * jnp.arange(half, dtype=f32) / head_dim)
    angles = jnp.arange(length, dtype=jnp.int32).astype(f32)[:, None] * frequency[None, :]
    cos_half, sin_half = jnp.cos(angles), jnp.sin(angles)
    cosine = jnp.concatenate([cos_half, cos_half], axis=1)
    sine = jnp.concatenate([-sin_half, sin_half], axis=1)
    cotangent_t = cotangent.T

    chosen = memory_docs[0] * rows_cache + memory_rows[0]
    picked = retrieve(chosen, cache_keys[0], cache_values[0], 0)
    query, key, value, normed_one_t = project(
        order, pieces, qkv, gain_one, cosine, sine, head_local, head_dim
    )
    picked_keys, picked_values = retrieve(chosen, partner_keys, partner_values, rows_cache, picked)
    attended_heads, lse = attend(
        query, key, value, picked_keys, picked_values, mem_block, mem_count
    )
    attended = lax.all_to_all(
        attended_heads.reshape(seq_count, tok_rows, group), "seq", 0, 0, tiled=True
    )
    residual, normed_two, normed_two_t, attended_t = mix(attended, big_a, tokens, gain_two)
    hid_a, gg_a, gu_a = gated(normed_two, cotangent, big_a, width, split_a)
    hid_b, gg_b, gu_b = gated(normed_two, cotangent, big_b, 0, rest)
    offset = width // split_a
    grad_residual, grad_branch, grad_mixed, grad_gain_two = norm_back(
        [gg_a, gu_a, gg_b, gu_b],
        [big_a, big_b],
        [(0, offset), (0, offset + 1), (1, 0), (1, 1)],
        big_a,
        residual,
        cotangent,
        gain_two,
        seq_count,
    )
    grad_heads = lax.all_to_all(grad_mixed, "seq", 0, 0, tiled=True).reshape(length, group)

    gate_up = products([normed_two_t], [gg_a, gg_b, gu_a, gu_b], [(0, 0), (0, 1), (0, 2), (0, 3)])
    down_out = products(
        [cotangent_t, attended_t], [hid_a, hid_b, grad_branch], [(0, 0), (0, 1), (1, 2)]
    )
    gain_cols = jnp.broadcast_to(grad_gain_two.T, (width, 128)).astype(bf16)
    down_out = jnp.concatenate([down_out, gain_cols], axis=1)
    gate_up = lax.psum_scatter(gate_up, both_axes, scatter_dimension=0, tiled=True)
    down_out = lax.psum_scatter(down_out, both_axes, scatter_dimension=0, tiled=True)

    wd_a = big_a[:, width + 2 * split_a :]
    wd_b = big_b[:, 2 * rest :]
    result = (residual + dot_nt(hid_a, wd_a) + dot_nt(hid_b, wd_b)).astype(bf16)

    dq, dk, dv = attend_back(
        query, key, value, picked_keys, picked_values, mem_block, mem_count,
        grad_heads, attended_heads, lse, cosine, sine,
    )
    grads = (dq, dk, dv)
    near = swap_seq(project_back(order, 1, grads, qkv), 1)
    far = swap_seq(project_back(order, 3, grads, qkv), 1)
    across = project_back(order, 2, grads, qkv).astype(f32) + far.astype(f32)
    across = swap_seq(across.astype(bf16), 2)
    own = project_back(order, 0, grads, qkv).astype(f32) + near.astype(f32)
    qkv_grad = products([normed_one_t], list(grads), [(0, 0), (0, 1), (0, 2)])
    grad_normed_one = own + across.astype(f32)

    inputs = tokens.astype(f32)
    scale = lax.rsqrt(jnp.mean(inputs * inputs, axis=-1, keepdims=True) + epsilon)
    unit = inputs * scale
    scaled = grad_normed_one * gain_one
    inner = jnp.mean(scaled * unit, axis=-1, keepdims=True)
    grad_tokens = (grad_residual + scale * (scaled - unit * inner)).astype(bf16)
    grad_gain_one = jnp.sum(grad_normed_one * unit, axis=0)

    def over_fsdp(array):
        moved = lax.all_to_all(
            array.reshape(fsdp_count, shard, array.shape[1]), "fsdp", 0, 0, tiled=True
        )
        return jnp.sum(moved.astype(f32), axis=0)

    qkv_sum = over_fsdp(qkv_grad).astype(bf16)
    qkv_all = spread(qkv_sum, "seq").astype(f32)
    grad_q, grad_k, grad_v = (
        qkv_all[:, :, k * group : (k + 1) * group].transpose(1, 0, 2).reshape(shard, width)
        for k in range(3)
    )
    gain_sum = over_fsdp(jnp.broadcast_to(grad_gain_one[:, None], (width, 128)).astype(bf16))
    gain_one_all = jnp.sum(spread(gain_sum.astype(bf16), "seq").astype(f32), axis=0)[:, 0]

    gate_up = spread(gate_up, "seq").reshape(shard, -1).astype(f32)
    down_out = spread(down_out, "seq").reshape(shard, -1).astype(f32)
    return (
        result,
        grad_tokens,
        grad_q,
        grad_k,
        grad_v,
        down_out[:, hidden_cols : hidden_cols + width],
        gate_up[:, :hidden_cols],
        gate_up[:, hidden_cols:],
        down_out[:, :hidden_cols].T,
        gain_one_all,
        down_out[:, hidden_cols + width],
    )


def solution(mesh):
    tok, row, col, one = P(("fsdp", "seq"), None), P("fsdp", None), P(None, "fsdp"), P("fsdp")
    cache = P("fsdp", "seq", None, None)
    return jax.shard_map(
        body,
        mesh=mesh,
        in_specs=(tok, tok) + (row,) * 6 + (col, one, one) + (cache,) * 4,
        out_specs=(tok, tok) + (row,) * 6 + (col, one, one),
        check_vma=False,
    )
```

```python
import functools

import jax
import jax.numpy as jnp
from jax import lax
from jax.experimental import pallas as pl
from jax.experimental.pallas import tpu as pltpu
from jax.sharding import PartitionSpec as P

epsilon = 1e-06
log2e = 1.4426950408889634
f32 = jnp.float32
bf16 = jnp.bfloat16
VMEM_LIMIT = 60 * 1024 * 1024
hint = 0.15


def dot(a, b):
    return jnp.dot(a, b, preferred_element_type=f32)


def dot_nt(a, b):
    return lax.dot_general(a, b, (((1,), (1,)), ((), ())), preferred_element_type=f32)


def dot_tn(a, b):
    return lax.dot_general(a, b, (((0,), (0,)), ((), ())), preferred_element_type=f32)


def call(
    kernel, grid, in_specs, out_specs, out_shape, flops, bytes_accessed, scratch=(), prefetch=0, aliases=None
):
    return pl.pallas_call(
        kernel,
        name=kernel.__qualname__.split(".")[0],
        grid_spec=pltpu.PrefetchScalarGridSpec(
            num_scalar_prefetch=prefetch,
            grid=grid,
            in_specs=in_specs,
            out_specs=out_specs,
            scratch_shapes=list(scratch),
        ),
        out_shape=out_shape,
        input_output_aliases=aliases or {},
        compiler_params=pltpu.CompilerParams(
            dimension_semantics=("arbitrary",) * len(grid), vmem_limit_bytes=VMEM_LIMIT
        ),
        cost_estimate=pl.CostEstimate(
            flops=int(flops * hint), bytes_accessed=int(bytes_accessed * hint), transcendentals=0
        ),
    )


def resident(shape, index):
    return pl.BlockSpec(shape, lambda *_: index, pipeline_mode=pl.Buffered(1))


def column_blocks(height, first, parts):
    return [resident((height, 256), (0, first // 256 + c)) for c in range(parts)]


def struct(shape, dtype):
    return jax.ShapeDtypeStruct(shape, dtype)


def swap_seq(array, bit):
    count = lax.axis_size("seq")
    return lax.ppermute(array, "seq", [(i, i ^ bit) for i in range(count)])


def spread(array, axis):
    count = lax.axis_size(axis)
    copies = jnp.broadcast_to(array[None], (count,) + array.shape)
    return lax.all_to_all(copies, axis, split_axis=0, concat_axis=0, tiled=True)


def project(order, pieces, weights, gain_row, cosine, sine, head_local, head_dim):
    rows, width = pieces[0].shape
    count = len(pieces)
    block = min(512, rows)
    steps = rows // block
    length = rows * count
    cols = weights.shape[1]
    group = head_local * head_dim

    def kernel(order_ref, *refs):
        xs = refs[:count]
        w_ref, g_ref, c_ref, s_ref, q_ref, k_ref, v_ref, vt_ref, nt_ref = refs[count:]
        slot = pl.program_id(0)

        def run(x_ref):
            x = x_ref[...].astype(f32)
            scale = lax.rsqrt(jnp.mean(x * x, axis=-1, keepdims=True) + epsilon)
            normed = (x * scale * g_ref[...]).astype(bf16)
            nt_ref[...] = normed.T
            lin = dot(normed, w_ref[...])
            cos, sin = c_ref[...], s_ref[...]
            for head in range(head_local):
                for part, out in ((0, q_ref), (1, k_ref)):
                    start = part * group + head * head_dim
                    u = lin[:, start : start + head_dim]
                    out[head] = (u * cos + pltpu.roll(u, head_dim // 2, 1) * sin).astype(bf16)
                start = 2 * group + head * head_dim
                v = lin[:, start : start + head_dim].astype(bf16)
                v_ref[head] = v
                vt_ref[head] = v.T

        for k in range(count):
            pl.when(slot == k)(functools.partial(run, xs[k]))

    def piece_spec(k):
        return pl.BlockSpec(
            (block, width),
            lambda slot, i, order_ref: (
                jnp.where(slot == k, i, jnp.where(slot < k, 0, steps - 1)),
                0,
            ),
        )

    def at_rows(slot, i, order_ref):
        return order_ref[slot] * steps + i

    head_spec = pl.BlockSpec((head_local, block, head_dim), lambda *a: (0, at_rows(*a), 0))
    table_spec = pl.BlockSpec((block, head_dim), lambda *a: (at_rows(*a), 0))
    heads = struct((head_local, length, head_dim), bf16)
    return call(
        kernel,
        (count, steps),
        [piece_spec(k) for k in range(count)]
        + [resident((width, cols), (0, 0)), resident((1, width), (0, 0)), table_spec, table_spec],
        [
            head_spec,
            head_spec,
            head_spec,
            pl.BlockSpec((head_local, head_dim, block), lambda *a: (0, 0, at_rows(*a))),
            pl.BlockSpec((width, block), lambda *a: (0, at_rows(*a))),
        ],
        [heads, heads, heads, struct((head_local, head_dim, length), bf16)]
        + [struct((width, length), bf16)],
        2 * length * width * cols,
        4 * length * width + 2 * length * cols + 8 * length * head_dim,
        prefetch=1,
    )(order, *pieces, weights, gain_row, cosine, sine)


def retrieve(chosen, keys, values, base, before=None):
    head_local, rows_cache, head_dim = keys.shape
    blocks, slots = chosen.shape[1:]
    per = min(4, blocks)
    total = blocks * slots

    def kernel(c_ref, k_ref, v_ref, *refs):
        if before is not None:
            bk_ref, bv_ref = refs[:2]
        ok_ref, ov_ref, table, mask = refs[-4:]

        @pl.when(pl.program_id(1) == 0)
        def _():
            table[:, :head_dim] = k_ref[0]
            table[:, head_dim:] = v_ref[0]

        for b in range(per):
            row = c_ref[0, 0, b : b + 1, :] - base
            column = jnp.broadcast_to(row, (slots, slots)).T
            lane = lax.broadcasted_iota(jnp.int32, (slots, slots), 1)
            for start in range(0, rows_cache, slots):
                mask[b * slots : (b + 1) * slots, start : start + slots] = jnp.where(
                    column == lane + start, 1.0, 0.0
                ).astype(bf16)
        picked = dot(mask[...], table[...])
        if before is not None:
            picked_keys = picked[:, :head_dim] + bk_ref[0].astype(f32)
            picked_values = picked[:, head_dim:] + bv_ref[0].astype(f32)
        else:
            picked_keys, picked_values = picked[:, :head_dim], picked[:, head_dim:]
        ok_ref[0] = picked_keys.astype(bf16)
        ov_ref[0] = picked_values.astype(bf16)

    out_spec = pl.BlockSpec((1, per * slots, head_dim), lambda h, i: (h, i, 0))
    table_spec = pl.BlockSpec((1, rows_cache, head_dim), lambda h, i: (h, 0, 0))
    extra = () if before is None else before
    out = struct((head_local, total, head_dim), bf16)
    return call(
        kernel,
        (head_local, blocks // per),
        [pl.BlockSpec((1, 1, per, slots), lambda h, i: (h, i, 0, 0)), table_spec, table_spec]
        + [out_spec] * len(extra),
        [out_spec, out_spec],
        [out, out],
        4 * head_local * total * rows_cache * head_dim,
        8 * head_local * total * head_dim,
        scratch=[
            pltpu.VMEM((rows_cache, 2 * head_dim), bf16),
            pltpu.VMEM((per * slots, rows_cache), bf16),
        ],
    )(chosen.reshape(head_local, blocks // per, per, slots), keys, values, *extra)


def attend(order, query, key, value_t, memory_keys, memory_values, mem_block, mem_count, count):
    head_local, length, head_dim = query.shape
    block = length // count
    half = block // 2
    groups = block // mem_block
    factor = head_dim ** (-0.5) * log2e

    def kernel(order_ref, q_ref, k_ref, vt_ref, mk_ref, mv_ref, *refs):
        o_refs, lse_ref = refs[:count], refs[count]
        index = pl.program_id(0)

        def memory(head):
            parts = []
            for g in range(groups):
                q = q_ref[head, g * mem_block : (g + 1) * mem_block, :]
                parts.append(dot_nt(mk_ref[head, g * mem_count : (g + 1) * mem_count, :], q))
            scores = jnp.concatenate(parts, axis=1) * factor
            top = jnp.max(scores, axis=0, keepdims=True)
            weight = jnp.exp2(scores - top)
            total = jnp.sum(weight, axis=0, keepdims=True)
            weight = weight.astype(bf16)
            values_t = mv_ref[head].T
            mixed = jnp.concatenate(
                [
                    dot(
                        values_t[:, g * mem_count : (g + 1) * mem_count],
                        weight[:, g * mem_block : (g + 1) * mem_block],
                    )
                    for g in range(groups)
                ],
                axis=1,
            )
            return top, total, mixed

        def step(head, carry, start, size, queries, offset):
            top, total, mixed = carry
            keys = k_ref[head, pl.ds(start, size), :]
            scores = dot_nt(keys, q_ref[head, queries, :]) * factor
            if offset is not None:
                row = lax.broadcasted_iota(jnp.int32, scores.shape, 0) + offset
                col = lax.broadcasted_iota(jnp.int32, scores.shape, 1) + (queries.start or 0)
                scores = jnp.where(row <= col, scores, -jnp.inf)
            new_top = jnp.maximum(top, jnp.max(scores, axis=0, keepdims=True))
            decay = jnp.exp2(top - new_top)
            weight = jnp.exp2(scores - new_top)
            total = total * decay + jnp.sum(weight, axis=0, keepdims=True)
            mixed = mixed * decay + dot(vt_ref[head, :, pl.ds(start, size)], weight.astype(bf16))
            return new_top, total, mixed

        every, later = slice(0, block), slice(half, block)
        carries = tuple(memory(head) for head in range(head_local))
        carries = lax.fori_loop(
            0,
            index,
            lambda j, c: tuple(
                step(head, c[head], pl.multiple_of(j * block, block), block, every, None)
                for head in range(head_local)
            ),
            carries,
        )
        start = pl.multiple_of(index * block, block)
        for head in range(head_local):
            carry = step(head, carries[head], start, half, every, 0)
            last = tuple(part[:, half:] for part in carry)
            middle = pl.multiple_of(start + half, half)
            last = step(head, last, middle, half, later, half)
            top, total, mixed = (
                jnp.concatenate([part[:, :half], end], axis=1) for part, end in zip(carry, last)
            )
            columns = slice(head * head_dim, (head + 1) * head_dim)
            mixed = (mixed / total).T.astype(bf16)
            for k in range(count):
                @pl.when(index == order_ref[k])
                def _():
                    o_refs[k][:, columns] = mixed
            lse = top + jnp.log2(total)
            lse_ref[0, head : head + 1, :] = lse[:, :half]
            lse_ref[1, head : head + 1, :] = lse[:, half:]

    full = resident((head_local, length, head_dim), (0, 0, 0))
    full_t = resident((head_local, head_dim, length), (0, 0, 0))
    rows = pl.BlockSpec((head_local, block, head_dim), lambda i, order_ref: (0, i, 0))
    mem_rows = pl.BlockSpec(
        (head_local, groups * mem_count, head_dim), lambda i, order_ref: (0, i, 0)
    )
    return call(
        kernel,
        (count,),
        [rows, full, full_t, mem_rows, mem_rows],
        [pl.BlockSpec((block, head_local * head_dim), lambda i, order_ref: (0, 0))] * count
        + [pl.BlockSpec((2, 8, half), lambda i, order_ref: (i, 0, 0))],
        [struct((block, head_local * head_dim), bf16)] * count
        + [struct((2 * count, 8, half), f32)],
        4 * head_local * length * length * head_dim,
        12 * head_local * length * head_dim,
        prefetch=1,
    )(order, query, key, value_t, memory_keys, memory_values)


def attend_back(
    order, query, key, value, memory_keys, memory_values, mem_block, mem_count, grads, attended, lse,
    cosine, sine, first, last, carried=None,
):
    head_local, length, head_dim = query.shape
    count, _, block = lse.shape
    pieces = len(grads)
    piece = length // pieces
    per = piece // block
    groups = block // mem_block
    scale = head_dim ** (-0.5)
    factor = scale * log2e
    opening, closing = first == 0, last == count

    def kernel(order_ref, q_ref, k_ref, v_ref, mk_ref, mv_ref, *refs):
        g_refs, refs = refs[:pieces], refs[pieces:]
        if opening:
            o_refs, refs = refs[:pieces], refs[pieces:]
        else:
            (part_ref, delta), refs = refs[:2], refs[5:]
        (lse_ref, c_ref, s_ref, dq_ref, dk_ref, dv_ref), refs = refs[:6], refs[6:]
        if opening and not closing:
            (rest_ref, delta), refs = refs[:2], refs[2:]
        elif opening:
            delta, refs = refs[0], refs[1:]
        dq_acc, do_ref = refs
        index = pl.program_id(0) + first

        def cols(head):
            return slice(head * head_dim, (head + 1) * head_dim)

        @pl.when(index == first)
        def _():
            for k in range(pieces):
                start = pl.multiple_of(order_ref[k] * piece, piece)
                do_ref[pl.ds(start, piece), :] = g_refs[k][...]
            if not opening:
                dq_acc[:, :, first * block :] = part_ref[...]
            else:
                for k in range(pieces):
                    for p in range(per):
                        rows = slice(p * block, (p + 1) * block)
                        for head in range(head_local):
                            do = g_refs[k][rows, cols(head)].astype(f32)
                            o = o_refs[k][rows, cols(head)].astype(f32)
                            row = jnp.sum((do * o).T, axis=0, keepdims=True)
                            delta[order_ref[k] * per + p, head : head + 1, :] = row

        row_id = lax.broadcasted_iota(jnp.int32, (block, block), 0)
        col_id = lax.broadcasted_iota(jnp.int32, (block, block), 1)
        keys_t = [k_ref[head].T for head in range(head_local)]

        def memory(head):
            start = pl.multiple_of(index * block, block)
            q = q_ref[head, pl.ds(start, block), :]
            do = do_ref[pl.ds(start, block), cols(head)]
            mk_t = mk_ref[head].T
            parts = []
            for g in range(groups):
                lanes = slice(g * mem_block, (g + 1) * mem_block)
                slots = slice(g * mem_count, (g + 1) * mem_count)
                scores = dot_nt(mk_ref[head, slots, :], q[lanes])
                weight = jnp.exp2(scores * factor - lse_ref[index, head : head + 1, lanes])
                dp = dot_nt(mv_ref[head, slots, :], do[lanes])
                ds = (weight * (dp - delta[index, head : head + 1, lanes])).astype(bf16)
                parts.append(dot(mk_t[:, slots], ds))
            return jnp.concatenate(parts, axis=1)

        def step(head, carry, i, masked):
            dk, dv = carry
            start = pl.multiple_of(i * block, block)
            q = q_ref[head, pl.ds(start, block), :]
            do = do_ref[pl.ds(start, block), cols(head)]
            k, v = k_ref[head], v_ref[head]
            weight = jnp.exp2(dot_nt(k, q) * factor - lse_ref[i, head : head + 1, :])
            if masked:
                weight = jnp.where(row_id <= col_id, weight, 0.0)
            dp = dot_nt(v, do)
            ds = (weight * (dp - delta[i, head : head + 1, :])).astype(bf16)
            dv = dv + dot(weight.astype(bf16), do)
            dk = dk + dot(ds, q)
            so_far = dq_acc[head, :, pl.ds(start, block)]
            if opening:
                so_far = jnp.where(index == 0, 0.0, so_far)
            total = so_far + dot(keys_t[head], ds)
            if masked:
                return dk, dv, total
            dq_acc[head, :, pl.ds(start, block)] = total
            return dk, dv

        cos, sin = c_ref[...], s_ref[...]

        def unrotate(grad_rows):
            u = (grad_rows * scale).astype(bf16).astype(f32)
            return (u * cos - pltpu.roll(u, head_dim // 2, 1) * sin).astype(bf16)

        zero = jnp.zeros((block, head_dim), f32)
        carries = []
        for head in range(head_local):
            dk, dv, dq = step(head, (zero, zero), index, True)
            dq_ref[:, cols(head)] = unrotate((dq + memory(head)).T)
            carries.append((dk, dv))
        carries = lax.fori_loop(
            index + 1,
            count,
            lambda i, c: tuple(step(head, c[head], i, False) for head in range(head_local)),
            tuple(carries),
        )
        for head, (dk, dv) in enumerate(carries):
            dk_ref[:, cols(head)] = unrotate(dk)
            dv_ref[:, cols(head)] = dv.astype(bf16)
        if opening and not closing:
            @pl.when(index == last - 1)
            def _():
                rest_ref[...] = dq_acc[:, :, last * block :]

    group = head_local * head_dim
    full = resident((head_local, length, head_dim), (0, 0, 0))
    flat = resident((piece, group), (0, 0))
    rows = pl.BlockSpec((head_local, block, head_dim), lambda i, o: (0, i + first, 0))
    mem_rows = pl.BlockSpec(
        (head_local, groups * mem_count, head_dim), lambda i, o: (0, i + first, 0)
    )
    table = pl.BlockSpec((block, head_dim), lambda i, o: (i + first, 0))
    out_rows = pl.BlockSpec((block, group), lambda i, o: (i + first, 0))
    out = struct((length, group), bf16)
    aliases = {}
    small = resident(lse.shape, (0, 0, 0))
    in_specs = [full, rows, rows, mem_rows, mem_rows] + [flat] * pieces
    inputs = [query, key, value, memory_keys, memory_values, *grads]
    out_specs, out_shape, scratch = [out_rows] * 3, [out] * 3, []
    if opening:
        in_specs += [flat] * pieces
        inputs += list(attended)
        if closing:
            scratch.append(pltpu.VMEM(lse.shape, f32))
        else:
            rest = (head_local, head_dim, length - last * block)
            out_specs += [pl.BlockSpec(rest, lambda i, o: (0, 0, 0)), pl.BlockSpec(lse.shape, lambda i, o: (0, 0, 0))]
            out_shape += [struct(rest, f32), struct(lse.shape, f32)]
    else:
        in_specs += [resident(carried[0].shape, (0, 0, 0)), small]
        in_specs += [pl.BlockSpec(memory_space=pl.ANY)] * 3
        aliases = {1 + len(inputs) + 2 + k: k for k in range(3)}
        inputs += list(carried)
    done = sum(count - j for j in range(first, last)) / (count * (count + 1) / 2)
    return call(
        kernel,
        (last - first,),
        in_specs + [small, table, table],
        out_specs,
        out_shape,
        done * 10 * head_local * length * length * head_dim // 2,
        24 * head_local * length * head_dim,
        scratch=scratch
        + [pltpu.VMEM((head_local, head_dim, length), f32), pltpu.VMEM((length, group), bf16)],
        prefetch=1,
        aliases=aliases,
    )(order, *inputs, lse, cosine, sine)


def mix(order, attended, weights, first, tokens, gain_row):
    count = len(attended)
    rows, group = attended[0].shape
    width = tokens.shape[1]
    block = min(256, rows)
    parts = width // 256

    def kernel(order_ref, *refs):
        a_refs = refs[:count]
        w_refs, refs = refs[count : count + parts], refs[count + parts :]
        x_ref, g_ref, res_ref, n_ref, nt_ref, at_ref = refs
        residual = x_ref[...].astype(f32)
        mixed = [None] * parts
        for k in range(count):
            start = pl.multiple_of(order_ref[k] * group, group)
            for c in range(parts):
                part = dot(a_refs[k][...], w_refs[c][pl.ds(start, group), :])
                mixed[c] = part if mixed[c] is None else mixed[c] + part
            at_ref[pl.ds(start, group), :] = a_refs[k][...].T
        residual = residual + jnp.concatenate(mixed, axis=1)
        scale = lax.rsqrt(jnp.mean(residual * residual, axis=-1, keepdims=True) + epsilon)
        normed = (residual * scale * g_ref[...]).astype(bf16)
        res_ref[...] = residual
        n_ref[...] = normed
        nt_ref[...] = normed.T

    rows_spec = pl.BlockSpec((block, width), lambda i, o: (i, 0))
    cols_spec = pl.BlockSpec((width, block), lambda i, o: (0, i))
    return call(
        kernel,
        (rows // block,),
        [pl.BlockSpec((block, group), lambda i, o: (i, 0))] * count
        + column_blocks(width, first, parts)
        + [rows_spec, resident((1, width), (0, 0))],
        [rows_spec, rows_spec, cols_spec, cols_spec],
        [struct((rows, width), f32), struct((rows, width), bf16)]
        + [struct((width, rows), bf16)] * 2,
        2 * rows * width * width,
        16 * rows * width,
        prefetch=1,
    )(order, *attended, *[weights] * parts, tokens, gain_row)


def gated(normed, cotangent, weights, first, hidden_cols):
    rows, width = normed.shape
    block = 256

    def kernel(n_ref, c_ref, wg_ref, wu_ref, wd_ref, h_ref, gg_ref, gu_ref):
        normed_block = n_ref[...]
        gate = dot(normed_block, wg_ref[...])
        up = dot(normed_block, wu_ref[...])
        grad = dot(c_ref[...], wd_ref[...])
        sg = 1.0 / (1.0 + jnp.exp(-gate))
        silu = gate * sg
        h_ref[...] = (silu * up).astype(bf16)
        gg_ref[...] = (grad * up * sg * (1.0 + gate * (1.0 - sg))).astype(bf16)
        gu_ref[...] = (grad * silu).astype(bf16)

    def weight_spec(k):
        offset = (first + k * hidden_cols) // block
        return pl.BlockSpec((width, block), lambda i: (0, i + offset))

    flat = resident((rows, width), (0, 0))
    out_spec = pl.BlockSpec((rows, block), lambda i: (0, i))
    return call(
        kernel,
        (hidden_cols // block,),
        [flat, flat] + [weight_spec(k) for k in range(3)],
        [out_spec] * 3,
        [struct((rows, hidden_cols), bf16)] * 3,
        6 * rows * width * hidden_cols,
        6 * (rows + width) * hidden_cols,
    )(normed, cotangent, weights, weights, weights)


def norm_back(order, grads, weights, first, residual, cotangent, gain_row):
    rows, width = residual.shape
    count = order.shape[0]
    block = min(256, rows)
    steps = width // block
    row_steps = rows // block
    group = width // count
    parts = width // 256
    n_grads = len(grads)

    def kernel(order_ref, *refs):
        g_refs, w_refs = refs[:n_grads], refs[n_grads : 2 * n_grads]
        wo_refs, refs = refs[2 * n_grads : 2 * n_grads + parts], refs[2 * n_grads + parts :]
        r_ref, c_ref, gain_ref, gres_ref, gb_ref = refs[:5]
        gm_refs, acc = refs[5 : 5 + count], refs[5 + count]
        step = pl.program_id(0)

        @pl.when(step < steps)
        def _():
            total = dot_nt(g_refs[0][...], w_refs[0][...])
            for k in range(1, n_grads):
                total = total + dot_nt(g_refs[k][...], w_refs[k][...])
            for d in range(steps):
                @pl.when(step == d)
                def _():
                    acc[:, d * block : (d + 1) * block] = total

        @pl.when(step >= steps)
        def _():
            start = pl.multiple_of((step - steps) * block, block)
            grad = acc[pl.ds(start, block), :]
            res = r_ref[...]
            scale = lax.rsqrt(jnp.mean(res * res, axis=-1, keepdims=True) + epsilon)
            unit = res * scale
            scaled = grad * gain_ref[...]
            inner = jnp.mean(scaled * unit, axis=-1, keepdims=True)
            gres = c_ref[...].astype(f32) + scale * (scaled - unit * inner)
            gres_ref[...] = gres
            branch = gres.astype(bf16)
            gb_ref[...] = branch
            for k in range(count):
                start_k = pl.multiple_of(order_ref[k] * group, group)
                mixed = None
                for c in range(parts):
                    part = dot_nt(
                        branch[:, c * 256 : (c + 1) * 256], wo_refs[c][pl.ds(start_k, group), :]
                    )
                    mixed = part if mixed is None else mixed + part
                gm_refs[k][...] = mixed.astype(bf16)

    def row(i):
        return jnp.maximum(i - steps, 0)

    rows_spec = pl.BlockSpec((block, width), lambda i, o: (row(i), 0))
    weight_specs = [
        pl.BlockSpec(
            (block, grads[k].shape[1]),
            functools.partial(lambda c, i, o: (jnp.minimum(i, steps - 1), c), k),
        )
        for k in range(n_grads)
    ]
    hidden_cols = sum(g.shape[1] for g in grads)
    return call(
        kernel,
        (steps + row_steps,),
        [resident(g.shape, (0, 0)) for g in grads]
        + weight_specs
        + column_blocks(width, first, parts)
        + [rows_spec, rows_spec, resident((1, width), (0, 0))],
        [
            rows_spec,
            rows_spec,
        ]
        + [pl.BlockSpec((block, group), lambda i, o: (row(i), 0))] * count,
        [
            struct((rows, width), f32),
            struct((rows, width), bf16),
        ]
        + [struct((rows, group), bf16)] * count,
        2 * rows * width * hidden_cols + 2 * rows * width * width,
        2 * (rows + width) * hidden_cols + 16 * rows * width,
        scratch=[pltpu.VMEM((rows, width), f32)],
        prefetch=1,
    )(order, *grads, *[weights] * (n_grads + parts), residual, cotangent, gain_row)


def products(select, lefts, rights, parts, added=None, joined=False):
    height = lefts[0].shape[0]
    block = min(256, height)
    n = len(rights)
    sizes = [r.shape[1] // p for r, p in zip(rights, parts)]
    added = added or []
    distinct = []
    for left in lefts:
        if not any(left is d for d in distinct):
            distinct.append(left)
    which = [next(i for i, d in enumerate(distinct) if d is left) for left in lefts]
    n_left, n_add = len(distinct), len(added)

    def kernel(select_ref, *refs):
        l_refs, r_refs, outs = refs[:n_left], refs[n_left : n_left + n], refs[n_left + n + n_add :]
        for k in range(n):
            total = dot(l_refs[which[k]][...], r_refs[k][...])
            if k < n_add:
                total = total + refs[n_left + n + k][...].astype(f32)
            if joined:
                start = sum(sizes[:k])
                outs[0][:, start : start + sizes[k]] = total.astype(bf16)
            else:
                outs[k][...] = total.astype(bf16)

    def right_spec(k):
        return pl.BlockSpec(
            (rights[k].shape[0], sizes[k]),
            lambda i, s: (0, s[0] if parts[k] > 1 else 0),
            pipeline_mode=pl.Buffered(1),
        )

    out_sizes = [sum(sizes)] if joined else sizes
    out_specs = [pl.BlockSpec((block, size), lambda i, s: (i, 0)) for size in out_sizes]
    return call(
        kernel,
        (height // block,),
        [pl.BlockSpec((block, d.shape[1]), lambda i, s: (i, 0)) for d in distinct]
        + [right_spec(k) for k in range(n)]
        + out_specs[:n_add],
        out_specs,
        [struct((height, size), bf16) for size in out_sizes],
        sum(2 * height * r.shape[0] * size for r, size in zip(rights, sizes)),
        2 * height * sum(sizes) + sum(2 * r.shape[0] * size for r, size in zip(rights, sizes)),
        prefetch=1,
    )(select, *distinct, *rights, *added)


def finish(residual, hidden, weights, first):
    rows, width = residual.shape
    block = min(256, rows)
    hidden_cols = hidden.shape[1]

    def kernel(r_ref, h_ref, w_ref, out_ref):
        out_ref[...] = (r_ref[...] + dot_nt(h_ref[...], w_ref[...])).astype(bf16)

    rows_spec = pl.BlockSpec((block, width), lambda i: (i, 0))
    return call(
        kernel,
        (rows // block,),
        [
            rows_spec,
            pl.BlockSpec((block, hidden_cols), lambda i: (i, 0)),
            resident((width, hidden_cols), (0, first)),
        ],
        rows_spec,
        struct((rows, width), bf16),
        2 * rows * width * hidden_cols,
        6 * rows * width + 2 * (rows + width) * hidden_cols,
    )(residual, hidden, weights)


def project_back(order, slot, grads, weights, added=(), part=(0, 1), last=None, into=None):
    length, group = grads[0].shape
    width = weights.shape[0]
    piece = length // order.shape[0]
    rows = piece // part[1]
    block = min(512 if last is None else 256, rows)
    steps = rows // block
    before = part[0] * steps
    n = len(added)

    def kernel(order_ref, a_ref, b_ref, c_ref, w_ref, *refs):
        total = dot_nt(a_ref[...], w_ref[:, :group])
        total = total + dot_nt(b_ref[...], w_ref[:, group : 2 * group])
        total = total + dot_nt(c_ref[...], w_ref[:, 2 * group :])
        for ref in refs[:n]:
            total = total + ref[...].astype(f32)
        if last is not None:
            x_ref, gain_ref, g_ref = refs[n : n + 3]
            x = x_ref[...].astype(f32)
            scale = lax.rsqrt(jnp.mean(x * x, axis=-1, keepdims=True) + epsilon)
            unit = x * scale
            scaled = total * gain_ref[...]
            inner = jnp.mean(scaled * unit, axis=-1, keepdims=True)
            total = g_ref[...] + scale * (scaled - unit * inner)
        refs[-1][...] = total.astype(bf16)

    def rows_of(array):
        first = before if array.shape[0] == piece else 0
        return pl.BlockSpec((block, width), lambda i, order_ref: (i + first, 0))

    def grad_rows(i, order_ref):
        return (order_ref[slot] * (piece // block) + before + i, 0)

    inputs = [*grads, weights, *added]
    in_specs = [pl.BlockSpec((block, group), grad_rows)] * 3 + [resident(weights.shape, (0, 0))]
    in_specs += [rows_of(a) for a in added]
    aliases = {}
    out = struct((rows, width), bf16)
    if last is not None:
        out = struct((piece, width), bf16)
        inputs += last
        in_specs += [rows_of(last[0]), resident((1, width), (0, 0)), rows_of(last[2])]
        if into is not None:
            aliases = {1 + len(inputs): 0}
            inputs.append(into)
            in_specs.append(pl.BlockSpec(memory_space=pl.ANY))
    return call(
        kernel,
        (steps,),
        in_specs,
        rows_of(out),
        out,
        6 * rows * width * group,
        2 * rows * (2 * width + 3 * group),
        prefetch=1,
        aliases=aliases,
    )(order, *inputs)


def pair_add(a, b):
    return (a.astype(f32) + b.astype(f32)).astype(bf16)


def axis_bits(axis, first=1):
    bits = []
    while first < lax.axis_size(axis):
        bits.append(first)
        first *= 2
    return bits


def trade(array, dim, axis, bit):
    count = lax.axis_size(axis)
    mine = (lax.axis_index(axis) // bit) % 2
    keep = lax.dynamic_index_in_dim(array, mine, axis=dim, keepdims=False)
    give = lax.dynamic_index_in_dim(array, 1 - mine, axis=dim, keepdims=False)
    return keep, lax.ppermute(give, axis, [(i, i ^ bit) for i in range(count)])


def scatter_start(array, turn, halve_seq):
    count = lax.axis_size("fsdp")
    bits = axis_bits("fsdp")
    bits = bits[turn % len(bits) :] + bits[: turn % len(bits)]
    left = axis_bits("fsdp")[::-1]
    array = array.reshape((2,) * len(bits) + (array.shape[0] // count, array.shape[1]))
    todo = [("fsdp", bit) for bit in bits]
    seq = [("seq", bit) for bit in axis_bits("seq", 2)]
    if halve_seq is not None:
        todo = seq + todo if halve_seq else todo + seq
    return exchange((array, None, todo, left, halve_seq))


def exchange(state):
    array, _, todo, left, halve_seq = state
    if not todo:
        return state
    axis, bit = todo[0]
    if axis == "fsdp":
        pair = trade(array, left.index(bit), axis, bit)
        left = [b for b in left if b != bit]
    elif halve_seq:
        rows, n = array.shape[-2:]
        array = array.reshape(array.shape[:-2] + (2, rows // 2, n))
        pair = trade(array, array.ndim - 3, axis, bit)
    else:
        pair = array, swap_seq(array, bit)
    return (*pair, todo[1:], left, halve_seq)


def settle(states, done, ahead):
    keeps, done = lax.optimization_barrier(([state[0] for state in states], done))
    arrays = [
        keep if state[1] is None else pair_add(keep, state[1])
        for keep, state in zip(keeps, states)
    ]
    arrays, ahead = lax.optimization_barrier((arrays, ahead))
    return [(a, None) + state[2:] for a, state in zip(arrays, states)], done, ahead


def rows_whole(state):
    array = state[0].reshape(state[0].shape[-2:])
    if state[4]:
        for bit in axis_bits("seq", 2)[::-1]:
            first = (lax.axis_index("seq") // bit) % 2 == 0
            array = both_ways(array, swap_seq(array, bit), first).reshape(-1, array.shape[1])
    return array


def both_ways(own, other, first):
    return jnp.stack([jnp.where(first, own, other), jnp.where(first, other, own)])


def join_halves(own):
    other = swap_seq(own, 1)
    first = lax.axis_index("seq") % 2 == 0
    own, other = own.astype(f32), other.astype(f32)
    return jnp.where(first, own, other), jnp.where(first, other, own)


def body(
    tokens, cotangent, query_weight, key_weight, value_weight, output_weight, gate_weight, up_weight,
    down_weight, attention_gain, feedforward_gain, cache_keys, cache_values, memory_rows, memory_docs,
):
    seq_count, fsdp_count = lax.axis_size("seq"), lax.axis_size("fsdp")
    here = lax.axis_index("seq")
    tok_rows, width = tokens.shape
    head_local, rows_cache, head_dim = cache_keys.shape[1:]
    group = head_local * head_dim
    length = tok_rows * seq_count
    mem_block = length // memory_rows.shape[2]
    mem_count = memory_rows.shape[3]
    shard = query_weight.shape[0]
    hidden_cols = gate_weight.shape[1]
    order = here ^ jnp.arange(seq_count, dtype=jnp.int32)

    gains = spread(jnp.stack([attention_gain, feedforward_gain]), "fsdp")
    gains = gains.transpose(1, 0, 2).reshape(2, width).astype(f32)
    gain_one, gain_two = gains[0:1], gains[1:2]
    own_cols = [
        lax.dynamic_slice_in_dim(w, here * group, group, axis=1)
        for w in (query_weight, key_weight, value_weight)
    ]
    qkv = spread(jnp.concatenate(own_cols, axis=1), "fsdp").reshape(width, 3 * group)

    pieces = [tokens, swap_seq(tokens, 1), swap_seq(tokens, 2)]
    pieces.append(swap_seq(pieces[2], 1))

    ring = [(i, (i + 1) % fsdp_count) for i in range(fsdp_count)]
    partner_keys = lax.ppermute(cache_keys[0], "fsdp", ring)
    partner_values = lax.ppermute(cache_values[0], "fsdp", ring)

    part = shard // seq_count

    def own_rows(w):
        return lax.dynamic_slice_in_dim(w, here * part, part, axis=0)

    own_wd = lax.dynamic_slice_in_dim(down_weight, here * part, part, axis=1).T
    own_part = jnp.concatenate(
        [own_rows(gate_weight), own_rows(up_weight), own_wd, own_rows(output_weight)], axis=1
    )
    big = lax.all_gather(own_part, ("fsdp", "seq"), axis=0, tiled=True)

    half = head_dim // 2
    frequency = 10000.0 ** (-2.0 * jnp.arange(half, dtype=f32) / head_dim)
    angles = jnp.arange(length, dtype=jnp.int32).astype(f32)[:, None] * frequency[None, :]
    cos_half, sin_half = jnp.cos(angles), jnp.sin(angles)
    cosine = jnp.concatenate([cos_half, cos_half], axis=1)
    sine = jnp.concatenate([-sin_half, sin_half], axis=1)
    cotangent_t = cotangent.T

    chosen = memory_docs[0] * rows_cache + memory_rows[0]
    picked = retrieve(chosen, cache_keys[0], cache_values[0], 0)
    query, key, value, value_t, normed_one_t = project(
        order, pieces, qkv, gain_one, cosine, sine, head_local, head_dim
    )
    picked_keys, picked_values = retrieve(chosen, partner_keys, partner_values, rows_cache, picked)
    *attended_heads, lse = attend(
        order, query, key, value_t, picked_keys, picked_values, mem_block, mem_count, seq_count
    )

    def by_distance(stack):
        return [stack[0]] + [swap_seq(stack[k], k) for k in range(1, seq_count)]

    attended = by_distance(attended_heads)
    residual, normed_two, normed_two_t, attended_t = mix(
        order, attended, big, 3 * hidden_cols, tokens, gain_two
    )
    hid, gg, gu = gated(normed_two, cotangent, big, 0, hidden_cols)
    own_half, other_half = (here % 2)[None].astype(jnp.int32), (1 - here % 2)[None].astype(jnp.int32)
    lefts, rights = [cotangent_t, normed_two_t, normed_two_t], [hid, gg, gu]
    given = products(other_half, lefts, rights, (2, 2, 2))
    given, gg_later = lax.optimization_barrier((given, gg))
    got = [swap_seq(g, 1) for g in given]
    grad_residual, grad_branch, *grad_mixed = norm_back(
        order, [gg_later, gu], big, 3 * hidden_cols, residual, cotangent, gain_two
    )
    grad_heads = by_distance(grad_mixed)
    own = products(own_half, [*lefts, attended_t], [*rights, grad_branch], (2, 2, 2, 1), got)
    grad_heads, own = lax.optimization_barrier((grad_heads, own))
    halved = (True, False, False, False)
    sums = [scatter_start(g, turn, h) for g, turn, h in zip(own, (0, 0, 1, 2), halved)]

    blocks = lse.shape[0]
    middle = 3 * blocks // 8
    attention = (order, query, key, value, picked_keys, picked_values, mem_block, mem_count)
    *grads, rest, delta = attend_back(
        *attention, grad_heads, attended_heads, lse, cosine, sine, 0, middle
    )
    sums, _, (rest, delta) = settle(sums, (), (rest, delta))
    sums = [exchange(g) for g in sums]
    grads = attend_back(
        *attention, grad_heads, None, lse, cosine, sine, middle, blocks, (rest, delta, *grads)
    )

    zero = jnp.zeros((1,), jnp.int32)
    (qkv_grad,) = products(zero, [normed_one_t] * 3, list(grads), (1, 1, 1), joined=True)
    sums, _, (qkv_grad, grads) = settle(sums, (), (qkv_grad, grads))
    qkv_state = scatter_start(qkv_grad, 0, None)
    sums = [exchange(g) for g in sums]
    far = project_back(order, 3, grads, qkv)
    far, grads = lax.optimization_barrier((far, grads))
    near = project_back(order, 1, grads, qkv)
    far = swap_seq(far, 1)
    near, far, grads = lax.optimization_barrier((near, far, grads))
    near = swap_seq(near, 1)
    across = project_back(order, 2, grads, qkv, [far])
    (qkv_state, *sums), _, (across, hid) = settle([qkv_state, *sums], across, (across, hid))
    across = [swap_seq(half, 2) for half in jnp.split(across, 2)]
    qkv_state, *sums = [exchange(g) for g in [qkv_state, *sums]]
    result = finish(residual, hid, big, 2)
    (qkv_state, *sums), result, (near, across[0]) = settle(
        [qkv_state, *sums], result, (near, across[0])
    )
    qkv_state, *sums = [exchange(g) for g in [qkv_state, *sums]]
    last = (tokens, gain_one, grad_residual)
    grad_tokens = project_back(order, 0, grads, qkv, [near, across[0]], (0, 2), last)
    (qkv_state, *sums), _, (grad_tokens, across[1]) = settle(
        [qkv_state, *sums], grad_tokens, (grad_tokens, across[1])
    )
    while any(state[2] for state in sums):
        sums = settle([exchange(g) for g in sums], (), ())[0]
    while qkv_state[2]:
        qkv_state = settle([exchange(qkv_state)], (), ())[0][0]
    qkv_sum = qkv_state[0].reshape(qkv_state[0].shape[-2:])
    by_piece = lambda a, other, bit: both_ways(a, other, (here // bit) % 2 == 0)
    pair = by_piece(qkv_sum, swap_seq(qkv_sum, 2), 2)
    qkv_all = by_piece(pair, swap_seq(pair, 1), 1)
    sums = [rows_whole(g) for g in sums]
    grad_down, grad_gate, grad_up = (jnp.concatenate(join_halves(g), axis=1) for g in sums[:3])
    grad_out = sums[3].astype(f32) + swap_seq(sums[3], 1).astype(f32)
    grad_tokens = project_back(
        order, 0, grads, qkv, [near, across[1]], (1, 2), last, grad_tokens
    )
    qkv_all = qkv_all.swapaxes(0, 1).reshape(seq_count, shard, 3 * group).astype(f32)
    grad_q, grad_k, grad_v = (
        qkv_all[:, :, k * group : (k + 1) * group].transpose(1, 0, 2).reshape(shard, width)
        for k in range(3)
    )

    def gain_grad(gain, pairs):
        total = sum(jnp.sum(w.astype(f32) * g, axis=1) for w, g in pairs)
        return total / gain.astype(f32)

    grad_gain_one = gain_grad(
        attention_gain, [(query_weight, grad_q), (key_weight, grad_k), (value_weight, grad_v)]
    )
    grad_gain_two = gain_grad(
        feedforward_gain, [(gate_weight, grad_gate), (up_weight, grad_up)]
    )
    grad_down = grad_down.T
    return (
        result,
        grad_tokens,
        grad_q,
        grad_k,
        grad_v,
        grad_out,
        grad_gate,
        grad_up,
        grad_down,
        grad_gain_one,
        grad_gain_two,
    )


def solution(mesh):
    tok, row, col, one = P(("fsdp", "seq"), None), P("fsdp", None), P(None, "fsdp"), P("fsdp")
    cache = P("fsdp", "seq", None, None)
    return jax.shard_map(
        body,
        mesh=mesh,
        in_specs=(tok, tok) + (row,) * 6 + (col, one, one) + (cache,) * 4,
        out_specs=(tok, tok) + (row,) * 6 + (col, one, one),
        check_vma=False,
    )
```

```python
import functools

import jax
import jax.numpy as jnp
from jax import lax
from jax.experimental import pallas as pl
from jax.experimental.pallas import tpu as pltpu
from jax.sharding import PartitionSpec as P

epsilon = 1e-06
log2e = 1.4426950408889634
f32 = jnp.float32
bf16 = jnp.bfloat16
VMEM_LIMIT = 60 * 1024 * 1024
hint = 0.15


def dot(a, b):
    return jnp.dot(a, b, preferred_element_type=f32)


def dot_nt(a, b):
    return lax.dot_general(a, b, (((1,), (1,)), ((), ())), preferred_element_type=f32)


def dot_tn(a, b):
    return lax.dot_general(a, b, (((0,), (0,)), ((), ())), preferred_element_type=f32)


def call(
    kernel, grid, in_specs, out_specs, out_shape, flops, bytes_accessed, scratch=(), prefetch=0, aliases=None
):
    return pl.pallas_call(
        kernel,
        name=kernel.__qualname__.split(".")[0],
        grid_spec=pltpu.PrefetchScalarGridSpec(
            num_scalar_prefetch=prefetch,
            grid=grid,
            in_specs=in_specs,
            out_specs=out_specs,
            scratch_shapes=list(scratch),
        ),
        out_shape=out_shape,
        input_output_aliases=aliases or {},
        compiler_params=pltpu.CompilerParams(
            dimension_semantics=("arbitrary",) * len(grid), vmem_limit_bytes=VMEM_LIMIT
        ),
        cost_estimate=pl.CostEstimate(
            flops=int(flops * hint), bytes_accessed=int(bytes_accessed * hint), transcendentals=0
        ),
    )


def resident(shape, index):
    return pl.BlockSpec(shape, lambda *_: index, pipeline_mode=pl.Buffered(1))


def column_blocks(height, first, parts):
    return [resident((height, 256), (0, first // 256 + c)) for c in range(parts)]


def struct(shape, dtype):
    return jax.ShapeDtypeStruct(shape, dtype)


def swap_seq(array, bit):
    count = lax.axis_size("seq")
    return lax.ppermute(array, "seq", [(i, i ^ bit) for i in range(count)])


def spread(array, axis):
    count = lax.axis_size(axis)
    copies = jnp.broadcast_to(array[None], (count,) + array.shape)
    return lax.all_to_all(copies, axis, split_axis=0, concat_axis=0, tiled=True)


def project(order, pieces, weights, gain_row, cosine, sine, head_local, head_dim):
    rows, width = pieces[0].shape
    count = len(pieces)
    block = min(512, rows)
    steps = rows // block
    length = rows * count
    cols = weights.shape[1]
    group = head_local * head_dim

    def kernel(order_ref, *refs):
        xs = refs[:count]
        w_ref, g_ref, c_ref, s_ref, q_ref, k_ref, v_ref, vt_ref, nt_ref, x_block = refs[count:]
        slot = pl.program_id(0)

        def run(x_ref):
            x = x_ref[...].astype(f32)
            scale = lax.rsqrt(jnp.mean(x * x, axis=-1, keepdims=True) + epsilon)
            normed = (x * scale * g_ref[...]).astype(bf16)
            nt_ref[...] = normed.T
            lin = dot(normed, w_ref[...])
            cos, sin = c_ref[...], s_ref[...]
            for head in range(head_local):
                for part, out in ((0, q_ref), (1, k_ref)):
                    start = part * group + head * head_dim
                    u = lin[:, start : start + head_dim]
                    out[head] = (u * cos + pltpu.roll(u, head_dim // 2, 1) * sin).astype(bf16)
                start = 2 * group + head * head_dim
                v = lin[:, start : start + head_dim].astype(bf16)
                v_ref[head] = v
                vt_ref[head] = v.T

        for k in range(count):
            @pl.when(slot == k)
            def _():
                x_block[...] = xs[k][...]

        run(x_block)

    def piece_spec(k):
        return pl.BlockSpec(
            (block, width),
            lambda slot, i, order_ref: (
                jnp.where(slot == k, i, jnp.where(slot < k, 0, steps - 1)),
                0,
            ),
        )

    def at_rows(slot, i, order_ref):
        return order_ref[slot] * steps + i

    head_spec = pl.BlockSpec((head_local, block, head_dim), lambda *a: (0, at_rows(*a), 0))
    table_spec = pl.BlockSpec((block, head_dim), lambda *a: (at_rows(*a), 0))
    heads = struct((head_local, length, head_dim), bf16)
    return call(
        kernel,
        (count, steps),
        [piece_spec(k) for k in range(count)]
        + [resident((width, cols), (0, 0)), resident((1, width), (0, 0)), table_spec, table_spec],
        [
            head_spec,
            head_spec,
            head_spec,
            pl.BlockSpec((head_local, head_dim, block), lambda *a: (0, 0, at_rows(*a))),
            pl.BlockSpec((width, block), lambda *a: (0, at_rows(*a))),
        ],
        [heads, heads, heads, struct((head_local, head_dim, length), bf16)]
        + [struct((width, length), bf16)],
        2 * length * width * cols,
        4 * length * width + 2 * length * cols + 8 * length * head_dim,
        scratch=[pltpu.VMEM((block, width), bf16)],
        prefetch=1,
    )(order, *pieces, weights, gain_row, cosine, sine)


def retrieve(chosen, keys, values, base, before=None):
    head_local, rows_cache, head_dim = keys.shape
    blocks, slots = chosen.shape[1:]
    per = min(4, blocks)
    total = blocks * slots

    def kernel(c_ref, k_ref, v_ref, *refs):
        if before is not None:
            bk_ref, bv_ref = refs[:2]
        ok_ref, ov_ref, table, mask = refs[-4:]

        @pl.when(pl.program_id(1) == 0)
        def _():
            table[:, :head_dim] = k_ref[0]
            table[:, head_dim:] = v_ref[0]

        for b in range(per):
            row = c_ref[0, 0, b : b + 1, :] - base
            column = jnp.broadcast_to(row, (slots, slots)).T
            lane = lax.broadcasted_iota(jnp.int32, (slots, slots), 1)
            for start in range(0, rows_cache, slots):
                mask[b * slots : (b + 1) * slots, start : start + slots] = jnp.where(
                    column == lane + start, 1.0, 0.0
                ).astype(bf16)
        picked = dot(mask[...], table[...])
        if before is not None:
            picked_keys = picked[:, :head_dim] + bk_ref[0].astype(f32)
            picked_values = picked[:, head_dim:] + bv_ref[0].astype(f32)
        else:
            picked_keys, picked_values = picked[:, :head_dim], picked[:, head_dim:]
        ok_ref[0] = picked_keys.astype(bf16)
        ov_ref[0] = picked_values.astype(bf16)

    out_spec = pl.BlockSpec((1, per * slots, head_dim), lambda h, i: (h, i, 0))
    table_spec = pl.BlockSpec((1, rows_cache, head_dim), lambda h, i: (h, 0, 0))
    extra = () if before is None else before
    out = struct((head_local, total, head_dim), bf16)
    return call(
        kernel,
        (head_local, blocks // per),
        [pl.BlockSpec((1, 1, per, slots), lambda h, i: (h, i, 0, 0)), table_spec, table_spec]
        + [out_spec] * len(extra),
        [out_spec, out_spec],
        [out, out],
        4 * head_local * total * rows_cache * head_dim,
        8 * head_local * total * head_dim,
        scratch=[
            pltpu.VMEM((rows_cache, 2 * head_dim), bf16),
            pltpu.VMEM((per * slots, rows_cache), bf16),
        ],
    )(chosen.reshape(head_local, blocks // per, per, slots), keys, values, *extra)


def attend(order, query, key, value_t, memory_keys, memory_values, mem_block, mem_count, count):
    head_local, length, head_dim = query.shape
    block = length // count
    half = block // 2
    groups = block // mem_block
    factor = head_dim ** (-0.5) * log2e

    def kernel(order_ref, q_ref, k_ref, vt_ref, mk_ref, mv_ref, *refs):
        o_refs, lse_ref = refs[:count], refs[count]
        index = pl.program_id(0)

        def memory(head):
            parts = []
            for g in range(groups):
                q = q_ref[head, g * mem_block : (g + 1) * mem_block, :]
                parts.append(dot_nt(mk_ref[head, g * mem_count : (g + 1) * mem_count, :], q))
            scores = jnp.concatenate(parts, axis=1) * factor
            top = jnp.max(scores, axis=0, keepdims=True)
            weight = jnp.exp2(scores - top)
            total = jnp.sum(weight, axis=0, keepdims=True)
            weight = weight.astype(bf16)
            values_t = mv_ref[head].T
            mixed = jnp.concatenate(
                [
                    dot(
                        values_t[:, g * mem_count : (g + 1) * mem_count],
                        weight[:, g * mem_block : (g + 1) * mem_block],
                    )
                    for g in range(groups)
                ],
                axis=1,
            )
            return top, total, mixed

        def step(head, carry, start, size, queries, offset):
            top, total, mixed = carry
            keys = k_ref[head, pl.ds(start, size), :]
            scores = dot_nt(keys, q_ref[head, queries, :]) * factor
            if offset is not None:
                row = lax.broadcasted_iota(jnp.int32, scores.shape, 0) + offset
                col = lax.broadcasted_iota(jnp.int32, scores.shape, 1) + (queries.start or 0)
                scores = jnp.where(row <= col, scores, -jnp.inf)
            new_top = jnp.maximum(top, jnp.max(scores, axis=0, keepdims=True))
            decay = jnp.exp2(top - new_top)
            weight = jnp.exp2(scores - new_top)
            total = total * decay + jnp.sum(weight, axis=0, keepdims=True)
            mixed = mixed * decay + dot(vt_ref[head, :, pl.ds(start, size)], weight.astype(bf16))
            return new_top, total, mixed

        every, later = slice(0, block), slice(half, block)
        carries = tuple(memory(head) for head in range(head_local))
        carries = lax.fori_loop(
            0,
            index,
            lambda j, c: tuple(
                step(head, c[head], pl.multiple_of(j * block, block), block, every, None)
                for head in range(head_local)
            ),
            carries,
        )
        start = pl.multiple_of(index * block, block)
        for head in range(head_local):
            carry = step(head, carries[head], start, half, every, 0)
            last = tuple(part[:, half:] for part in carry)
            middle = pl.multiple_of(start + half, half)
            last = step(head, last, middle, half, later, half)
            top, total, mixed = (
                jnp.concatenate([part[:, :half], end], axis=1) for part, end in zip(carry, last)
            )
            columns = slice(head * head_dim, (head + 1) * head_dim)
            mixed = (mixed / total).T.astype(bf16)
            for k in range(count):
                @pl.when(index == order_ref[k])
                def _():
                    o_refs[k][:, columns] = mixed
            lse = top + jnp.log2(total)
            lse_ref[0, head : head + 1, :] = lse[:, :half]
            lse_ref[1, head : head + 1, :] = lse[:, half:]

    full = resident((head_local, length, head_dim), (0, 0, 0))
    full_t = resident((head_local, head_dim, length), (0, 0, 0))
    rows = pl.BlockSpec((head_local, block, head_dim), lambda i, order_ref: (0, i, 0))
    mem_rows = pl.BlockSpec(
        (head_local, groups * mem_count, head_dim), lambda i, order_ref: (0, i, 0)
    )
    return call(
        kernel,
        (count,),
        [rows, full, full_t, mem_rows, mem_rows],
        [pl.BlockSpec((block, head_local * head_dim), lambda i, order_ref: (0, 0))] * count
        + [pl.BlockSpec((2, 8, half), lambda i, order_ref: (i, 0, 0))],
        [struct((block, head_local * head_dim), bf16)] * count
        + [struct((2 * count, 8, half), f32)],
        4 * head_local * length * length * head_dim,
        12 * head_local * length * head_dim,
        prefetch=1,
    )(order, query, key, value_t, memory_keys, memory_values)


def attend_back(
    order, query, key, value, memory_keys, memory_values, mem_block, mem_count, grads, attended, lse,
    cosine, sine, first, last, carried=None,
):
    head_local, length, head_dim = query.shape
    count, _, block = lse.shape
    pieces = len(grads)
    piece = length // pieces
    per = piece // block
    groups = block // mem_block
    scale = head_dim ** (-0.5)
    factor = scale * log2e
    opening, closing = first == 0, last == count

    def kernel(order_ref, q_ref, k_ref, v_ref, mk_ref, mv_ref, *refs):
        g_refs, refs = refs[:pieces], refs[pieces:]
        if opening:
            o_refs, refs = refs[:pieces], refs[pieces:]
        else:
            (part_ref, delta), refs = refs[:2], refs[5:]
        (lse_ref, c_ref, s_ref, dq_ref, dk_ref, dv_ref), refs = refs[:6], refs[6:]
        if opening and not closing:
            (rest_ref, delta), refs = refs[:2], refs[2:]
        elif opening:
            delta, refs = refs[0], refs[1:]
        dq_acc, do_ref = refs
        index = pl.program_id(0) + first

        def cols(head):
            return slice(head * head_dim, (head + 1) * head_dim)

        @pl.when(index == first)
        def _():
            for k in range(pieces):
                start = pl.multiple_of(order_ref[k] * piece, piece)
                do_ref[pl.ds(start, piece), :] = g_refs[k][...]
            if not opening:
                dq_acc[:, :, first * block :] = part_ref[...]
            else:
                for k in range(pieces):
                    for p in range(per):
                        rows = slice(p * block, (p + 1) * block)
                        for head in range(head_local):
                            do = g_refs[k][rows, cols(head)].astype(f32)
                            o = o_refs[k][rows, cols(head)].astype(f32)
                            row = jnp.sum((do * o).T, axis=0, keepdims=True)
                            delta[order_ref[k] * per + p, head : head + 1, :] = row

        row_id = lax.broadcasted_iota(jnp.int32, (block, block), 0)
        col_id = lax.broadcasted_iota(jnp.int32, (block, block), 1)
        keys_t = [k_ref[head].T for head in range(head_local)]

        def memory(head):
            start = pl.multiple_of(index * block, block)
            q = q_ref[head, pl.ds(start, block), :]
            do = do_ref[pl.ds(start, block), cols(head)]
            mk_t = mk_ref[head].T
            parts = []
            for g in range(groups):
                lanes = slice(g * mem_block, (g + 1) * mem_block)
                slots = slice(g * mem_count, (g + 1) * mem_count)
                scores = dot_nt(mk_ref[head, slots, :], q[lanes])
                weight = jnp.exp2(scores * factor - lse_ref[index, head : head + 1, lanes])
                dp = dot_nt(mv_ref[head, slots, :], do[lanes])
                ds = (weight * (dp - delta[index, head : head + 1, lanes])).astype(bf16)
                parts.append(dot(mk_t[:, slots], ds))
            return jnp.concatenate(parts, axis=1)

        def step(head, carry, i, masked):
            dk, dv = carry
            start = pl.multiple_of(i * block, block)
            q = q_ref[head, pl.ds(start, block), :]
            do = do_ref[pl.ds(start, block), cols(head)]
            k, v = k_ref[head], v_ref[head]
            weight = jnp.exp2(dot_nt(k, q) * factor - lse_ref[i, head : head + 1, :])
            if masked:
                weight = jnp.where(row_id <= col_id, weight, 0.0)
            dp = dot_nt(v, do)
            ds = (weight * (dp - delta[i, head : head + 1, :])).astype(bf16)
            dv = dv + dot(weight.astype(bf16), do)
            dk = dk + dot(ds, q)
            so_far = dq_acc[head, :, pl.ds(start, block)]
            if opening:
                so_far = jnp.where(index == 0, 0.0, so_far)
            total = so_far + dot(keys_t[head], ds)
            if masked:
                return dk, dv, total
            dq_acc[head, :, pl.ds(start, block)] = total
            return dk, dv

        cos, sin = c_ref[...], s_ref[...]

        def unrotate(grad_rows):
            u = (grad_rows * scale).astype(bf16).astype(f32)
            return (u * cos - pltpu.roll(u, head_dim // 2, 1) * sin).astype(bf16)

        zero = jnp.zeros((block, head_dim), f32)
        carries = []
        for head in range(head_local):
            dk, dv, dq = step(head, (zero, zero), index, True)
            dq_ref[:, cols(head)] = unrotate((dq + memory(head)).T)
            carries.append((dk, dv))
        carries = lax.fori_loop(
            index + 1,
            count,
            lambda i, c: tuple(step(head, c[head], i, False) for head in range(head_local)),
            tuple(carries),
        )
        for head, (dk, dv) in enumerate(carries):
            dk_ref[:, cols(head)] = unrotate(dk)
            dv_ref[:, cols(head)] = dv.astype(bf16)
        if opening and not closing:
            @pl.when(index == last - 1)
            def _():
                rest_ref[...] = dq_acc[:, :, last * block :]

    group = head_local * head_dim
    full = resident((head_local, length, head_dim), (0, 0, 0))
    flat = resident((piece, group), (0, 0))
    rows = pl.BlockSpec((head_local, block, head_dim), lambda i, o: (0, i + first, 0))
    mem_rows = pl.BlockSpec(
        (head_local, groups * mem_count, head_dim), lambda i, o: (0, i + first, 0)
    )
    table = pl.BlockSpec((block, head_dim), lambda i, o: (i + first, 0))
    out_rows = pl.BlockSpec((block, group), lambda i, o: (i + first, 0))
    out = struct((length, group), bf16)
    aliases = {}
    small = resident(lse.shape, (0, 0, 0))
    in_specs = [full, rows, rows, mem_rows, mem_rows] + [flat] * pieces
    inputs = [query, key, value, memory_keys, memory_values, *grads]
    out_specs, out_shape, scratch = [out_rows] * 3, [out] * 3, []
    if opening:
        in_specs += [flat] * pieces
        inputs += list(attended)
        if closing:
            scratch.append(pltpu.VMEM(lse.shape, f32))
        else:
            rest = (head_local, head_dim, length - last * block)
            out_specs += [pl.BlockSpec(rest, lambda i, o: (0, 0, 0)), pl.BlockSpec(lse.shape, lambda i, o: (0, 0, 0))]
            out_shape += [struct(rest, f32), struct(lse.shape, f32)]
    else:
        in_specs += [resident(carried[0].shape, (0, 0, 0)), small]
        in_specs += [pl.BlockSpec(memory_space=pl.ANY)] * 3
        aliases = {1 + len(inputs) + 2 + k: k for k in range(3)}
        inputs += list(carried)
    done = sum(count - j for j in range(first, last)) / (count * (count + 1) / 2)
    return call(
        kernel,
        (last - first,),
        in_specs + [small, table, table],
        out_specs,
        out_shape,
        done * 10 * head_local * length * length * head_dim // 2,
        24 * head_local * length * head_dim,
        scratch=scratch
        + [pltpu.VMEM((head_local, head_dim, length), f32), pltpu.VMEM((length, group), bf16)],
        prefetch=1,
        aliases=aliases,
    )(order, *inputs, lse, cosine, sine)


def mix(order, attended, weights, first, tokens, gain_row, places):
    count = len(attended)
    rows, group = attended[0].shape
    width = tokens.shape[1]
    block = min(256, rows)
    parts = width // 256

    def kernel(order_ref, *refs):
        a_refs = refs[:count]
        w_refs, refs = refs[count : count + parts], refs[count + parts :]
        x_ref, g_ref, res_ref, n_ref, nt_ref, at_ref = refs
        residual = x_ref[...].astype(f32)
        mixed = [None] * parts
        for k in range(count):
            start = pl.multiple_of(order_ref[k] * group, group)
            for c in range(parts):
                part = dot(a_refs[k][...], w_refs[c][pl.ds(start, group), :])
                mixed[c] = part if mixed[c] is None else mixed[c] + part
            at_ref[pl.ds(start, group), :] = a_refs[k][...].T
        residual = residual + jnp.concatenate(mixed, axis=1)
        scale = lax.rsqrt(jnp.mean(residual * residual, axis=-1, keepdims=True) + epsilon)
        normed = (residual * scale * g_ref[...]).astype(bf16)
        res_ref[...] = residual
        n_ref[...] = normed
        normed_t = normed.T
        size = width // len(places)
        for source, place in enumerate(places):
            nt_ref[place * size : (place + 1) * size, :] = normed_t[source * size : (source + 1) * size]

    rows_spec = pl.BlockSpec((block, width), lambda i, o: (i, 0))
    cols_spec = pl.BlockSpec((width, block), lambda i, o: (0, i))
    return call(
        kernel,
        (rows // block,),
        [pl.BlockSpec((block, group), lambda i, o: (i, 0))] * count
        + column_blocks(width, first, parts)
        + [rows_spec, resident((1, width), (0, 0))],
        [rows_spec, rows_spec, cols_spec, cols_spec],
        [struct((rows, width), f32), struct((rows, width), bf16)]
        + [struct((width, rows), bf16)] * 2,
        2 * rows * width * width,
        16 * rows * width,
        prefetch=1,
    )(order, *attended, *[weights] * parts, tokens, gain_row)


def gated(normed, cotangent, weights, first, hidden_cols):
    rows, width = normed.shape
    block = 256

    def kernel(n_ref, c_ref, wg_ref, wu_ref, wd_ref, h_ref, gg_ref, gu_ref):
        normed_block = n_ref[...]
        gate = dot(normed_block, wg_ref[...])
        up = dot(normed_block, wu_ref[...])
        grad = dot(c_ref[...], wd_ref[...])
        sg = 1.0 / (1.0 + jnp.exp(-gate))
        silu = gate * sg
        h_ref[...] = (silu * up).astype(bf16)
        gg_ref[...] = (grad * up * sg * (1.0 + gate * (1.0 - sg))).astype(bf16)
        gu_ref[...] = (grad * silu).astype(bf16)

    def weight_spec(k):
        offset = (first + k * hidden_cols) // block
        return pl.BlockSpec((width, block), lambda i: (0, i + offset))

    flat = resident((rows, width), (0, 0))
    out_spec = pl.BlockSpec((rows, block), lambda i: (0, i))
    return call(
        kernel,
        (hidden_cols // block,),
        [flat, flat] + [weight_spec(k) for k in range(3)],
        [out_spec] * 3,
        [struct((rows, hidden_cols), bf16)] * 3,
        6 * rows * width * hidden_cols,
        6 * (rows + width) * hidden_cols,
    )(normed, cotangent, weights, weights, weights)


def norm_back(order, grads, weights, first, residual, cotangent, gain_row):
    rows, width = residual.shape
    count = order.shape[0]
    block = min(256, rows)
    steps = width // block
    row_steps = rows // block
    group = width // count
    parts = width // 256
    n_grads = len(grads)

    def kernel(order_ref, *refs):
        g_refs, w_refs = refs[:n_grads], refs[n_grads : 2 * n_grads]
        wo_refs, refs = refs[2 * n_grads : 2 * n_grads + parts], refs[2 * n_grads + parts :]
        r_ref, c_ref, gain_ref, gres_ref, gb_ref = refs[:5]
        gm_refs, acc = refs[5 : 5 + count], refs[5 + count]
        step = pl.program_id(0)

        @pl.when(step < steps)
        def _():
            total = dot_nt(g_refs[0][...], w_refs[0][...])
            for k in range(1, n_grads):
                total = total + dot_nt(g_refs[k][...], w_refs[k][...])
            for d in range(steps):
                @pl.when(step == d)
                def _():
                    acc[:, d * block : (d + 1) * block] = total

        @pl.when(step >= steps)
        def _():
            start = pl.multiple_of((step - steps) * block, block)
            grad = acc[pl.ds(start, block), :]
            res = r_ref[...]
            scale = lax.rsqrt(jnp.mean(res * res, axis=-1, keepdims=True) + epsilon)
            unit = res * scale
            scaled = grad * gain_ref[...]
            inner = jnp.mean(scaled * unit, axis=-1, keepdims=True)
            gres = c_ref[...].astype(f32) + scale * (scaled - unit * inner)
            gres_ref[...] = gres
            branch = gres.astype(bf16)
            gb_ref[...] = branch
            for k in range(count):
                start_k = pl.multiple_of(order_ref[k] * group, group)
                mixed = None
                for c in range(parts):
                    part = dot_nt(
                        branch[:, c * 256 : (c + 1) * 256], wo_refs[c][pl.ds(start_k, group), :]
                    )
                    mixed = part if mixed is None else mixed + part
                gm_refs[k][...] = mixed.astype(bf16)

    def row(i):
        return jnp.maximum(i - steps, 0)

    rows_spec = pl.BlockSpec((block, width), lambda i, o: (row(i), 0))
    weight_specs = [
        pl.BlockSpec(
            (block, grads[k].shape[1]),
            functools.partial(lambda c, i, o: (jnp.minimum(i, steps - 1), c), k),
        )
        for k in range(n_grads)
    ]
    hidden_cols = sum(g.shape[1] for g in grads)
    return call(
        kernel,
        (steps + row_steps,),
        [resident(g.shape, (0, 0)) for g in grads]
        + weight_specs
        + column_blocks(width, first, parts)
        + [rows_spec, rows_spec, resident((1, width), (0, 0))],
        [
            rows_spec,
            rows_spec,
        ]
        + [pl.BlockSpec((block, group), lambda i, o: (row(i), 0))] * count,
        [
            struct((rows, width), f32),
            struct((rows, width), bf16),
        ]
        + [struct((rows, group), bf16)] * count,
        2 * rows * width * hidden_cols + 2 * rows * width * width,
        2 * (rows + width) * hidden_cols + 16 * rows * width,
        scratch=[pltpu.VMEM((rows, width), f32)],
        prefetch=1,
    )(order, *grads, *[weights] * (n_grads + parts), residual, cotangent, gain_row)


def products(select, lefts, rights, parts, added=None, joined=False, halves=None):
    height = lefts[0].shape[0]
    block = min(256, height) if halves is None else height // 4
    n = len(rights)
    sizes = [r.shape[1] // p for r, p in zip(rights, parts)]
    added = added or []
    distinct = []
    for left in lefts:
        if not any(left is d for d in distinct):
            distinct.append(left)
    which = [next(i for i, d in enumerate(distinct) if d is left) for left in lefts]
    n_left, n_add = len(distinct), len(added)

    def kernel(select_ref, *refs):
        l_refs, r_refs, outs = refs[:n_left], refs[n_left : n_left + n], refs[n_left + n + n_add :]
        for k in range(n):
            total = dot(l_refs[which[k]][...], r_refs[k][...])
            if k < n_add:
                total = total + refs[n_left + n + k][...].astype(f32)
            if halves is not None:
                step, mine = pl.program_id(0), select_ref[1 + k]
                keep = (step // 2 if halves[k] == 0 else step % 2) == mine
                for cond, out in ((keep, outs[k]), (jnp.logical_not(keep), outs[n + k])):
                    @pl.when(cond)
                    def _():
                        out[...] = total.astype(bf16)
            elif joined:
                start = sum(sizes[:k])
                outs[0][:, start : start + sizes[k]] = total.astype(bf16)
            else:
                outs[k][...] = total.astype(bf16)

    def right_spec(k):
        return pl.BlockSpec(
            (rights[k].shape[0], sizes[k]),
            lambda i, s: (0, s[0] if parts[k] > 1 else 0),
            pipeline_mode=pl.Buffered(1),
        )

    out_sizes = [sum(sizes)] if joined else sizes
    out_specs = [pl.BlockSpec((block, size), lambda i, s: (i, 0)) for size in out_sizes]
    add_specs = out_specs[:n_add]
    out_shape = [struct((height, size), bf16) for size in out_sizes]
    if halves is not None:

        def half_spec(k, kept):
            def index(i, s):
                value = s[1 + k] if kept else 1 - s[1 + k]
                return (jnp.clip(i - 2 * value, 0, 1) if halves[k] == 0 else i // 2, 0)

            return pl.BlockSpec((block, sizes[k]), index)

        out_specs = [half_spec(k, kept) for kept in (True, False) for k in range(n)]
        out_shape = [struct((height // 2, size), bf16) for size in sizes] * 2
    return call(
        kernel,
        (height // block,),
        [pl.BlockSpec((block, d.shape[1]), lambda i, s: (i, 0)) for d in distinct]
        + [right_spec(k) for k in range(n)]
        + add_specs,
        out_specs,
        out_shape,
        sum(2 * height * r.shape[0] * size for r, size in zip(rights, sizes)),
        2 * height * sum(sizes) + sum(2 * r.shape[0] * size for r, size in zip(rights, sizes)),
        prefetch=1,
    )(select, *distinct, *rights, *added)


def finish(residual, hidden, weights, first):
    rows, width = residual.shape
    block = min(256, rows)
    hidden_cols = hidden.shape[1]

    def kernel(r_ref, h_ref, w_ref, out_ref):
        out_ref[...] = (r_ref[...] + dot_nt(h_ref[...], w_ref[...])).astype(bf16)

    rows_spec = pl.BlockSpec((block, width), lambda i: (i, 0))
    return call(
        kernel,
        (rows // block,),
        [
            rows_spec,
            pl.BlockSpec((block, hidden_cols), lambda i: (i, 0)),
            resident((width, hidden_cols), (0, first)),
        ],
        rows_spec,
        struct((rows, width), bf16),
        2 * rows * width * hidden_cols,
        6 * rows * width + 2 * (rows + width) * hidden_cols,
    )(residual, hidden, weights)


def project_back(order, slot, grads, weights, added=(), part=(0, 1), last=None, into=None):
    length, group = grads[0].shape
    width = weights.shape[0]
    piece = length // order.shape[0]
    rows = piece // part[1]
    block = min(512 if last is None else 256, rows)
    steps = rows // block
    before = part[0] * steps
    n = len(added)

    def kernel(order_ref, a_ref, b_ref, c_ref, w_ref, *refs):
        total = dot_nt(a_ref[...], w_ref[:, :group])
        total = total + dot_nt(b_ref[...], w_ref[:, group : 2 * group])
        total = total + dot_nt(c_ref[...], w_ref[:, 2 * group :])
        for ref in refs[:n]:
            total = total + ref[...].astype(f32)
        if last is not None:
            x_ref, gain_ref, g_ref = refs[n : n + 3]
            x = x_ref[...].astype(f32)
            scale = lax.rsqrt(jnp.mean(x * x, axis=-1, keepdims=True) + epsilon)
            unit = x * scale
            scaled = total * gain_ref[...]
            inner = jnp.mean(scaled * unit, axis=-1, keepdims=True)
            total = g_ref[...] + scale * (scaled - unit * inner)
        refs[-1][...] = total.astype(bf16)

    def rows_of(array):
        first = before if array.shape[0] == piece else 0
        return pl.BlockSpec((block, width), lambda i, order_ref: (i + first, 0))

    def grad_rows(i, order_ref):
        return (order_ref[slot] * (piece // block) + before + i, 0)

    inputs = [*grads, weights, *added]
    in_specs = [pl.BlockSpec((block, group), grad_rows)] * 3 + [resident(weights.shape, (0, 0))]
    in_specs += [rows_of(a) for a in added]
    aliases = {}
    out = struct((rows, width), bf16)
    if last is not None:
        out = struct((piece, width), bf16)
        inputs += last
        in_specs += [rows_of(last[0]), resident((1, width), (0, 0)), rows_of(last[2])]
        if into is not None:
            aliases = {1 + len(inputs): 0}
            inputs.append(into)
            in_specs.append(pl.BlockSpec(memory_space=pl.ANY))
    return call(
        kernel,
        (steps,),
        in_specs,
        rows_of(out),
        out,
        6 * rows * width * group,
        2 * rows * (2 * width + 3 * group),
        prefetch=1,
        aliases=aliases,
    )(order, *inputs)


def pair_add(a, b):
    return (a.astype(f32) + b.astype(f32)).astype(bf16)


def axis_bits(axis, first=1):
    bits = []
    while first < lax.axis_size(axis):
        bits.append(first)
        first *= 2
    return bits


def trade(array, dim, axis, bit):
    count = lax.axis_size(axis)
    mine = (lax.axis_index(axis) // bit) % 2
    keep = lax.dynamic_index_in_dim(array, mine, axis=dim, keepdims=False)
    give = lax.dynamic_index_in_dim(array, 1 - mine, axis=dim, keepdims=False)
    return keep, lax.ppermute(give, axis, [(i, i ^ bit) for i in range(count)])


def scatter_start(array, turn, halve_at):
    count = lax.axis_size("fsdp")
    bits = axis_bits("fsdp")
    bits = bits[turn % len(bits) :] + bits[: turn % len(bits)]
    left = axis_bits("fsdp")[::-1]
    array = array.reshape((2,) * len(bits) + (array.shape[0] // count, array.shape[1]))
    todo = [("fsdp", bit) for bit in bits]
    if halve_at is not None:
        todo[halve_at:halve_at] = [("seq", bit) for bit in axis_bits("seq", 2)]
    return exchange((array, None, todo, left))


def scatter_from(keep, give, axis, bit, left, todo, rows):
    count = lax.axis_size(axis)
    got = lax.ppermute(give, axis, [(i, i ^ bit) for i in range(count)])
    shape = (2,) * len(left) + (rows, keep.shape[1])
    return keep.reshape(shape), got.reshape(shape), todo, left


def exchange(state):
    array, _, todo, left = state
    if not todo:
        return state
    axis, bit = todo[0]
    if axis == "fsdp":
        pair = trade(array, left.index(bit), axis, bit)
        left = [b for b in left if b != bit]
    else:
        rows, n = array.shape[-2:]
        array = array.reshape(array.shape[:-2] + (2, rows // 2, n))
        pair = trade(array, array.ndim - 3, axis, bit)
    return (*pair, todo[1:], left)


def settle(states, done, ahead):
    keeps, done = lax.optimization_barrier(([state[0] for state in states], done))
    arrays = [
        keep if state[1] is None else pair_add(keep, state[1])
        for keep, state in zip(keeps, states)
    ]
    arrays, ahead = lax.optimization_barrier((arrays, ahead))
    return [(a, None) + state[2:] for a, state in zip(arrays, states)], done, ahead


def rows_whole(array, other):
    first = (lax.axis_index("seq") // 2) % 2 == 0
    return both_ways(array, other, first).reshape(-1, array.shape[1])


def last_rows(state):
    return state[0].reshape(state[0].shape[-2:])


def both_ways(own, other, first):
    return jnp.stack([jnp.where(first, own, other), jnp.where(first, other, own)])


def feedforward_ends(half, joined, other, gate_weight, up_weight, gain):
    rows, hidden_cols = gate_weight.shape
    width = joined.shape[1] - 3 * (hidden_cols // 2)
    size = hidden_cols // 2

    def kernel(half_ref, j_ref, o_ref, wg_ref, wu_ref, gain_ref, g_ref, u_ref, d_ref, out_ref, gg_ref):
        def both(k):
            columns = slice(k * size, (k + 1) * size)
            own, far = j_ref[:, columns].astype(f32), o_ref[:, columns].astype(f32)
            lower = half_ref[0] == 0
            return jnp.concatenate(
                [jnp.where(lower, own, far), jnp.where(lower, far, own)], axis=1
            )

        down, gate, up = both(0), both(1), both(2)
        g_ref[...] = gate
        u_ref[...] = up
        d_ref[...] = down.T
        out_ref[...] = j_ref[:, 3 * size :].astype(f32) + o_ref[:, 3 * size :].astype(f32)
        total = jnp.sum(
            wg_ref[...].astype(f32) * gate + wu_ref[...].astype(f32) * up, axis=1, keepdims=True
        )
        gg_ref[...] = total / gain_ref[...]

    whole = lambda shape: pl.BlockSpec(shape, lambda i, h: (0, 0))
    shapes = [(rows, hidden_cols)] * 2 + [(hidden_cols, rows), (rows, width), (rows, 1)]
    *ends, gain_grad = call(
        kernel,
        (1,),
        [whole(joined.shape)] * 2 + [whole(gate_weight.shape)] * 2 + [whole((rows, 1))],
        [whole(shape) for shape in shapes],
        [struct(shape, f32) for shape in shapes],
        4 * rows * hidden_cols,
        20 * rows * hidden_cols,
        prefetch=1,
    )(half, joined, other, gate_weight, up_weight, gain.astype(f32)[:, None])
    return *ends, gain_grad[:, 0]


def projection_ends(order, pieces, weights, gain):
    rows, width = weights[0].shape
    count = len(pieces)
    group = width // count

    def kernel(order_ref, *refs):
        p_refs, refs = refs[:count], refs[count:]
        w_refs, gain_ref, outs, gg_ref = refs[:3], refs[3], refs[4:7], refs[7]
        for k in range(count):
            start = pl.multiple_of(order_ref[k] * group, group)
            for j in range(3):
                outs[j][:, pl.ds(start, group)] = p_refs[k][
                    :, j * group : (j + 1) * group
                ].astype(f32)
        total = None
        for j in range(3):
            part = jnp.sum(w_refs[j][...].astype(f32) * outs[j][...], axis=1, keepdims=True)
            total = part if total is None else total + part
        gg_ref[...] = total / gain_ref[...]

    whole = lambda shape: pl.BlockSpec(shape, lambda i, o: (0, 0))
    shapes = [(rows, width)] * 3 + [(rows, 1)]
    *ends, gain_grad = call(
        kernel,
        (1,),
        [whole(pieces[0].shape)] * count + [whole((rows, width))] * 3 + [whole((rows, 1))],
        [whole(shape) for shape in shapes],
        [struct(shape, f32) for shape in shapes],
        6 * rows * width,
        24 * rows * width,
        prefetch=1,
    )(order, *pieces, *weights, gain.astype(f32)[:, None])
    return *ends, gain_grad[:, 0]


def body(
    tokens, cotangent, query_weight, key_weight, value_weight, output_weight, gate_weight, up_weight,
    down_weight, attention_gain, feedforward_gain, cache_keys, cache_values, memory_rows, memory_docs,
):
    seq_count, fsdp_count = lax.axis_size("seq"), lax.axis_size("fsdp")
    here = lax.axis_index("seq")
    tok_rows, width = tokens.shape
    head_local, rows_cache, head_dim = cache_keys.shape[1:]
    group = head_local * head_dim
    length = tok_rows * seq_count
    mem_block = length // memory_rows.shape[2]
    mem_count = memory_rows.shape[3]
    shard = query_weight.shape[0]
    hidden_cols = gate_weight.shape[1]
    order = here ^ jnp.arange(seq_count, dtype=jnp.int32)

    gains = spread(jnp.stack([attention_gain, feedforward_gain]), "fsdp")
    gains = gains.transpose(1, 0, 2).reshape(2, width).astype(f32)
    gain_one, gain_two = gains[0:1], gains[1:2]
    own_cols = [
        lax.dynamic_slice_in_dim(w, here * group, group, axis=1)
        for w in (query_weight, key_weight, value_weight)
    ]
    qkv = spread(jnp.concatenate(own_cols, axis=1), "fsdp").reshape(width, 3 * group)

    pieces = [tokens, swap_seq(tokens, 1), swap_seq(tokens, 2)]
    pieces.append(swap_seq(pieces[2], 1))

    ring = [(i, (i + 1) % fsdp_count) for i in range(fsdp_count)]
    partner_keys = lax.ppermute(cache_keys[0], "fsdp", ring)
    partner_values = lax.ppermute(cache_values[0], "fsdp", ring)

    part = shard // seq_count

    def own_rows(w):
        return lax.dynamic_slice_in_dim(w, here * part, part, axis=0)

    own_wd = lax.dynamic_slice_in_dim(down_weight, here * part, part, axis=1).T
    own_part = jnp.concatenate(
        [own_rows(gate_weight), own_rows(up_weight), own_wd, own_rows(output_weight)], axis=1
    )
    big = lax.all_gather(own_part, ("fsdp", "seq"), axis=0, tiled=True)

    half = head_dim // 2
    frequency = 10000.0 ** (-2.0 * jnp.arange(half, dtype=f32) / head_dim)
    angles = jnp.arange(length, dtype=jnp.int32).astype(f32)[:, None] * frequency[None, :]
    cos_half, sin_half = jnp.cos(angles), jnp.sin(angles)
    cosine = jnp.concatenate([cos_half, cos_half], axis=1)
    sine = jnp.concatenate([-sin_half, sin_half], axis=1)
    cotangent_t = cotangent.T.reshape(fsdp_count, 2, shard // 2, tok_rows)
    cotangent_t = cotangent_t.swapaxes(0, 1).reshape(width, tok_rows)
    places = [
        (f % 4 // 2 + f % 2 * 2) * (fsdp_count // 4) + f // 4 for f in range(fsdp_count)
    ]

    chosen = memory_docs[0] * rows_cache + memory_rows[0]
    picked = retrieve(chosen, cache_keys[0], cache_values[0], 0)
    query, key, value, value_t, normed_one_t = project(
        order, pieces, qkv, gain_one, cosine, sine, head_local, head_dim
    )
    picked_keys, picked_values = retrieve(chosen, partner_keys, partner_values, rows_cache, picked)
    *attended_heads, lse = attend(
        order, query, key, value_t, picked_keys, picked_values, mem_block, mem_count, seq_count
    )

    def by_distance(stack):
        return [stack[0]] + [swap_seq(stack[k], k) for k in range(1, seq_count)]

    attended = by_distance(attended_heads)
    residual, normed_two, normed_two_t, attended_t = mix(
        order, attended, big, 3 * hidden_cols, tokens, gain_two, places
    )
    hid, gg, gu = gated(normed_two, cotangent, big, 0, hidden_cols)
    own_half, other_half = (here % 2)[None].astype(jnp.int32), (1 - here % 2)[None].astype(jnp.int32)
    lefts, rights = [cotangent_t, normed_two_t, normed_two_t], [hid, gg, gu]
    given = products(other_half, lefts, rights, (2, 2, 2))
    given, gg_later = lax.optimization_barrier((given, gg))
    got = [swap_seq(g, 1) for g in given]
    grad_residual, grad_branch, *grad_mixed = norm_back(
        order, [gg_later, gu], big, 3 * hidden_cols, residual, cotangent, gain_two
    )
    grad_heads = by_distance(grad_mixed)
    bits, upper = axis_bits("fsdp"), axis_bits("seq", 2)
    firsts = (("seq", upper[0]), ("fsdp", bits[0]), ("fsdp", bits[1]), ("fsdp", bits[-1]))
    mine = [(lax.axis_index(axis) // bit) % 2 for axis, bit in firsts]
    select = jnp.stack([here % 2, *mine]).astype(jnp.int32)
    own = products(
        select, [*lefts, attended_t], [*rights, grad_branch], (2, 2, 2, 1), got, halves=(0, 0, 1, 0)
    )
    grad_heads, own = lax.optimization_barrier((grad_heads, own))
    down = bits[::-1]
    over = lambda *picks: [("fsdp", b) if b else ("seq", upper[0]) for b in picks]
    sums = [
        scatter_from(keep, give, axis, bit, left, todo, rows)
        for keep, give, (axis, bit), left, todo, rows in zip(
            own[:4],
            own[4:],
            firsts,
            (down, [bits[1], *down[: -2]], [bits[0], *down[: -2]], down[1:]),
            (
                over(*bits),
                over(0, *bits[1:]),
                over(0, bits[0], *bits[2:]),
                over(*bits[:-1], 0),
            ),
            (shard // 2, shard, shard, shard),
        )
    ]

    blocks = lse.shape[0]
    middle = 3 * blocks // 8
    attention = (order, query, key, value, picked_keys, picked_values, mem_block, mem_count)
    *grads, rest, delta = attend_back(
        *attention, grad_heads, attended_heads, lse, cosine, sine, 0, middle
    )
    sums, _, (rest, delta) = settle(sums, (), (rest, delta))
    sums = [exchange(g) for g in sums]
    grads = attend_back(
        *attention, grad_heads, None, lse, cosine, sine, middle, blocks, (rest, delta, *grads)
    )

    zero = jnp.zeros((1,), jnp.int32)
    sums, _, grads = settle(sums, (), grads)
    sums = [exchange(g) for g in sums]
    far_part = project_back(order, 3, grads, qkv)
    far = swap_seq(far_part, 1)
    far_part, grads = lax.optimization_barrier((far_part, grads))
    near_part = project_back(order, 1, grads, qkv)
    near = swap_seq(near_part, 1)
    far, near_part, grads = lax.optimization_barrier((far, near_part, grads))
    half = project_back(order, 2, grads, qkv, [far], (0, 2))
    across = [swap_seq(half, 2)]
    half, grads = lax.optimization_barrier((half, grads))
    half = project_back(order, 2, grads, qkv, [far], (1, 2))
    across.append(swap_seq(half, 2))
    half, grads = lax.optimization_barrier((half, grads))
    (qkv_grad,) = products(zero, [normed_one_t] * 3, list(grads), (1, 1, 1), joined=True)
    qkv_state = scatter_start(qkv_grad, 0, None)
    across[0], qkv_grad, grads = lax.optimization_barrier((across[0], qkv_grad, grads))
    sums, across[0], near = settle(sums, across[0], near)
    sums = [exchange(g) for g in sums]
    (qkv_state, *sums), _, near = settle([qkv_state, *sums], (), near)
    while any(state[2] for state in sums):
        sums = settle([exchange(g) for g in sums], (), ())[0]
    qkv_state = exchange(qkv_state)
    joined = jnp.concatenate([last_rows(state) for state in sums], axis=1)
    lower = swap_seq(joined, upper[0])
    last = (tokens, gain_one, grad_residual)
    grad_tokens = project_back(order, 0, grads, qkv, [near, across[0]], (0, 2), last)
    (qkv_state,), grad_tokens, (hid, across[1]) = settle(
        [qkv_state], grad_tokens, (hid, across[1])
    )
    qkv_state = exchange(qkv_state)
    result = finish(residual, hid, big, 2)
    grad_tokens = project_back(
        order, 0, grads, qkv, [near, across[1]], (1, 2), last, grad_tokens
    )
    joined, grad_tokens = lax.optimization_barrier((joined, grad_tokens))
    joined = rows_whole(joined, lower)
    other = swap_seq(joined, 1)
    (qkv_state,), _, _ = settle([qkv_state], (result, grad_tokens), ())
    while qkv_state[2]:
        qkv_state = settle([exchange(qkv_state)], (), ())[0][0]
    qkv_pieces = by_distance([last_rows(qkv_state)] * seq_count)
    grad_gate, grad_up, grad_down, grad_out, grad_gain_two = feedforward_ends(
        own_half, joined, other, gate_weight, up_weight, feedforward_gain
    )
    qkv_pieces[0], grad_out = lax.optimization_barrier((qkv_pieces[0], grad_out))
    grad_q, grad_k, grad_v, grad_gain_one = projection_ends(
        order, qkv_pieces, (query_weight, key_weight, value_weight), attention_gain
    )
    return (
        result,
        grad_tokens,
        grad_q,
        grad_k,
        grad_v,
        grad_out,
        grad_gate,
        grad_up,
        grad_down,
        grad_gain_one,
        grad_gain_two,
    )


def solution(mesh):
    tok, row, col, one = P(("fsdp", "seq"), None), P("fsdp", None), P(None, "fsdp"), P("fsdp")
    cache = P("fsdp", "seq", None, None)
    return jax.shard_map(
        body,
        mesh=mesh,
        in_specs=(tok, tok) + (row,) * 6 + (col, one, one) + (cache,) * 4,
        out_specs=(tok, tok) + (row,) * 6 + (col, one, one),
        check_vma=False,
    )
```

```python
import functools

import jax
import jax.numpy as jnp
from jax import lax
from jax.experimental import pallas as pl
from jax.experimental.pallas import tpu as pltpu
from jax.sharding import PartitionSpec as P

epsilon = 1e-06
log2e = 1.4426950408889634
f32 = jnp.float32
bf16 = jnp.bfloat16
VMEM_LIMIT = 60 * 1024 * 1024
hint = 0.15


def dot(a, b):
    return jnp.dot(a, b, preferred_element_type=f32)


def dot_nt(a, b):
    return lax.dot_general(a, b, (((1,), (1,)), ((), ())), preferred_element_type=f32)


def dot_tn(a, b):
    return lax.dot_general(a, b, (((0,), (0,)), ((), ())), preferred_element_type=f32)


def call(
    kernel, grid, in_specs, out_specs, out_shape, flops, bytes_accessed, scratch=(), prefetch=0, aliases=None
):
    return pl.pallas_call(
        kernel,
        name=kernel.__qualname__.split(".")[0],
        grid_spec=pltpu.PrefetchScalarGridSpec(
            num_scalar_prefetch=prefetch,
            grid=grid,
            in_specs=in_specs,
            out_specs=out_specs,
            scratch_shapes=list(scratch),
        ),
        out_shape=out_shape,
        input_output_aliases=aliases or {},
        compiler_params=pltpu.CompilerParams(
            dimension_semantics=("arbitrary",) * len(grid), vmem_limit_bytes=VMEM_LIMIT
        ),
        cost_estimate=pl.CostEstimate(
            flops=int(flops * hint), bytes_accessed=int(bytes_accessed * hint), transcendentals=0
        ),
    )


def resident(shape, index):
    return pl.BlockSpec(shape, lambda *_: index, pipeline_mode=pl.Buffered(1))


def column_blocks(height, first, parts):
    return [resident((height, 256), (0, first // 256 + c)) for c in range(parts)]


def struct(shape, dtype):
    return jax.ShapeDtypeStruct(shape, dtype)


def swap_seq(array, bit):
    count = lax.axis_size("seq")
    return lax.ppermute(array, "seq", [(i, i ^ bit) for i in range(count)])


def spread(array, axis):
    count = lax.axis_size(axis)
    copies = jnp.broadcast_to(array[None], (count,) + array.shape)
    return lax.all_to_all(copies, axis, split_axis=0, concat_axis=0, tiled=True)


def project(order, pieces, weights, gain_row, cosine, sine, head_local, head_dim):
    rows, width = pieces[0].shape
    count = len(pieces)
    block = min(512, rows)
    steps = rows // block
    length = rows * count
    cols = weights.shape[1]
    group = head_local * head_dim

    def kernel(order_ref, *refs):
        xs = refs[:count]
        w_ref, g_ref, c_ref, s_ref, q_ref, k_ref, v_ref, vt_ref, nt_ref, x_block = refs[count:]
        slot = pl.program_id(0)

        def run(x_ref):
            x = x_ref[...].astype(f32)
            scale = lax.rsqrt(jnp.mean(x * x, axis=-1, keepdims=True) + epsilon)
            normed = (x * scale * g_ref[...]).astype(bf16)
            nt_ref[...] = normed.T
            lin = dot(normed, w_ref[...])
            cos, sin = c_ref[...], s_ref[...]
            for head in range(head_local):
                for part, out in ((0, q_ref), (1, k_ref)):
                    start = part * group + head * head_dim
                    u = lin[:, start : start + head_dim]
                    out[head] = (u * cos + pltpu.roll(u, head_dim // 2, 1) * sin).astype(bf16)
                start = 2 * group + head * head_dim
                v = lin[:, start : start + head_dim].astype(bf16)
                v_ref[head] = v
                vt_ref[head] = v.T

        for k in range(count):
            @pl.when(slot == k)
            def _():
                x_block[...] = xs[k][...]

        run(x_block)

    def piece_spec(k):
        return pl.BlockSpec(
            (block, width),
            lambda slot, i, order_ref: (
                jnp.where(slot == k, i, jnp.where(slot < k, 0, steps - 1)),
                0,
            ),
        )

    def at_rows(slot, i, order_ref):
        return order_ref[slot] * steps + i

    head_spec = pl.BlockSpec((head_local, block, head_dim), lambda *a: (0, at_rows(*a), 0))
    table_spec = pl.BlockSpec((block, head_dim), lambda *a: (at_rows(*a), 0))
    heads = struct((head_local, length, head_dim), bf16)
    return call(
        kernel,
        (count, steps),
        [piece_spec(k) for k in range(count)]
        + [resident((width, cols), (0, 0)), resident((1, width), (0, 0)), table_spec, table_spec],
        [
            head_spec,
            head_spec,
            head_spec,
            pl.BlockSpec((head_local, head_dim, block), lambda *a: (0, 0, at_rows(*a))),
            pl.BlockSpec((width, block), lambda *a: (0, at_rows(*a))),
        ],
        [heads, heads, heads, struct((head_local, head_dim, length), bf16)]
        + [struct((width, length), bf16)],
        2 * length * width * cols,
        4 * length * width + 2 * length * cols + 8 * length * head_dim,
        scratch=[pltpu.VMEM((block, width), bf16)],
        prefetch=1,
    )(order, *pieces, weights, gain_row, cosine, sine)


def retrieve(chosen, keys, values, base, before=None):
    head_local, rows_cache, head_dim = keys.shape
    blocks, slots = chosen.shape[1:]
    per = min(4, blocks)
    total = blocks * slots

    def kernel(c_ref, k_ref, v_ref, *refs):
        if before is not None:
            bk_ref, bv_ref = refs[:2]
        ok_ref, ov_ref, table, mask = refs[-4:]

        @pl.when(pl.program_id(1) == 0)
        def _():
            table[:, :head_dim] = k_ref[0]
            table[:, head_dim:] = v_ref[0]

        for b in range(per):
            row = c_ref[0, 0, b : b + 1, :] - base
            column = jnp.broadcast_to(row, (slots, slots)).T
            lane = lax.broadcasted_iota(jnp.int32, (slots, slots), 1)
            for start in range(0, rows_cache, slots):
                mask[b * slots : (b + 1) * slots, start : start + slots] = jnp.where(
                    column == lane + start, 1.0, 0.0
                ).astype(bf16)
        picked = dot(mask[...], table[...])
        if before is not None:
            picked_keys = picked[:, :head_dim] + bk_ref[0].astype(f32)
            picked_values = picked[:, head_dim:] + bv_ref[0].astype(f32)
        else:
            picked_keys, picked_values = picked[:, :head_dim], picked[:, head_dim:]
        ok_ref[0] = picked_keys.astype(bf16)
        ov_ref[0] = picked_values.astype(bf16)

    out_spec = pl.BlockSpec((1, per * slots, head_dim), lambda h, i: (h, i, 0))
    table_spec = pl.BlockSpec((1, rows_cache, head_dim), lambda h, i: (h, 0, 0))
    extra = () if before is None else before
    out = struct((head_local, total, head_dim), bf16)
    return call(
        kernel,
        (head_local, blocks // per),
        [pl.BlockSpec((1, 1, per, slots), lambda h, i: (h, i, 0, 0)), table_spec, table_spec]
        + [out_spec] * len(extra),
        [out_spec, out_spec],
        [out, out],
        4 * head_local * total * rows_cache * head_dim,
        8 * head_local * total * head_dim,
        scratch=[
            pltpu.VMEM((rows_cache, 2 * head_dim), bf16),
            pltpu.VMEM((per * slots, rows_cache), bf16),
        ],
    )(chosen.reshape(head_local, blocks // per, per, slots), keys, values, *extra)


def attend(order, query, key, value_t, memory_keys, memory_values, mem_block, mem_count, count):
    head_local, length, head_dim = query.shape
    block = length // count
    half = block // 2
    groups = block // mem_block
    factor = head_dim ** (-0.5) * log2e

    def kernel(order_ref, q_ref, k_ref, vt_ref, mk_ref, mv_ref, *refs):
        o_refs, lse_ref = refs[:count], refs[count]
        index = pl.program_id(0)

        def memory(head):
            parts = []
            for g in range(groups):
                q = q_ref[head, g * mem_block : (g + 1) * mem_block, :]
                parts.append(dot_nt(mk_ref[head, g * mem_count : (g + 1) * mem_count, :], q))
            scores = jnp.concatenate(parts, axis=1) * factor
            top = jnp.max(scores, axis=0, keepdims=True)
            weight = jnp.exp2(scores - top)
            total = jnp.sum(weight, axis=0, keepdims=True)
            weight = weight.astype(bf16)
            values_t = mv_ref[head].T
            mixed = jnp.concatenate(
                [
                    dot(
                        values_t[:, g * mem_count : (g + 1) * mem_count],
                        weight[:, g * mem_block : (g + 1) * mem_block],
                    )
                    for g in range(groups)
                ],
                axis=1,
            )
            return top, total, mixed

        def step(head, carry, start, size, queries, offset):
            top, total, mixed = carry
            keys = k_ref[head, pl.ds(start, size), :]
            scores = dot_nt(keys, q_ref[head, queries, :]) * factor
            if offset is not None:
                row = lax.broadcasted_iota(jnp.int32, scores.shape, 0) + offset
                col = lax.broadcasted_iota(jnp.int32, scores.shape, 1) + (queries.start or 0)
                scores = jnp.where(row <= col, scores, -jnp.inf)
            new_top = jnp.maximum(top, jnp.max(scores, axis=0, keepdims=True))
            decay = jnp.exp2(top - new_top)
            weight = jnp.exp2(scores - new_top)
            total = total * decay + jnp.sum(weight, axis=0, keepdims=True)
            mixed = mixed * decay + dot(vt_ref[head, :, pl.ds(start, size)], weight.astype(bf16))
            return new_top, total, mixed

        every, later = slice(0, block), slice(half, block)
        carries = tuple(memory(head) for head in range(head_local))
        carries = lax.fori_loop(
            0,
            index,
            lambda j, c: tuple(
                step(head, c[head], pl.multiple_of(j * block, block), block, every, None)
                for head in range(head_local)
            ),
            carries,
        )
        start = pl.multiple_of(index * block, block)
        for head in range(head_local):
            carry = step(head, carries[head], start, half, every, 0)
            last = tuple(part[:, half:] for part in carry)
            middle = pl.multiple_of(start + half, half)
            last = step(head, last, middle, half, later, half)
            top, total, mixed = (
                jnp.concatenate([part[:, :half], end], axis=1) for part, end in zip(carry, last)
            )
            columns = slice(head * head_dim, (head + 1) * head_dim)
            mixed = (mixed / total).T.astype(bf16)
            for k in range(count):
                @pl.when(index == order_ref[k])
                def _():
                    o_refs[k][:, columns] = mixed
            lse = top + jnp.log2(total)
            lse_ref[0, head : head + 1, :] = lse[:, :half]
            lse_ref[1, head : head + 1, :] = lse[:, half:]

    full = resident((head_local, length, head_dim), (0, 0, 0))
    full_t = resident((head_local, head_dim, length), (0, 0, 0))
    rows = pl.BlockSpec((head_local, block, head_dim), lambda i, order_ref: (0, i, 0))
    mem_rows = pl.BlockSpec(
        (head_local, groups * mem_count, head_dim), lambda i, order_ref: (0, i, 0)
    )
    return call(
        kernel,
        (count,),
        [rows, full, full_t, mem_rows, mem_rows],
        [pl.BlockSpec((block, head_local * head_dim), lambda i, order_ref: (0, 0))] * count
        + [pl.BlockSpec((2, 8, half), lambda i, order_ref: (i, 0, 0))],
        [struct((block, head_local * head_dim), bf16)] * count
        + [struct((2 * count, 8, half), f32)],
        4 * head_local * length * length * head_dim,
        12 * head_local * length * head_dim,
        prefetch=1,
    )(order, query, key, value_t, memory_keys, memory_values)


def attend_back(
    order, query, key, value, memory_keys, memory_values, mem_block, mem_count, grads, attended, lse,
    cosine, sine, first, last, carried=None,
):
    head_local, length, head_dim = query.shape
    count, _, block = lse.shape
    pieces = len(grads)
    piece = length // pieces
    per = piece // block
    groups = block // mem_block
    scale = head_dim ** (-0.5)
    factor = scale * log2e
    opening, closing = first == 0, last == count

    def kernel(order_ref, q_ref, k_ref, v_ref, mk_ref, mv_ref, *refs):
        g_refs, refs = refs[:pieces], refs[pieces:]
        if opening:
            o_refs, refs = refs[:pieces], refs[pieces:]
        else:
            (part_ref, delta), refs = refs[:2], refs[5:]
        (lse_ref, c_ref, s_ref, dq_ref, dk_ref, dv_ref), refs = refs[:6], refs[6:]
        if opening and not closing:
            (rest_ref, delta), refs = refs[:2], refs[2:]
        elif opening:
            delta, refs = refs[0], refs[1:]
        dq_acc, do_ref = refs
        index = pl.program_id(0) + first

        def cols(head):
            return slice(head * head_dim, (head + 1) * head_dim)

        @pl.when(index == first)
        def _():
            for k in range(pieces):
                start = pl.multiple_of(order_ref[k] * piece, piece)
                do_ref[pl.ds(start, piece), :] = g_refs[k][...]
            if not opening:
                dq_acc[:, :, first * block :] = part_ref[...]
            else:
                for k in range(pieces):
                    for p in range(per):
                        rows = slice(p * block, (p + 1) * block)
                        for head in range(head_local):
                            do = g_refs[k][rows, cols(head)].astype(f32)
                            o = o_refs[k][rows, cols(head)].astype(f32)
                            row = jnp.sum((do * o).T, axis=0, keepdims=True)
                            delta[order_ref[k] * per + p, head : head + 1, :] = row

        row_id = lax.broadcasted_iota(jnp.int32, (block, block), 0)
        col_id = lax.broadcasted_iota(jnp.int32, (block, block), 1)
        keys_t = [k_ref[head].T for head in range(head_local)]

        def memory(head):
            start = pl.multiple_of(index * block, block)
            q = q_ref[head, pl.ds(start, block), :]
            do = do_ref[pl.ds(start, block), cols(head)]
            mk_t = mk_ref[head].T
            parts = []
            for g in range(groups):
                lanes = slice(g * mem_block, (g + 1) * mem_block)
                slots = slice(g * mem_count, (g + 1) * mem_count)
                scores = dot_nt(mk_ref[head, slots, :], q[lanes])
                weight = jnp.exp2(scores * factor - lse_ref[index, head : head + 1, lanes])
                dp = dot_nt(mv_ref[head, slots, :], do[lanes])
                ds = (weight * (dp - delta[index, head : head + 1, lanes])).astype(bf16)
                parts.append(dot(mk_t[:, slots], ds))
            return jnp.concatenate(parts, axis=1)

        def step(head, carry, i, masked):
            dk, dv = carry
            start = pl.multiple_of(i * block, block)
            q = q_ref[head, pl.ds(start, block), :]
            do = do_ref[pl.ds(start, block), cols(head)]
            k, v = k_ref[head], v_ref[head]
            weight = jnp.exp2(dot_nt(k, q) * factor - lse_ref[i, head : head + 1, :])
            if masked:
                weight = jnp.where(row_id <= col_id, weight, 0.0)
            dp = dot_nt(v, do)
            ds = (weight * (dp - delta[i, head : head + 1, :])).astype(bf16)
            dv = dv + dot(weight.astype(bf16), do)
            dk = dk + dot(ds, q)
            so_far = dq_acc[head, :, pl.ds(start, block)]
            if opening:
                so_far = jnp.where(index == 0, 0.0, so_far)
            total = so_far + dot(keys_t[head], ds)
            if masked:
                return dk, dv, total
            dq_acc[head, :, pl.ds(start, block)] = total
            return dk, dv

        cos, sin = c_ref[...], s_ref[...]

        def unrotate(grad_rows):
            u = (grad_rows * scale).astype(bf16).astype(f32)
            return (u * cos - pltpu.roll(u, head_dim // 2, 1) * sin).astype(bf16)

        zero = jnp.zeros((block, head_dim), f32)
        carries = []
        for head in range(head_local):
            dk, dv, dq = step(head, (zero, zero), index, True)
            dq_ref[:, cols(head)] = unrotate((dq + memory(head)).T)
            carries.append((dk, dv))
        carries = lax.fori_loop(
            index + 1,
            count,
            lambda i, c: tuple(step(head, c[head], i, False) for head in range(head_local)),
            tuple(carries),
        )
        for head, (dk, dv) in enumerate(carries):
            dk_ref[:, cols(head)] = unrotate(dk)
            dv_ref[:, cols(head)] = dv.astype(bf16)
        if opening and not closing:
            @pl.when(index == last - 1)
            def _():
                rest_ref[...] = dq_acc[:, :, last * block :]

    group = head_local * head_dim
    full = resident((head_local, length, head_dim), (0, 0, 0))
    flat = resident((piece, group), (0, 0))
    rows = pl.BlockSpec((head_local, block, head_dim), lambda i, o: (0, i + first, 0))
    mem_rows = pl.BlockSpec(
        (head_local, groups * mem_count, head_dim), lambda i, o: (0, i + first, 0)
    )
    table = pl.BlockSpec((block, head_dim), lambda i, o: (i + first, 0))
    out_rows = pl.BlockSpec((block, group), lambda i, o: (i + first, 0))
    out = struct((length, group), bf16)
    aliases = {}
    small = resident(lse.shape, (0, 0, 0))
    in_specs = [full, rows, rows, mem_rows, mem_rows] + [flat] * pieces
    inputs = [query, key, value, memory_keys, memory_values, *grads]
    out_specs, out_shape, scratch = [out_rows] * 3, [out] * 3, []
    if opening:
        in_specs += [flat] * pieces
        inputs += list(attended)
        if closing:
            scratch.append(pltpu.VMEM(lse.shape, f32))
        else:
            rest = (head_local, head_dim, length - last * block)
            out_specs += [pl.BlockSpec(rest, lambda i, o: (0, 0, 0)), pl.BlockSpec(lse.shape, lambda i, o: (0, 0, 0))]
            out_shape += [struct(rest, f32), struct(lse.shape, f32)]
    else:
        in_specs += [resident(carried[0].shape, (0, 0, 0)), small]
        in_specs += [pl.BlockSpec(memory_space=pl.ANY)] * 3
        aliases = {1 + len(inputs) + 2 + k: k for k in range(3)}
        inputs += list(carried)
    done = sum(count - j for j in range(first, last)) / (count * (count + 1) / 2)
    return call(
        kernel,
        (last - first,),
        in_specs + [small, table, table],
        out_specs,
        out_shape,
        done * 10 * head_local * length * length * head_dim // 2,
        24 * head_local * length * head_dim,
        scratch=scratch
        + [pltpu.VMEM((head_local, head_dim, length), f32), pltpu.VMEM((length, group), bf16)],
        prefetch=1,
        aliases=aliases,
    )(order, *inputs, lse, cosine, sine)


def mix(order, attended, weights, first, tokens, gain_row, places):
    count = len(attended)
    rows, group = attended[0].shape
    width = tokens.shape[1]
    block = min(256, rows)
    parts = width // 256

    def kernel(order_ref, *refs):
        a_refs = refs[:count]
        w_refs, refs = refs[count : count + parts], refs[count + parts :]
        x_ref, g_ref, res_ref, n_ref, nt_ref, at_ref = refs
        residual = x_ref[...].astype(f32)
        mixed = [None] * parts
        for k in range(count):
            start = pl.multiple_of(order_ref[k] * group, group)
            for c in range(parts):
                part = dot(a_refs[k][...], w_refs[c][pl.ds(start, group), :])
                mixed[c] = part if mixed[c] is None else mixed[c] + part
            at_ref[pl.ds(start, group), :] = a_refs[k][...].T
        residual = residual + jnp.concatenate(mixed, axis=1)
        scale = lax.rsqrt(jnp.mean(residual * residual, axis=-1, keepdims=True) + epsilon)
        normed = (residual * scale * g_ref[...]).astype(bf16)
        res_ref[...] = residual
        n_ref[...] = normed
        normed_t = normed.T
        size = width // len(places)
        for source, place in enumerate(places):
            nt_ref[place * size : (place + 1) * size, :] = normed_t[source * size : (source + 1) * size]

    rows_spec = pl.BlockSpec((block, width), lambda i, o: (i, 0))
    cols_spec = pl.BlockSpec((width, block), lambda i, o: (0, i))
    return call(
        kernel,
        (rows // block,),
        [pl.BlockSpec((block, group), lambda i, o: (i, 0))] * count
        + column_blocks(width, first, parts)
        + [rows_spec, resident((1, width), (0, 0))],
        [rows_spec, rows_spec, cols_spec, cols_spec],
        [struct((rows, width), f32), struct((rows, width), bf16)]
        + [struct((width, rows), bf16)] * 2,
        2 * rows * width * width,
        16 * rows * width,
        prefetch=1,
    )(order, *attended, *[weights] * parts, tokens, gain_row)


def gated(normed, cotangent, weights, first, hidden_cols):
    rows, width = normed.shape
    block = 256

    def kernel(n_ref, c_ref, wg_ref, wu_ref, wd_ref, h_ref, gg_ref, gu_ref):
        normed_block = n_ref[...]
        gate = dot(normed_block, wg_ref[...])
        up = dot(normed_block, wu_ref[...])
        grad = dot(c_ref[...], wd_ref[...])
        sg = 1.0 / (1.0 + jnp.exp(-gate))
        silu = gate * sg
        h_ref[...] = (silu * up).astype(bf16)
        gg_ref[...] = (grad * up * sg * (1.0 + gate * (1.0 - sg))).astype(bf16)
        gu_ref[...] = (grad * silu).astype(bf16)

    def weight_spec(k):
        offset = (first + k * hidden_cols) // block
        return pl.BlockSpec((width, block), lambda i: (0, i + offset))

    flat = resident((rows, width), (0, 0))
    out_spec = pl.BlockSpec((rows, block), lambda i: (0, i))
    return call(
        kernel,
        (hidden_cols // block,),
        [flat, flat] + [weight_spec(k) for k in range(3)],
        [out_spec] * 3,
        [struct((rows, hidden_cols), bf16)] * 3,
        6 * rows * width * hidden_cols,
        6 * (rows + width) * hidden_cols,
    )(normed, cotangent, weights, weights, weights)


def norm_back(order, grads, weights, first, residual, cotangent, gain_row):
    rows, width = residual.shape
    count = order.shape[0]
    block = min(256, rows)
    steps = width // block
    row_steps = rows // block
    group = width // count
    parts = width // 256
    n_grads = len(grads)

    def kernel(order_ref, *refs):
        g_refs, w_refs = refs[:n_grads], refs[n_grads : 2 * n_grads]
        wo_refs, refs = refs[2 * n_grads : 2 * n_grads + parts], refs[2 * n_grads + parts :]
        r_ref, c_ref, gain_ref, gres_ref, gb_ref = refs[:5]
        gm_refs, acc = refs[5 : 5 + count], refs[5 + count]
        step = pl.program_id(0)

        @pl.when(step < steps)
        def _():
            total = dot_nt(g_refs[0][...], w_refs[0][...])
            for k in range(1, n_grads):
                total = total + dot_nt(g_refs[k][...], w_refs[k][...])
            acc[:, pl.ds(pl.multiple_of(step * block, block), block)] = total

        @pl.when(step >= steps)
        def _():
            start = pl.multiple_of((step - steps) * block, block)
            grad = acc[pl.ds(start, block), :]
            res = r_ref[...]
            scale = lax.rsqrt(jnp.mean(res * res, axis=-1, keepdims=True) + epsilon)
            unit = res * scale
            scaled = grad * gain_ref[...]
            inner = jnp.mean(scaled * unit, axis=-1, keepdims=True)
            gres = c_ref[...].astype(f32) + scale * (scaled - unit * inner)
            gres_ref[...] = gres
            branch = gres.astype(bf16)
            gb_ref[...] = branch
            for k in range(count):
                start_k = pl.multiple_of(order_ref[k] * group, group)
                mixed = None
                for c in range(parts):
                    part = dot_nt(
                        branch[:, c * 256 : (c + 1) * 256], wo_refs[c][pl.ds(start_k, group), :]
                    )
                    mixed = part if mixed is None else mixed + part
                gm_refs[k][...] = mixed.astype(bf16)

    def row(i):
        return jnp.maximum(i - steps, 0)

    rows_spec = pl.BlockSpec((block, width), lambda i, o: (row(i), 0))
    weight_specs = [
        pl.BlockSpec(
            (block, grads[k].shape[1]),
            functools.partial(lambda c, i, o: (jnp.minimum(i, steps - 1), c), k),
        )
        for k in range(n_grads)
    ]
    hidden_cols = sum(g.shape[1] for g in grads)
    return call(
        kernel,
        (steps + row_steps,),
        [resident(g.shape, (0, 0)) for g in grads]
        + weight_specs
        + column_blocks(width, first, parts)
        + [rows_spec, rows_spec, resident((1, width), (0, 0))],
        [
            rows_spec,
            rows_spec,
        ]
        + [pl.BlockSpec((block, group), lambda i, o: (row(i), 0))] * count,
        [
            struct((rows, width), f32),
            struct((rows, width), bf16),
        ]
        + [struct((rows, group), bf16)] * count,
        2 * rows * width * hidden_cols + 2 * rows * width * width,
        2 * (rows + width) * hidden_cols + 16 * rows * width,
        scratch=[pltpu.VMEM((rows, width), f32)],
        prefetch=1,
    )(order, *grads, *[weights] * (n_grads + parts), residual, cotangent, gain_row)


def products(select, lefts, rights, parts, added=None, joined=False, halves=None):
    height = lefts[0].shape[0]
    block = min(256, height) if halves is None else height // 4
    n = len(rights)
    sizes = [r.shape[1] // p for r, p in zip(rights, parts)]
    added = added or []
    distinct = []
    for left in lefts:
        if not any(left is d for d in distinct):
            distinct.append(left)
    which = [next(i for i, d in enumerate(distinct) if d is left) for left in lefts]
    n_left, n_add = len(distinct), len(added)

    def kernel(select_ref, *refs):
        l_refs, r_refs, outs = refs[:n_left], refs[n_left : n_left + n], refs[n_left + n + n_add :]
        def product(k):
            total = dot(l_refs[which[k]][...], r_refs[k][...])
            if k < n_add:
                total = total + refs[n_left + n + k][...].astype(f32)
            return total.astype(bf16)

        for k in range(n):
            if halves is not None:
                step, mine = pl.program_id(0), select_ref[1 + k]
                keep = (step // 2 if halves[k] == 0 else step % 2) == mine
                for cond, out in ((keep, outs[k]), (jnp.logical_not(keep), outs[n + k])):
                    @pl.when(cond)
                    def _():
                        out[...] = product(k)
            elif joined:
                start = sum(sizes[:k])
                outs[0][:, start : start + sizes[k]] = product(k)
            else:
                outs[k][...] = product(k)

    def right_spec(k):
        return pl.BlockSpec(
            (rights[k].shape[0], sizes[k]),
            lambda i, s: (0, s[0] if parts[k] > 1 else 0),
            pipeline_mode=pl.Buffered(1),
        )

    out_sizes = [sum(sizes)] if joined else sizes
    out_specs = [pl.BlockSpec((block, size), lambda i, s: (i, 0)) for size in out_sizes]
    add_specs = out_specs[:n_add]
    out_shape = [struct((height, size), bf16) for size in out_sizes]
    if halves is not None:

        def half_spec(k, kept):
            def index(i, s):
                value = s[1 + k] if kept else 1 - s[1 + k]
                return (jnp.clip(i - 2 * value, 0, 1) if halves[k] == 0 else i // 2, 0)

            return pl.BlockSpec((block, sizes[k]), index)

        out_specs = [half_spec(k, kept) for kept in (True, False) for k in range(n)]
        out_shape = [struct((height // 2, size), bf16) for size in sizes] * 2
    return call(
        kernel,
        (height // block,),
        [pl.BlockSpec((block, d.shape[1]), lambda i, s: (i, 0)) for d in distinct]
        + [right_spec(k) for k in range(n)]
        + add_specs,
        out_specs,
        out_shape,
        sum(2 * height * r.shape[0] * size for r, size in zip(rights, sizes)),
        2 * height * sum(sizes) + sum(2 * r.shape[0] * size for r, size in zip(rights, sizes)),
        prefetch=1,
    )(select, *distinct, *rights, *added)


def finish(residual, hidden, weights, first):
    rows, width = residual.shape
    block = min(256, rows)
    hidden_cols = hidden.shape[1]

    def kernel(r_ref, h_ref, w_ref, out_ref):
        out_ref[...] = (r_ref[...] + dot_nt(h_ref[...], w_ref[...])).astype(bf16)

    rows_spec = pl.BlockSpec((block, width), lambda i: (i, 0))
    return call(
        kernel,
        (rows // block,),
        [
            rows_spec,
            pl.BlockSpec((block, hidden_cols), lambda i: (i, 0)),
            resident((width, hidden_cols), (0, first)),
        ],
        rows_spec,
        struct((rows, width), bf16),
        2 * rows * width * hidden_cols,
        6 * rows * width + 2 * (rows + width) * hidden_cols,
    )(residual, hidden, weights)


def project_back(order, slot, grads, weights, added=(), part=(0, 1), last=None, into=None):
    length, group = grads[0].shape
    width = weights.shape[0]
    piece = length // order.shape[0]
    rows = piece // part[1]
    block = min(512 if last is None else 256, rows)
    steps = rows // block
    before = part[0] * steps
    n = len(added)

    def kernel(order_ref, a_ref, b_ref, c_ref, w_ref, *refs):
        total = dot_nt(a_ref[...], w_ref[:, :group])
        total = total + dot_nt(b_ref[...], w_ref[:, group : 2 * group])
        total = total + dot_nt(c_ref[...], w_ref[:, 2 * group :])
        for ref in refs[:n]:
            total = total + ref[...].astype(f32)
        if last is not None:
            x_ref, gain_ref, g_ref = refs[n : n + 3]
            x = x_ref[...].astype(f32)
            scale = lax.rsqrt(jnp.mean(x * x, axis=-1, keepdims=True) + epsilon)
            unit = x * scale
            scaled = total * gain_ref[...]
            inner = jnp.mean(scaled * unit, axis=-1, keepdims=True)
            total = g_ref[...] + scale * (scaled - unit * inner)
        refs[-1][...] = total.astype(bf16)

    def rows_of(array):
        first = before if array.shape[0] == piece else 0
        return pl.BlockSpec((block, width), lambda i, order_ref: (i + first, 0))

    def grad_rows(i, order_ref):
        return (order_ref[slot] * (piece // block) + before + i, 0)

    inputs = [*grads, weights, *added]
    in_specs = [pl.BlockSpec((block, group), grad_rows)] * 3 + [resident(weights.shape, (0, 0))]
    in_specs += [rows_of(a) for a in added]
    aliases = {}
    out = struct((rows, width), bf16)
    if last is not None:
        out = struct((piece, width), bf16)
        inputs += last
        in_specs += [rows_of(last[0]), resident((1, width), (0, 0)), rows_of(last[2])]
        if into is not None:
            aliases = {1 + len(inputs): 0}
            inputs.append(into)
            in_specs.append(pl.BlockSpec(memory_space=pl.ANY))
    return call(
        kernel,
        (steps,),
        in_specs,
        rows_of(out),
        out,
        6 * rows * width * group,
        2 * rows * (2 * width + 3 * group),
        prefetch=1,
        aliases=aliases,
    )(order, *inputs)


def pair_add(a, b):
    return (a.astype(f32) + b.astype(f32)).astype(bf16)


def axis_bits(axis, first=1):
    bits = []
    while first < lax.axis_size(axis):
        bits.append(first)
        first *= 2
    return bits


def trade(array, dim, axis, bit):
    count = lax.axis_size(axis)
    mine = (lax.axis_index(axis) // bit) % 2
    keep = lax.dynamic_index_in_dim(array, mine, axis=dim, keepdims=False)
    give = lax.dynamic_index_in_dim(array, 1 - mine, axis=dim, keepdims=False)
    return keep, lax.ppermute(give, axis, [(i, i ^ bit) for i in range(count)])


def scatter_start(array, turn, halve_at):
    count = lax.axis_size("fsdp")
    bits = axis_bits("fsdp")
    bits = bits[turn % len(bits) :] + bits[: turn % len(bits)]
    left = axis_bits("fsdp")[::-1]
    array = array.reshape((2,) * len(bits) + (array.shape[0] // count, array.shape[1]))
    todo = [("fsdp", bit) for bit in bits]
    if halve_at is not None:
        todo[halve_at:halve_at] = [("seq", bit) for bit in axis_bits("seq", 2)]
    return exchange((array, None, todo, left))


def scatter_from(keep, give, axis, bit, left, todo, rows):
    count = lax.axis_size(axis)
    got = lax.ppermute(give, axis, [(i, i ^ bit) for i in range(count)])
    shape = (2,) * len(left) + (rows, keep.shape[1])
    return keep.reshape(shape), got.reshape(shape), todo, left


def exchange(state):
    array, _, todo, left = state
    if not todo:
        return state
    axis, bit = todo[0]
    if axis == "fsdp":
        pair = trade(array, left.index(bit), axis, bit)
        left = [b for b in left if b != bit]
    else:
        rows, n = array.shape[-2:]
        array = array.reshape(array.shape[:-2] + (2, rows // 2, n))
        pair = trade(array, array.ndim - 3, axis, bit)
    return (*pair, todo[1:], left)


def settle(states, done, ahead):
    keeps, done = lax.optimization_barrier(([state[0] for state in states], done))
    arrays = [
        keep if state[1] is None else pair_add(keep, state[1])
        for keep, state in zip(keeps, states)
    ]
    arrays, ahead = lax.optimization_barrier((arrays, ahead))
    return [(a, None) + state[2:] for a, state in zip(arrays, states)], done, ahead


def rows_whole(array, other):
    first = (lax.axis_index("seq") // 2) % 2 == 0
    return both_ways(array, other, first).reshape(-1, array.shape[1])


def last_rows(state):
    return state[0].reshape(state[0].shape[-2:])


def both_ways(own, other, first):
    return jnp.stack([jnp.where(first, own, other), jnp.where(first, other, own)])


def feedforward_ends(half, joined, other, gate_weight, up_weight, gain):
    rows, hidden_cols = gate_weight.shape
    width = joined.shape[1] - 3 * (hidden_cols // 2)
    size = hidden_cols // 2

    def kernel(half_ref, j_ref, o_ref, wg_ref, wu_ref, gain_ref, g_ref, u_ref, d_ref, out_ref, gg_ref):
        def both(k):
            columns = slice(k * size, (k + 1) * size)
            own, far = j_ref[:, columns].astype(f32), o_ref[:, columns].astype(f32)
            lower = half_ref[0] == 0
            return jnp.concatenate(
                [jnp.where(lower, own, far), jnp.where(lower, far, own)], axis=1
            )

        down, gate, up = both(0), both(1), both(2)
        g_ref[...] = gate
        u_ref[...] = up
        d_ref[...] = down.T
        out_ref[...] = j_ref[:, 3 * size :].astype(f32) + o_ref[:, 3 * size :].astype(f32)
        total = jnp.sum(
            wg_ref[...].astype(f32) * gate + wu_ref[...].astype(f32) * up, axis=1, keepdims=True
        )
        gg_ref[...] = total / gain_ref[...]

    whole = lambda shape: pl.BlockSpec(shape, lambda i, h: (0, 0))
    shapes = [(rows, hidden_cols)] * 2 + [(hidden_cols, rows), (rows, width), (rows, 1)]
    *ends, gain_grad = call(
        kernel,
        (1,),
        [whole(joined.shape)] * 2 + [whole(gate_weight.shape)] * 2 + [whole((rows, 1))],
        [whole(shape) for shape in shapes],
        [struct(shape, f32) for shape in shapes],
        4 * rows * hidden_cols,
        20 * rows * hidden_cols,
        prefetch=1,
    )(half, joined, other, gate_weight, up_weight, gain.astype(f32)[:, None])
    return *ends, gain_grad[:, 0]


def projection_ends(order, pieces, weights, gain):
    rows, width = weights[0].shape
    count = len(pieces)
    group = width // count

    def kernel(order_ref, *refs):
        p_refs, refs = refs[:count], refs[count:]
        w_refs, gain_ref, outs, gg_ref = refs[:3], refs[3], refs[4:7], refs[7]
        for k in range(count):
            start = pl.multiple_of(order_ref[k] * group, group)
            for j in range(3):
                outs[j][:, pl.ds(start, group)] = p_refs[k][
                    :, j * group : (j + 1) * group
                ].astype(f32)
        total = None
        for j in range(3):
            part = jnp.sum(w_refs[j][...].astype(f32) * outs[j][...], axis=1, keepdims=True)
            total = part if total is None else total + part
        gg_ref[...] = total / gain_ref[...]

    whole = lambda shape: pl.BlockSpec(shape, lambda i, o: (0, 0))
    shapes = [(rows, width)] * 3 + [(rows, 1)]
    *ends, gain_grad = call(
        kernel,
        (1,),
        [whole(pieces[0].shape)] * count + [whole((rows, width))] * 3 + [whole((rows, 1))],
        [whole(shape) for shape in shapes],
        [struct(shape, f32) for shape in shapes],
        6 * rows * width,
        24 * rows * width,
        prefetch=1,
    )(order, *pieces, *weights, gain.astype(f32)[:, None])
    return *ends, gain_grad[:, 0]


def body(
    tokens, cotangent, query_weight, key_weight, value_weight, output_weight, gate_weight, up_weight,
    down_weight, attention_gain, feedforward_gain, cache_keys, cache_values, memory_rows, memory_docs,
):
    seq_count, fsdp_count = lax.axis_size("seq"), lax.axis_size("fsdp")
    here = lax.axis_index("seq")
    tok_rows, width = tokens.shape
    head_local, rows_cache, head_dim = cache_keys.shape[1:]
    group = head_local * head_dim
    length = tok_rows * seq_count
    mem_block = length // memory_rows.shape[2]
    mem_count = memory_rows.shape[3]
    shard = query_weight.shape[0]
    hidden_cols = gate_weight.shape[1]
    order = here ^ jnp.arange(seq_count, dtype=jnp.int32)

    gains = spread(jnp.stack([attention_gain, feedforward_gain]), "fsdp")
    gains = gains.transpose(1, 0, 2).reshape(2, width).astype(f32)
    gain_one, gain_two = gains[0:1], gains[1:2]
    own_cols = [
        lax.dynamic_slice_in_dim(w, here * group, group, axis=1)
        for w in (query_weight, key_weight, value_weight)
    ]
    qkv = spread(jnp.concatenate(own_cols, axis=1), "fsdp").reshape(width, 3 * group)

    pieces = [tokens, swap_seq(tokens, 1), swap_seq(tokens, 2)]
    pieces.append(swap_seq(pieces[2], 1))

    ring = [(i, (i + 1) % fsdp_count) for i in range(fsdp_count)]
    partner_keys = lax.ppermute(cache_keys[0], "fsdp", ring)
    partner_values = lax.ppermute(cache_values[0], "fsdp", ring)

    part = shard // seq_count

    def own_rows(w):
        return lax.dynamic_slice_in_dim(w, here * part, part, axis=0)

    own_wd = lax.dynamic_slice_in_dim(down_weight, here * part, part, axis=1).T
    own_part = jnp.concatenate(
        [own_rows(gate_weight), own_rows(up_weight), own_wd, own_rows(output_weight)], axis=1
    )
    big = lax.all_gather(own_part, ("fsdp", "seq"), axis=0, tiled=True)

    half = head_dim // 2
    frequency = 10000.0 ** (-2.0 * jnp.arange(half, dtype=f32) / head_dim)
    near_count = 64
    near_angles = jnp.arange(near_count, dtype=f32)[:, None] * frequency[None, :]
    far_angles = jnp.arange(0, length, near_count).astype(f32)[:, None] * frequency[None, :]
    near_angles, far_angles = near_angles[None], far_angles[:, None]
    near_cos, near_sin, far_cos, far_sin = lax.optimization_barrier(
        (jnp.cos(near_angles), jnp.sin(near_angles), jnp.cos(far_angles), jnp.sin(far_angles))
    )
    cos_half = (far_cos * near_cos - far_sin * near_sin).reshape(length, half)
    sin_half = (far_sin * near_cos + far_cos * near_sin).reshape(length, half)
    cosine = jnp.concatenate([cos_half, cos_half], axis=1)
    sine = jnp.concatenate([-sin_half, sin_half], axis=1)
    cotangent_t = cotangent.T.reshape(fsdp_count, 2, shard // 2, tok_rows)
    cotangent_t = cotangent_t.swapaxes(0, 1).reshape(width, tok_rows)
    places = [
        (f % 4 // 2 + f % 2 * 2) * (fsdp_count // 4) + f // 4 for f in range(fsdp_count)
    ]

    chosen = memory_docs[0] * rows_cache + memory_rows[0]
    picked = retrieve(chosen, cache_keys[0], cache_values[0], 0)
    query, key, value, value_t, normed_one_t = project(
        order, pieces, qkv, gain_one, cosine, sine, head_local, head_dim
    )
    picked_keys, picked_values = retrieve(chosen, partner_keys, partner_values, rows_cache, picked)
    *attended_heads, lse = attend(
        order, query, key, value_t, picked_keys, picked_values, mem_block, mem_count, seq_count
    )

    def by_distance(stack):
        return [stack[0]] + [swap_seq(stack[k], k) for k in range(1, seq_count)]

    attended = by_distance(attended_heads)
    residual, normed_two, normed_two_t, attended_t = mix(
        order, attended, big, 3 * hidden_cols, tokens, gain_two, places
    )
    hid, gg, gu = gated(normed_two, cotangent, big, 0, hidden_cols)
    own_half, other_half = (here % 2)[None].astype(jnp.int32), (1 - here % 2)[None].astype(jnp.int32)
    lefts, rights = [cotangent_t, normed_two_t, normed_two_t], [hid, gg, gu]
    given = products(other_half, lefts, rights, (2, 2, 2))
    given, gg_later = lax.optimization_barrier((given, gg))
    got = [swap_seq(g, 1) for g in given]
    grad_residual, grad_branch, *grad_mixed = norm_back(
        order, [gg_later, gu], big, 3 * hidden_cols, residual, cotangent, gain_two
    )
    grad_heads = by_distance(grad_mixed)
    bits, upper = axis_bits("fsdp"), axis_bits("seq", 2)
    firsts = (("seq", upper[0]), ("fsdp", bits[0]), ("fsdp", bits[1]), ("fsdp", bits[-1]))
    mine = [(lax.axis_index(axis) // bit) % 2 for axis, bit in firsts]
    select = jnp.stack([here % 2, *mine]).astype(jnp.int32)
    own = products(
        select, [*lefts, attended_t], [*rights, grad_branch], (2, 2, 2, 1), got, halves=(0, 0, 1, 0)
    )
    grad_heads, own = lax.optimization_barrier((grad_heads, own))
    down = bits[::-1]
    over = lambda *picks: [("fsdp", b) if b else ("seq", upper[0]) for b in picks]
    sums = [
        scatter_from(keep, give, axis, bit, left, todo, rows)
        for keep, give, (axis, bit), left, todo, rows in zip(
            own[:4],
            own[4:],
            firsts,
            (down, [bits[1], *down[: -2]], [bits[0], *down[: -2]], down[1:]),
            (
                over(*bits),
                over(0, *bits[1:]),
                over(0, *bits[2:], bits[0]),
                over(bits[0], 0, *bits[1:-1]),
            ),
            (shard // 2, shard, shard, shard),
        )
    ]

    blocks = lse.shape[0]
    middle = 3 * blocks // 8
    attention = (order, query, key, value, picked_keys, picked_values, mem_block, mem_count)
    *grads, rest, delta = attend_back(
        *attention, grad_heads, attended_heads, lse, cosine, sine, 0, middle
    )
    sums, _, (rest, delta) = settle(sums, (), (rest, delta))
    sums = [exchange(g) for g in sums]
    grads = attend_back(
        *attention, grad_heads, None, lse, cosine, sine, middle, blocks, (rest, delta, *grads)
    )

    zero = jnp.zeros((1,), jnp.int32)
    sums, _, grads = settle(sums, (), grads)
    sums = [exchange(g) for g in sums]
    far_part = project_back(order, 3, grads, qkv)
    far = swap_seq(far_part, 1)
    far_part, grads = lax.optimization_barrier((far_part, grads))
    near_part = project_back(order, 1, grads, qkv)
    near = swap_seq(near_part, 1)
    far, near_part, grads = lax.optimization_barrier((far, near_part, grads))
    half = project_back(order, 2, grads, qkv, [far], (0, 2))
    across = [swap_seq(half, 2)]
    half, grads = lax.optimization_barrier((half, grads))
    half = project_back(order, 2, grads, qkv, [far], (1, 2))
    across.append(swap_seq(half, 2))
    half, grads = lax.optimization_barrier((half, grads))
    (qkv_grad,) = products(zero, [normed_one_t] * 3, list(grads), (1, 1, 1), joined=True)
    qkv_state = scatter_start(qkv_grad, 0, None)
    across[0], qkv_grad, grads = lax.optimization_barrier((across[0], qkv_grad, grads))
    sums, across[0], near = settle(sums, across[0], near)
    sums = [exchange(g) for g in sums]
    (qkv_state, *sums), _, near = settle([qkv_state, *sums], (), near)
    while any(state[2] for state in sums):
        sums = settle([exchange(g) for g in sums], (), ())[0]
    qkv_state = exchange(qkv_state)
    joined = jnp.concatenate([last_rows(state) for state in sums], axis=1)
    lower = swap_seq(joined, upper[0])
    last = (tokens, gain_one, grad_residual)
    grad_tokens = project_back(order, 0, grads, qkv, [near, across[0]], (0, 2), last)
    (qkv_state,), grad_tokens, (hid, across[1]) = settle(
        [qkv_state], grad_tokens, (hid, across[1])
    )
    qkv_state = exchange(qkv_state)
    result = finish(residual, hid, big, 2)
    grad_tokens = project_back(
        order, 0, grads, qkv, [near, across[1]], (1, 2), last, grad_tokens
    )
    joined, grad_tokens = lax.optimization_barrier((joined, grad_tokens))
    joined = rows_whole(joined, lower)
    other = swap_seq(joined, 1)
    (qkv_state,), _, _ = settle([qkv_state], (result, grad_tokens), ())
    while qkv_state[2]:
        qkv_state = settle([exchange(qkv_state)], (), ())[0][0]
    qkv_pieces = by_distance([last_rows(qkv_state)] * seq_count)
    grad_gate, grad_up, grad_down, grad_out, grad_gain_two = feedforward_ends(
        own_half, joined, other, gate_weight, up_weight, feedforward_gain
    )
    qkv_pieces[0], grad_out = lax.optimization_barrier((qkv_pieces[0], grad_out))
    grad_q, grad_k, grad_v, grad_gain_one = projection_ends(
        order, qkv_pieces, (query_weight, key_weight, value_weight), attention_gain
    )
    return (
        result,
        grad_tokens,
        grad_q,
        grad_k,
        grad_v,
        grad_out,
        grad_gate,
        grad_up,
        grad_down,
        grad_gain_one,
        grad_gain_two,
    )


def solution(mesh):
    tok, row, col, one = P(("fsdp", "seq"), None), P("fsdp", None), P(None, "fsdp"), P("fsdp")
    cache = P("fsdp", "seq", None, None)
    return jax.shard_map(
        body,
        mesh=mesh,
        in_specs=(tok, tok) + (row,) * 6 + (col, one, one) + (cache,) * 4,
        out_specs=(tok, tok) + (row,) * 6 + (col, one, one),
        check_vma=False,
    )
```

```python
import functools

import jax
import jax.numpy as jnp
from jax import lax
from jax.experimental import pallas as pl
from jax.experimental.pallas import tpu as pltpu
from jax.sharding import PartitionSpec as P

epsilon = 1e-06
log2e = 1.4426950408889634
f32 = jnp.float32
bf16 = jnp.bfloat16
VMEM_LIMIT = 60 * 1024 * 1024
hint = 0.15


def dot(a, b):
    return jnp.dot(a, b, preferred_element_type=f32)


def dot_nt(a, b):
    return lax.dot_general(a, b, (((1,), (1,)), ((), ())), preferred_element_type=f32)


def dot_tn(a, b):
    return lax.dot_general(a, b, (((0,), (0,)), ((), ())), preferred_element_type=f32)


def call(
    kernel, grid, in_specs, out_specs, out_shape, flops, bytes_accessed, scratch=(), prefetch=0, aliases=None
):
    return pl.pallas_call(
        kernel,
        name=kernel.__qualname__.split(".")[0],
        grid_spec=pltpu.PrefetchScalarGridSpec(
            num_scalar_prefetch=prefetch,
            grid=grid,
            in_specs=in_specs,
            out_specs=out_specs,
            scratch_shapes=list(scratch),
        ),
        out_shape=out_shape,
        input_output_aliases=aliases or {},
        compiler_params=pltpu.CompilerParams(
            dimension_semantics=("arbitrary",) * len(grid), vmem_limit_bytes=VMEM_LIMIT
        ),
        cost_estimate=pl.CostEstimate(
            flops=int(flops * hint), bytes_accessed=int(bytes_accessed * hint), transcendentals=0
        ),
    )


def resident(shape, index):
    return pl.BlockSpec(shape, lambda *_: index, pipeline_mode=pl.Buffered(1))


def column_blocks(height, first, parts):
    return [resident((height, 256), (0, first // 256 + c)) for c in range(parts)]


def struct(shape, dtype):
    return jax.ShapeDtypeStruct(shape, dtype)


def swap_seq(array, bit):
    count = lax.axis_size("seq")
    return lax.ppermute(array, "seq", [(i, i ^ bit) for i in range(count)])


def spread(array, axis):
    count = lax.axis_size(axis)
    copies = jnp.broadcast_to(array[None], (count,) + array.shape)
    return lax.all_to_all(copies, axis, split_axis=0, concat_axis=0, tiled=True)


def project(order, pieces, weights, gain_row, cosine, sine, head_local, head_dim):
    rows, width = pieces[0].shape
    count = len(pieces)
    block = min(512, rows)
    steps = rows // block
    length = rows * count
    cols = weights.shape[1]
    group = head_local * head_dim

    def kernel(order_ref, *refs):
        xs = refs[:count]
        w_ref, g_ref, c_ref, s_ref, q_ref, k_ref, v_ref, vt_ref, nt_ref, x_block = refs[count:]
        slot = pl.program_id(0)

        def run(x_ref):
            x = x_ref[...].astype(f32)
            scale = lax.rsqrt(jnp.mean(x * x, axis=-1, keepdims=True) + epsilon)
            normed = (x * scale * g_ref[...]).astype(bf16)
            nt_ref[...] = normed.T
            lin = dot(normed, w_ref[...])
            cos, sin = c_ref[...], s_ref[...]
            for head in range(head_local):
                for part, out in ((0, q_ref), (1, k_ref)):
                    start = part * group + head * head_dim
                    u = lin[:, start : start + head_dim]
                    out[head] = (u * cos + pltpu.roll(u, head_dim // 2, 1) * sin).astype(bf16)
                start = 2 * group + head * head_dim
                v = lin[:, start : start + head_dim].astype(bf16)
                v_ref[head] = v
                vt_ref[head] = v.T

        for k in range(count):
            @pl.when(slot == k)
            def _():
                x_block[...] = xs[k][...]

        run(x_block)

    def piece_spec(k):
        return pl.BlockSpec(
            (block, width),
            lambda slot, i, order_ref: (
                jnp.where(slot == k, i, jnp.where(slot < k, 0, steps - 1)),
                0,
            ),
        )

    def at_rows(slot, i, order_ref):
        return order_ref[slot] * steps + i

    head_spec = pl.BlockSpec((head_local, block, head_dim), lambda *a: (0, at_rows(*a), 0))
    table_spec = pl.BlockSpec((block, head_dim), lambda *a: (at_rows(*a), 0))
    heads = struct((head_local, length, head_dim), bf16)
    return call(
        kernel,
        (count, steps),
        [piece_spec(k) for k in range(count)]
        + [resident((width, cols), (0, 0)), resident((1, width), (0, 0)), table_spec, table_spec],
        [
            head_spec,
            head_spec,
            head_spec,
            pl.BlockSpec((head_local, head_dim, block), lambda *a: (0, 0, at_rows(*a))),
            pl.BlockSpec((width, block), lambda *a: (0, at_rows(*a))),
        ],
        [heads, heads, heads, struct((head_local, head_dim, length), bf16)]
        + [struct((width, length), bf16)],
        2 * length * width * cols,
        4 * length * width + 2 * length * cols + 8 * length * head_dim,
        scratch=[pltpu.VMEM((block, width), bf16)],
        prefetch=1,
    )(order, *pieces, weights, gain_row, cosine, sine)


def retrieve(chosen, keys, values, base, before=None):
    head_local, rows_cache, head_dim = keys.shape
    blocks, slots = chosen.shape[1:]
    per = min(4, blocks)
    total = blocks * slots

    def kernel(c_ref, k_ref, v_ref, *refs):
        if before is not None:
            bk_ref, bv_ref = refs[:2]
        ok_ref, ov_ref, table, mask = refs[-4:]

        @pl.when(pl.program_id(1) == 0)
        def _():
            table[:, :head_dim] = k_ref[0]
            table[:, head_dim:] = v_ref[0]

        for b in range(per):
            row = c_ref[0, 0, b : b + 1, :] - base
            column = jnp.broadcast_to(row, (slots, slots)).T
            lane = lax.broadcasted_iota(jnp.int32, (slots, slots), 1)
            for start in range(0, rows_cache, slots):
                mask[b * slots : (b + 1) * slots, start : start + slots] = jnp.where(
                    column == lane + start, 1.0, 0.0
                ).astype(bf16)
        picked = dot(mask[...], table[...])
        if before is not None:
            picked_keys = picked[:, :head_dim] + bk_ref[0].astype(f32)
            picked_values = picked[:, head_dim:] + bv_ref[0].astype(f32)
        else:
            picked_keys, picked_values = picked[:, :head_dim], picked[:, head_dim:]
        ok_ref[0] = picked_keys.astype(bf16)
        ov_ref[0] = picked_values.astype(bf16)

    out_spec = pl.BlockSpec((1, per * slots, head_dim), lambda h, i: (h, i, 0))
    table_spec = pl.BlockSpec((1, rows_cache, head_dim), lambda h, i: (h, 0, 0))
    extra = () if before is None else before
    out = struct((head_local, total, head_dim), bf16)
    return call(
        kernel,
        (head_local, blocks // per),
        [pl.BlockSpec((1, 1, per, slots), lambda h, i: (h, i, 0, 0)), table_spec, table_spec]
        + [out_spec] * len(extra),
        [out_spec, out_spec],
        [out, out],
        4 * head_local * total * rows_cache * head_dim,
        8 * head_local * total * head_dim,
        scratch=[
            pltpu.VMEM((rows_cache, 2 * head_dim), bf16),
            pltpu.VMEM((per * slots, rows_cache), bf16),
        ],
    )(chosen.reshape(head_local, blocks // per, per, slots), keys, values, *extra)


def attend(order, query, key, value_t, memory_keys, memory_values, mem_block, mem_count, count):
    head_local, length, head_dim = query.shape
    block = length // count
    half = block // 2
    groups = block // mem_block
    factor = head_dim ** (-0.5) * log2e

    def kernel(order_ref, q_ref, k_ref, vt_ref, mk_ref, mv_ref, *refs):
        o_refs, lse_ref = refs[:count], refs[count]
        index = pl.program_id(0)

        def memory(head):
            parts = []
            for g in range(groups):
                q = q_ref[head, g * mem_block : (g + 1) * mem_block, :]
                parts.append(dot_nt(mk_ref[head, g * mem_count : (g + 1) * mem_count, :], q))
            scores = jnp.concatenate(parts, axis=1) * factor
            top = jnp.max(scores, axis=0, keepdims=True)
            weight = jnp.exp2(scores - top)
            total = jnp.sum(weight, axis=0, keepdims=True)
            weight = weight.astype(bf16)
            values_t = mv_ref[head].T
            mixed = jnp.concatenate(
                [
                    dot(
                        values_t[:, g * mem_count : (g + 1) * mem_count],
                        weight[:, g * mem_block : (g + 1) * mem_block],
                    )
                    for g in range(groups)
                ],
                axis=1,
            )
            return top, total, mixed

        def step(head, carry, start, size, queries, offset):
            top, total, mixed = carry
            keys = k_ref[head, pl.ds(start, size), :]
            scores = dot_nt(keys, q_ref[head, queries, :]) * factor
            if offset is not None:
                row = lax.broadcasted_iota(jnp.int32, scores.shape, 0) + offset
                col = lax.broadcasted_iota(jnp.int32, scores.shape, 1) + (queries.start or 0)
                scores = jnp.where(row <= col, scores, -jnp.inf)
            new_top = jnp.maximum(top, jnp.max(scores, axis=0, keepdims=True))
            decay = jnp.exp2(top - new_top)
            weight = jnp.exp2(scores - new_top)
            total = total * decay + jnp.sum(weight, axis=0, keepdims=True)
            mixed = mixed * decay + dot(vt_ref[head, :, pl.ds(start, size)], weight.astype(bf16))
            return new_top, total, mixed

        every, later = slice(0, block), slice(half, block)
        carries = tuple(memory(head) for head in range(head_local))
        carries = lax.fori_loop(
            0,
            index,
            lambda j, c: tuple(
                step(head, c[head], pl.multiple_of(j * block, block), block, every, None)
                for head in range(head_local)
            ),
            carries,
        )
        start = pl.multiple_of(index * block, block)
        for head in range(head_local):
            carry = step(head, carries[head], start, half, every, 0)
            last = tuple(part[:, half:] for part in carry)
            middle = pl.multiple_of(start + half, half)
            last = step(head, last, middle, half, later, half)
            top, total, mixed = (
                jnp.concatenate([part[:, :half], end], axis=1) for part, end in zip(carry, last)
            )
            columns = slice(head * head_dim, (head + 1) * head_dim)
            mixed = (mixed / total).T.astype(bf16)
            for k in range(count):
                @pl.when(index == order_ref[k])
                def _():
                    o_refs[k][:, columns] = mixed
            lse = top + jnp.log2(total)
            lse_ref[0, head : head + 1, :] = lse[:, :half]
            lse_ref[1, head : head + 1, :] = lse[:, half:]

    full = resident((head_local, length, head_dim), (0, 0, 0))
    full_t = resident((head_local, head_dim, length), (0, 0, 0))
    rows = pl.BlockSpec((head_local, block, head_dim), lambda i, order_ref: (0, i, 0))
    mem_rows = pl.BlockSpec(
        (head_local, groups * mem_count, head_dim), lambda i, order_ref: (0, i, 0)
    )
    return call(
        kernel,
        (count,),
        [rows, full, full_t, mem_rows, mem_rows],
        [pl.BlockSpec((block, head_local * head_dim), lambda i, order_ref: (0, 0))] * count
        + [pl.BlockSpec((2, 8, half), lambda i, order_ref: (i, 0, 0))],
        [struct((block, head_local * head_dim), bf16)] * count
        + [struct((2 * count, 8, half), f32)],
        4 * head_local * length * length * head_dim,
        12 * head_local * length * head_dim,
        prefetch=1,
    )(order, query, key, value_t, memory_keys, memory_values)


def attend_back(
    order, query, key, value, memory_keys, memory_values, mem_block, mem_count, grads, attended, lse,
    cosine, sine, first, last, carried=None,
):
    head_local, length, head_dim = query.shape
    count, _, block = lse.shape
    pieces = len(grads)
    piece = length // pieces
    per = piece // block
    groups = block // mem_block
    scale = head_dim ** (-0.5)
    factor = scale * log2e
    opening, closing = first == 0, last == count

    def kernel(order_ref, q_ref, k_ref, v_ref, mk_ref, mv_ref, *refs):
        g_refs, refs = refs[:pieces], refs[pieces:]
        if opening:
            o_refs, refs = refs[:pieces], refs[pieces:]
        else:
            (part_ref, delta), refs = refs[:2], refs[5:]
        (lse_ref, c_ref, s_ref, dq_ref, dk_ref, dv_ref), refs = refs[:6], refs[6:]
        if opening and not closing:
            (rest_ref, delta), refs = refs[:2], refs[2:]
        elif opening:
            delta, refs = refs[0], refs[1:]
        dq_acc, do_ref = refs
        index = pl.program_id(0) + first

        def cols(head):
            return slice(head * head_dim, (head + 1) * head_dim)

        @pl.when(index == first)
        def _():
            for k in range(pieces):
                start = pl.multiple_of(order_ref[k] * piece, piece)
                do_ref[pl.ds(start, piece), :] = g_refs[k][...]
            if not opening:
                dq_acc[:, :, first * block :] = part_ref[...]
            else:
                for k in range(pieces):
                    for p in range(per):
                        rows = slice(p * block, (p + 1) * block)
                        for head in range(head_local):
                            do = g_refs[k][rows, cols(head)].astype(f32)
                            o = o_refs[k][rows, cols(head)].astype(f32)
                            row = jnp.sum((do * o).T, axis=0, keepdims=True)
                            delta[order_ref[k] * per + p, head : head + 1, :] = row

        row_id = lax.broadcasted_iota(jnp.int32, (block, block), 0)
        col_id = lax.broadcasted_iota(jnp.int32, (block, block), 1)
        keys_t = [k_ref[head].T for head in range(head_local)]

        def memory(head):
            start = pl.multiple_of(index * block, block)
            q = q_ref[head, pl.ds(start, block), :]
            do = do_ref[pl.ds(start, block), cols(head)]
            scores = dot_nt(mk_ref[head], q)
            weight = jnp.exp2(scores * factor - lse_ref[index, head : head + 1, :])
            slot = lax.broadcasted_iota(jnp.int32, scores.shape, 0) // mem_count
            own = slot == lax.broadcasted_iota(jnp.int32, scores.shape, 1) // mem_block
            dp = dot_nt(mv_ref[head], do)
            ds = jnp.where(own, weight * (dp - delta[index, head : head + 1, :]), 0.0)
            return dot(mk_ref[head].T, ds.astype(bf16))

        def step(head, carry, i, masked):
            dk, dv = carry
            start = pl.multiple_of(i * block, block)
            q = q_ref[head, pl.ds(start, block), :]
            do = do_ref[pl.ds(start, block), cols(head)]
            k, v = k_ref[head], v_ref[head]
            weight = jnp.exp2(dot_nt(k, q) * factor - lse_ref[i, head : head + 1, :])
            if masked:
                weight = jnp.where(row_id <= col_id, weight, 0.0)
            dp = dot_nt(v, do)
            ds = (weight * (dp - delta[i, head : head + 1, :])).astype(bf16)
            dv = dv + dot(weight.astype(bf16), do)
            dk = dk + dot(ds, q)
            so_far = dq_acc[head, :, pl.ds(start, block)]
            if opening:
                so_far = jnp.where(index == 0, 0.0, so_far)
            total = so_far + dot(keys_t[head], ds)
            if masked:
                return dk, dv, total
            dq_acc[head, :, pl.ds(start, block)] = total
            return dk, dv

        cos, sin = c_ref[...], s_ref[...]

        def unrotate(grad_rows):
            u = (grad_rows * scale).astype(bf16).astype(f32)
            return (u * cos - pltpu.roll(u, head_dim // 2, 1) * sin).astype(bf16)

        zero = jnp.zeros((block, head_dim), f32)
        carries = []
        for head in range(head_local):
            dk, dv, dq = step(head, (zero, zero), index, True)
            dq_ref[:, cols(head)] = unrotate((dq + memory(head)).T)
            carries.append((dk, dv))
        carries = lax.fori_loop(
            index + 1,
            count,
            lambda i, c: tuple(step(head, c[head], i, False) for head in range(head_local)),
            tuple(carries),
        )
        for head, (dk, dv) in enumerate(carries):
            dk_ref[:, cols(head)] = unrotate(dk)
            dv_ref[:, cols(head)] = dv.astype(bf16)
        if opening and not closing:
            @pl.when(index == last - 1)
            def _():
                rest_ref[...] = dq_acc[:, :, last * block :]

    group = head_local * head_dim
    full = resident((head_local, length, head_dim), (0, 0, 0))
    flat = resident((piece, group), (0, 0))
    rows = pl.BlockSpec((head_local, block, head_dim), lambda i, o: (0, i + first, 0))
    mem_rows = pl.BlockSpec(
        (head_local, groups * mem_count, head_dim), lambda i, o: (0, i + first, 0)
    )
    table = pl.BlockSpec((block, head_dim), lambda i, o: (i + first, 0))
    out_rows = pl.BlockSpec((block, group), lambda i, o: (i + first, 0))
    out = struct((length, group), bf16)
    aliases = {}
    small = resident(lse.shape, (0, 0, 0))
    in_specs = [full, rows, rows, mem_rows, mem_rows] + [flat] * pieces
    inputs = [query, key, value, memory_keys, memory_values, *grads]
    out_specs, out_shape, scratch = [out_rows] * 3, [out] * 3, []
    if opening:
        in_specs += [flat] * pieces
        inputs += list(attended)
        if closing:
            scratch.append(pltpu.VMEM(lse.shape, f32))
        else:
            rest = (head_local, head_dim, length - last * block)
            out_specs += [pl.BlockSpec(rest, lambda i, o: (0, 0, 0)), pl.BlockSpec(lse.shape, lambda i, o: (0, 0, 0))]
            out_shape += [struct(rest, f32), struct(lse.shape, f32)]
    else:
        in_specs += [resident(carried[0].shape, (0, 0, 0)), small]
        in_specs += [pl.BlockSpec(memory_space=pl.ANY)] * 3
        aliases = {1 + len(inputs) + 2 + k: k for k in range(3)}
        inputs += list(carried)
    done = sum(count - j for j in range(first, last)) / (count * (count + 1) / 2)
    return call(
        kernel,
        (last - first,),
        in_specs + [small, table, table],
        out_specs,
        out_shape,
        done * 10 * head_local * length * length * head_dim // 2,
        24 * head_local * length * head_dim,
        scratch=scratch
        + [pltpu.VMEM((head_local, head_dim, length), f32), pltpu.VMEM((length, group), bf16)],
        prefetch=1,
        aliases=aliases,
    )(order, *inputs, lse, cosine, sine)


def mix(order, attended, weights, first, tokens, gain_row, places):
    count = len(attended)
    rows, group = attended[0].shape
    width = tokens.shape[1]
    block = min(256, rows)
    parts = width // 256

    def kernel(order_ref, *refs):
        a_refs = refs[:count]
        w_refs, refs = refs[count : count + parts], refs[count + parts :]
        x_ref, g_ref, res_ref, n_ref, nt_ref, at_ref = refs
        residual = x_ref[...].astype(f32)
        mixed = [None] * parts
        for k in range(count):
            start = pl.multiple_of(order_ref[k] * group, group)
            for c in range(parts):
                part = dot(a_refs[k][...], w_refs[c][pl.ds(start, group), :])
                mixed[c] = part if mixed[c] is None else mixed[c] + part
            at_ref[pl.ds(start, group), :] = a_refs[k][...].T
        residual = residual + jnp.concatenate(mixed, axis=1)
        scale = lax.rsqrt(jnp.mean(residual * residual, axis=-1, keepdims=True) + epsilon)
        normed = (residual * scale * g_ref[...]).astype(bf16)
        res_ref[...] = residual
        n_ref[...] = normed
        normed_t = normed.T
        size = width // len(places)
        for source, place in enumerate(places):
            nt_ref[place * size : (place + 1) * size, :] = normed_t[source * size : (source + 1) * size]

    rows_spec = pl.BlockSpec((block, width), lambda i, o: (i, 0))
    cols_spec = pl.BlockSpec((width, block), lambda i, o: (0, i))
    return call(
        kernel,
        (rows // block,),
        [pl.BlockSpec((block, group), lambda i, o: (i, 0))] * count
        + column_blocks(width, first, parts)
        + [rows_spec, resident((1, width), (0, 0))],
        [rows_spec, rows_spec, cols_spec, cols_spec],
        [struct((rows, width), f32), struct((rows, width), bf16)]
        + [struct((width, rows), bf16)] * 2,
        2 * rows * width * width,
        16 * rows * width,
        prefetch=1,
    )(order, *attended, *[weights] * parts, tokens, gain_row)


def gated(normed, cotangent, weights, first, hidden_cols):
    rows, width = normed.shape
    block = 256

    def kernel(n_ref, c_ref, wg_ref, wu_ref, wd_ref, h_ref, gg_ref, gu_ref):
        normed_block = n_ref[...]
        gate = dot(normed_block, wg_ref[...])
        up = dot(normed_block, wu_ref[...])
        grad = dot(c_ref[...], wd_ref[...])
        sg = 1.0 / (1.0 + jnp.exp(-gate))
        silu = gate * sg
        h_ref[...] = (silu * up).astype(bf16)
        gg_ref[...] = (grad * up * sg * (1.0 + gate * (1.0 - sg))).astype(bf16)
        gu_ref[...] = (grad * silu).astype(bf16)

    def weight_spec(k):
        offset = (first + k * hidden_cols) // block
        return pl.BlockSpec((width, block), lambda i: (0, i + offset))

    flat = resident((rows, width), (0, 0))
    out_spec = pl.BlockSpec((rows, block), lambda i: (0, i))
    return call(
        kernel,
        (hidden_cols // block,),
        [flat, flat] + [weight_spec(k) for k in range(3)],
        [out_spec] * 3,
        [struct((rows, hidden_cols), bf16)] * 3,
        6 * rows * width * hidden_cols,
        6 * (rows + width) * hidden_cols,
    )(normed, cotangent, weights, weights, weights)


def norm_back(order, grads, weights, first, residual, cotangent, gain_row):
    rows, width = residual.shape
    count = order.shape[0]
    block = min(256, rows)
    steps = width // block
    row_steps = rows // block
    group = width // count
    parts = width // 256
    n_grads = len(grads)

    def kernel(order_ref, *refs):
        g_refs, w_refs = refs[:n_grads], refs[n_grads : 2 * n_grads]
        wo_refs, refs = refs[2 * n_grads : 2 * n_grads + parts], refs[2 * n_grads + parts :]
        r_ref, c_ref, gain_ref, gres_ref, gb_ref = refs[:5]
        gm_refs, acc = refs[5 : 5 + count], refs[5 + count]
        step = pl.program_id(0)

        @pl.when(step < steps)
        def _():
            total = dot_nt(g_refs[0][...], w_refs[0][...])
            for k in range(1, n_grads):
                total = total + dot_nt(g_refs[k][...], w_refs[k][...])
            acc[:, pl.ds(pl.multiple_of(step * block, block), block)] = total

        @pl.when(step >= steps)
        def _():
            start = pl.multiple_of((step - steps) * block, block)
            grad = acc[pl.ds(start, block), :]
            res = r_ref[...]
            scale = lax.rsqrt(jnp.mean(res * res, axis=-1, keepdims=True) + epsilon)
            unit = res * scale
            scaled = grad * gain_ref[...]
            inner = jnp.mean(scaled * unit, axis=-1, keepdims=True)
            gres = c_ref[...].astype(f32) + scale * (scaled - unit * inner)
            gres_ref[...] = gres
            branch = gres.astype(bf16)
            gb_ref[...] = branch
            for k in range(count):
                start_k = pl.multiple_of(order_ref[k] * group, group)
                mixed = None
                for c in range(parts):
                    part = dot_nt(
                        branch[:, c * 256 : (c + 1) * 256], wo_refs[c][pl.ds(start_k, group), :]
                    )
                    mixed = part if mixed is None else mixed + part
                gm_refs[k][...] = mixed.astype(bf16)

    def row(i):
        return jnp.maximum(i - steps, 0)

    rows_spec = pl.BlockSpec((block, width), lambda i, o: (row(i), 0))
    weight_specs = [
        pl.BlockSpec(
            (block, grads[k].shape[1]),
            functools.partial(lambda c, i, o: (jnp.minimum(i, steps - 1), c), k),
        )
        for k in range(n_grads)
    ]
    hidden_cols = sum(g.shape[1] for g in grads)
    return call(
        kernel,
        (steps + row_steps,),
        [resident(g.shape, (0, 0)) for g in grads]
        + weight_specs
        + column_blocks(width, first, parts)
        + [rows_spec, rows_spec, resident((1, width), (0, 0))],
        [
            rows_spec,
            rows_spec,
        ]
        + [pl.BlockSpec((block, group), lambda i, o: (row(i), 0))] * count,
        [
            struct((rows, width), f32),
            struct((rows, width), bf16),
        ]
        + [struct((rows, group), bf16)] * count,
        2 * rows * width * hidden_cols + 2 * rows * width * width,
        2 * (rows + width) * hidden_cols + 16 * rows * width,
        scratch=[pltpu.VMEM((rows, width), f32)],
        prefetch=1,
    )(order, *grads, *[weights] * (n_grads + parts), residual, cotangent, gain_row)


def products(select, lefts, rights, parts, added=None, joined=False, halves=None):
    height = lefts[0].shape[0]
    block = min(256, height) if halves is None else height // 4
    n = len(rights)
    sizes = [r.shape[1] // p for r, p in zip(rights, parts)]
    added = added or []
    distinct = []
    for left in lefts:
        if not any(left is d for d in distinct):
            distinct.append(left)
    which = [next(i for i, d in enumerate(distinct) if d is left) for left in lefts]
    n_left, n_add = len(distinct), len(added)

    def kernel(select_ref, *refs):
        l_refs, r_refs, outs = refs[:n_left], refs[n_left : n_left + n], refs[n_left + n + n_add :]
        def product(k):
            total = dot(l_refs[which[k]][...], r_refs[k][...])
            if k < n_add:
                total = total + refs[n_left + n + k][...].astype(f32)
            return total.astype(bf16)

        for k in range(n):
            if halves is not None:
                step, mine = pl.program_id(0), select_ref[1 + k]
                keep = (step // 2 if halves[k] == 0 else step % 2) == mine
                for cond, out in ((keep, outs[k]), (jnp.logical_not(keep), outs[n + k])):
                    @pl.when(cond)
                    def _():
                        out[...] = product(k)
            elif joined:
                start = sum(sizes[:k])
                outs[0][:, start : start + sizes[k]] = product(k)
            else:
                outs[k][...] = product(k)

    def right_spec(k):
        return pl.BlockSpec(
            (rights[k].shape[0], sizes[k]),
            lambda i, s: (0, s[0] if parts[k] > 1 else 0),
            pipeline_mode=pl.Buffered(1),
        )

    out_sizes = [sum(sizes)] if joined else sizes
    out_specs = [pl.BlockSpec((block, size), lambda i, s: (i, 0)) for size in out_sizes]
    add_specs = out_specs[:n_add]
    out_shape = [struct((height, size), bf16) for size in out_sizes]
    if halves is not None:

        def half_spec(k, kept):
            def index(i, s):
                value = s[1 + k] if kept else 1 - s[1 + k]
                return (jnp.clip(i - 2 * value, 0, 1) if halves[k] == 0 else i // 2, 0)

            return pl.BlockSpec((block, sizes[k]), index)

        out_specs = [half_spec(k, kept) for kept in (True, False) for k in range(n)]
        out_shape = [struct((height // 2, size), bf16) for size in sizes] * 2
    return call(
        kernel,
        (height // block,),
        [pl.BlockSpec((block, d.shape[1]), lambda i, s: (i, 0)) for d in distinct]
        + [right_spec(k) for k in range(n)]
        + add_specs,
        out_specs,
        out_shape,
        sum(2 * height * r.shape[0] * size for r, size in zip(rights, sizes)),
        2 * height * sum(sizes) + sum(2 * r.shape[0] * size for r, size in zip(rights, sizes)),
        prefetch=1,
    )(select, *distinct, *rights, *added)


def finish(residual, hidden, weights, first):
    rows, width = residual.shape
    block = min(256, rows)
    hidden_cols = hidden.shape[1]

    def kernel(r_ref, h_ref, w_ref, out_ref):
        out_ref[...] = (r_ref[...] + dot_nt(h_ref[...], w_ref[...])).astype(bf16)

    rows_spec = pl.BlockSpec((block, width), lambda i: (i, 0))
    return call(
        kernel,
        (rows // block,),
        [
            rows_spec,
            pl.BlockSpec((block, hidden_cols), lambda i: (i, 0)),
            resident((width, hidden_cols), (0, first)),
        ],
        rows_spec,
        struct((rows, width), bf16),
        2 * rows * width * hidden_cols,
        6 * rows * width + 2 * (rows + width) * hidden_cols,
    )(residual, hidden, weights)


def project_back(order, slot, grads, weights, added=(), part=(0, 1), last=None, into=None):
    length, group = grads[0].shape
    width = weights.shape[0]
    piece = length // order.shape[0]
    rows = piece // part[1]
    block = min(512 if last is None else 256, rows)
    steps = rows // block
    before = part[0] * steps
    n = len(added)

    def kernel(order_ref, a_ref, b_ref, c_ref, w_ref, *refs):
        total = dot_nt(a_ref[...], w_ref[:, :group])
        total = total + dot_nt(b_ref[...], w_ref[:, group : 2 * group])
        total = total + dot_nt(c_ref[...], w_ref[:, 2 * group :])
        for ref in refs[:n]:
            total = total + ref[...].astype(f32)
        if last is not None:
            x_ref, gain_ref, g_ref = refs[n : n + 3]
            x = x_ref[...].astype(f32)
            scale = lax.rsqrt(jnp.mean(x * x, axis=-1, keepdims=True) + epsilon)
            unit = x * scale
            scaled = total * gain_ref[...]
            inner = jnp.mean(scaled * unit, axis=-1, keepdims=True)
            total = g_ref[...] + scale * (scaled - unit * inner)
        refs[-1][...] = total.astype(bf16)

    def rows_of(array):
        first = before if array.shape[0] == piece else 0
        return pl.BlockSpec((block, width), lambda i, order_ref: (i + first, 0))

    def grad_rows(i, order_ref):
        return (order_ref[slot] * (piece // block) + before + i, 0)

    inputs = [*grads, weights, *added]
    in_specs = [pl.BlockSpec((block, group), grad_rows)] * 3 + [resident(weights.shape, (0, 0))]
    in_specs += [rows_of(a) for a in added]
    aliases = {}
    out = struct((rows, width), bf16)
    if last is not None:
        out = struct((piece, width), bf16)
        inputs += last
        in_specs += [rows_of(last[0]), resident((1, width), (0, 0)), rows_of(last[2])]
        if into is not None:
            aliases = {1 + len(inputs): 0}
            inputs.append(into)
            in_specs.append(pl.BlockSpec(memory_space=pl.ANY))
    return call(
        kernel,
        (steps,),
        in_specs,
        rows_of(out),
        out,
        6 * rows * width * group,
        2 * rows * (2 * width + 3 * group),
        prefetch=1,
        aliases=aliases,
    )(order, *inputs)


def pair_add(a, b):
    return (a.astype(f32) + b.astype(f32)).astype(bf16)


def axis_bits(axis, first=1):
    bits = []
    while first < lax.axis_size(axis):
        bits.append(first)
        first *= 2
    return bits


def trade(array, dim, axis, bit):
    count = lax.axis_size(axis)
    mine = (lax.axis_index(axis) // bit) % 2
    keep = lax.dynamic_index_in_dim(array, mine, axis=dim, keepdims=False)
    give = lax.dynamic_index_in_dim(array, 1 - mine, axis=dim, keepdims=False)
    return keep, lax.ppermute(give, axis, [(i, i ^ bit) for i in range(count)])


def scatter_start(array, turn, halve_at):
    count = lax.axis_size("fsdp")
    bits = axis_bits("fsdp")
    bits = bits[turn % len(bits) :] + bits[: turn % len(bits)]
    left = axis_bits("fsdp")[::-1]
    array = array.reshape((2,) * len(bits) + (array.shape[0] // count, array.shape[1]))
    todo = [("fsdp", bit) for bit in bits]
    if halve_at is not None:
        todo[halve_at:halve_at] = [("seq", bit) for bit in axis_bits("seq", 2)]
    return exchange((array, None, todo, left))


def scatter_from(keep, give, axis, bit, left, todo, rows):
    count = lax.axis_size(axis)
    got = lax.ppermute(give, axis, [(i, i ^ bit) for i in range(count)])
    shape = (2,) * len(left) + (rows, keep.shape[1])
    return keep.reshape(shape), got.reshape(shape), todo, left


def exchange(state):
    array, _, todo, left = state
    if not todo:
        return state
    axis, bit = todo[0]
    if axis == "fsdp":
        pair = trade(array, left.index(bit), axis, bit)
        left = [b for b in left if b != bit]
    else:
        rows, n = array.shape[-2:]
        array = array.reshape(array.shape[:-2] + (2, rows // 2, n))
        pair = trade(array, array.ndim - 3, axis, bit)
    return (*pair, todo[1:], left)


def settle(states, done, ahead):
    keeps, done = lax.optimization_barrier(([state[0] for state in states], done))
    arrays = [
        keep if state[1] is None else pair_add(keep, state[1])
        for keep, state in zip(keeps, states)
    ]
    arrays, ahead = lax.optimization_barrier((arrays, ahead))
    return [(a, None) + state[2:] for a, state in zip(arrays, states)], done, ahead


def rows_whole(array, other):
    first = (lax.axis_index("seq") // 2) % 2 == 0
    return both_ways(array, other, first).reshape(-1, array.shape[1])


def last_rows(state):
    return state[0].reshape(state[0].shape[-2:])


def both_ways(own, other, first):
    return jnp.stack([jnp.where(first, own, other), jnp.where(first, other, own)])


def feedforward_ends(half, joined, other, gate_weight, up_weight, gain):
    rows, hidden_cols = gate_weight.shape
    width = joined.shape[1] - 3 * (hidden_cols // 2)
    size = hidden_cols // 2

    def kernel(half_ref, j_ref, o_ref, wg_ref, wu_ref, gain_ref, g_ref, u_ref, d_ref, out_ref, gg_ref):
        def both(k):
            columns = slice(k * size, (k + 1) * size)
            own, far = j_ref[:, columns].astype(f32), o_ref[:, columns].astype(f32)
            lower = half_ref[0] == 0
            return jnp.concatenate(
                [jnp.where(lower, own, far), jnp.where(lower, far, own)], axis=1
            )

        down, gate, up = both(0), both(1), both(2)
        g_ref[...] = gate
        u_ref[...] = up
        d_ref[...] = down.T
        out_ref[...] = j_ref[:, 3 * size :].astype(f32) + o_ref[:, 3 * size :].astype(f32)
        total = jnp.sum(
            wg_ref[...].astype(f32) * gate + wu_ref[...].astype(f32) * up, axis=1, keepdims=True
        )
        gg_ref[...] = jnp.broadcast_to(total / gain_ref[...], (rows, 128)).T[0:1, :]

    whole = lambda shape: pl.BlockSpec(shape, lambda i, h: (0, 0))
    shapes = [(rows, hidden_cols)] * 2 + [(hidden_cols, rows), (rows, width), (1, rows)]
    *ends, gain_grad = call(
        kernel,
        (1,),
        [whole(joined.shape)] * 2 + [whole(gate_weight.shape)] * 2 + [whole((rows, 1))],
        [whole(shape) for shape in shapes],
        [struct(shape, f32) for shape in shapes],
        4 * rows * hidden_cols,
        20 * rows * hidden_cols,
        prefetch=1,
    )(half, joined, other, gate_weight, up_weight, gain.astype(f32)[:, None])
    return *ends, gain_grad[0]


def projection_ends(order, pieces, weights, gain):
    rows, width = weights[0].shape
    count = len(pieces)
    group = width // count

    def kernel(order_ref, *refs):
        p_refs, refs = refs[:count], refs[count:]
        w_refs, gain_ref, outs, gg_ref = refs[:3], refs[3], refs[4:7], refs[7]
        for k in range(count):
            start = pl.multiple_of(order_ref[k] * group, group)
            for j in range(3):
                outs[j][:, pl.ds(start, group)] = p_refs[k][
                    :, j * group : (j + 1) * group
                ].astype(f32)
        total = None
        for j in range(3):
            part = jnp.sum(w_refs[j][...].astype(f32) * outs[j][...], axis=1, keepdims=True)
            total = part if total is None else total + part
        gg_ref[...] = jnp.broadcast_to(total / gain_ref[...], (rows, 128)).T[0:1, :]

    whole = lambda shape: pl.BlockSpec(shape, lambda i, o: (0, 0))
    shapes = [(rows, width)] * 3 + [(1, rows)]
    *ends, gain_grad = call(
        kernel,
        (1,),
        [whole(pieces[0].shape)] * count + [whole((rows, width))] * 3 + [whole((rows, 1))],
        [whole(shape) for shape in shapes],
        [struct(shape, f32) for shape in shapes],
        6 * rows * width,
        24 * rows * width,
        prefetch=1,
    )(order, *pieces, *weights, gain.astype(f32)[:, None])
    return *ends, gain_grad[0]


def body(
    tokens, cotangent, query_weight, key_weight, value_weight, output_weight, gate_weight, up_weight,
    down_weight, attention_gain, feedforward_gain, cache_keys, cache_values, memory_rows, memory_docs,
):
    seq_count, fsdp_count = lax.axis_size("seq"), lax.axis_size("fsdp")
    here = lax.axis_index("seq")
    tok_rows, width = tokens.shape
    head_local, rows_cache, head_dim = cache_keys.shape[1:]
    group = head_local * head_dim
    length = tok_rows * seq_count
    mem_block = length // memory_rows.shape[2]
    mem_count = memory_rows.shape[3]
    shard = query_weight.shape[0]
    hidden_cols = gate_weight.shape[1]
    order = here ^ jnp.arange(seq_count, dtype=jnp.int32)

    gains = spread(jnp.stack([attention_gain, feedforward_gain]), "fsdp")
    gains = gains.transpose(1, 0, 2).reshape(2, width).astype(f32)
    gain_one, gain_two = gains[0:1], gains[1:2]
    own_cols = [
        lax.dynamic_slice_in_dim(w, here * group, group, axis=1)
        for w in (query_weight, key_weight, value_weight)
    ]
    qkv = spread(jnp.concatenate(own_cols, axis=1), "fsdp").reshape(width, 3 * group)

    pieces = [tokens, swap_seq(tokens, 1), swap_seq(tokens, 2)]
    pieces.append(swap_seq(pieces[2], 1))

    ring = [(i, (i + 1) % fsdp_count) for i in range(fsdp_count)]
    partner_keys = lax.ppermute(cache_keys[0], "fsdp", ring)
    partner_values = lax.ppermute(cache_values[0], "fsdp", ring)

    part = shard // seq_count

    def own_rows(w):
        return lax.dynamic_slice_in_dim(w, here * part, part, axis=0)

    own_wd = lax.dynamic_slice_in_dim(down_weight, here * part, part, axis=1).T
    own_part = jnp.concatenate(
        [own_rows(gate_weight), own_rows(up_weight), own_wd, own_rows(output_weight)], axis=1
    )
    big = lax.all_gather(own_part, ("fsdp", "seq"), axis=0, tiled=True)

    half = head_dim // 2
    frequency = 10000.0 ** (-2.0 * jnp.arange(half, dtype=f32) / head_dim)
    near_count = 64
    near_angles = jnp.arange(near_count, dtype=f32)[:, None] * frequency[None, :]
    far_angles = jnp.arange(0, length, near_count).astype(f32)[:, None] * frequency[None, :]
    near_angles, far_angles = near_angles[None], far_angles[:, None]
    near_cos, near_sin, far_cos, far_sin = lax.optimization_barrier(
        (jnp.cos(near_angles), jnp.sin(near_angles), jnp.cos(far_angles), jnp.sin(far_angles))
    )
    cos_half = (far_cos * near_cos - far_sin * near_sin).reshape(length, half)
    sin_half = (far_sin * near_cos + far_cos * near_sin).reshape(length, half)
    cosine = jnp.concatenate([cos_half, cos_half], axis=1)
    sine = jnp.concatenate([-sin_half, sin_half], axis=1)
    cotangent_t = cotangent.T.reshape(fsdp_count, 2, shard // 2, tok_rows)
    cotangent_t = cotangent_t.swapaxes(0, 1).reshape(width, tok_rows)
    places = [
        (f % 4 // 2 + f % 2 * 2) * (fsdp_count // 4) + f // 4 for f in range(fsdp_count)
    ]

    chosen = memory_docs[0] * rows_cache + memory_rows[0]
    picked = retrieve(chosen, cache_keys[0], cache_values[0], 0)
    query, key, value, value_t, normed_one_t = project(
        order, pieces, qkv, gain_one, cosine, sine, head_local, head_dim
    )
    picked_keys, picked_values = retrieve(chosen, partner_keys, partner_values, rows_cache, picked)
    *attended_heads, lse = attend(
        order, query, key, value_t, picked_keys, picked_values, mem_block, mem_count, seq_count
    )

    def by_distance(stack):
        return [stack[0]] + [swap_seq(stack[k], k) for k in range(1, seq_count)]

    attended = by_distance(attended_heads)
    residual, normed_two, normed_two_t, attended_t = mix(
        order, attended, big, 3 * hidden_cols, tokens, gain_two, places
    )
    hid, gg, gu = gated(normed_two, cotangent, big, 0, hidden_cols)
    own_half, other_half = (here % 2)[None].astype(jnp.int32), (1 - here % 2)[None].astype(jnp.int32)
    lefts, rights = [cotangent_t, normed_two_t, normed_two_t], [hid, gg, gu]
    given = products(other_half, lefts, rights, (2, 2, 2))
    given, gg_later = lax.optimization_barrier((given, gg))
    got = [swap_seq(g, 1) for g in given]
    grad_residual, grad_branch, *grad_mixed = norm_back(
        order, [gg_later, gu], big, 3 * hidden_cols, residual, cotangent, gain_two
    )
    grad_heads = by_distance(grad_mixed)
    bits, upper = axis_bits("fsdp"), axis_bits("seq", 2)
    firsts = (("seq", upper[0]), ("fsdp", bits[0]), ("fsdp", bits[1]), ("fsdp", bits[-1]))
    mine = [(lax.axis_index(axis) // bit) % 2 for axis, bit in firsts]
    select = jnp.stack([here % 2, *mine]).astype(jnp.int32)
    own = products(
        select, [*lefts, attended_t], [*rights, grad_branch], (2, 2, 2, 1), got, halves=(0, 0, 1, 0)
    )
    grad_heads, own = lax.optimization_barrier((grad_heads, own))
    down = bits[::-1]
    over = lambda *picks: [("fsdp", b) if b else ("seq", upper[0]) for b in picks]
    sums = [
        scatter_from(keep, give, axis, bit, left, todo, rows)
        for keep, give, (axis, bit), left, todo, rows in zip(
            own[:4],
            own[4:],
            firsts,
            (down, [bits[1], *down[: -2]], [bits[0], *down[: -2]], down[1:]),
            (
                over(*bits),
                over(0, *bits[1:]),
                over(0, *bits[2:], bits[0]),
                over(bits[0], 0, *bits[1:-1]),
            ),
            (shard // 2, shard, shard, shard),
        )
    ]

    blocks = lse.shape[0]
    middle = 3 * blocks // 8
    attention = (order, query, key, value, picked_keys, picked_values, mem_block, mem_count)
    *grads, rest, delta = attend_back(
        *attention, grad_heads, attended_heads, lse, cosine, sine, 0, middle
    )
    sums, _, (rest, delta) = settle(sums, (), (rest, delta))
    sums = [exchange(g) for g in sums]
    grads = attend_back(
        *attention, grad_heads, None, lse, cosine, sine, middle, blocks, (rest, delta, *grads)
    )

    zero = jnp.zeros((1,), jnp.int32)
    sums, _, grads = settle(sums, (), grads)
    sums = [exchange(g) for g in sums]
    far_part = project_back(order, 3, grads, qkv)
    far = swap_seq(far_part, 1)
    far_part, grads = lax.optimization_barrier((far_part, grads))
    near_part = project_back(order, 1, grads, qkv)
    near = swap_seq(near_part, 1)
    far, near_part, grads = lax.optimization_barrier((far, near_part, grads))
    half = project_back(order, 2, grads, qkv, [far], (0, 2))
    across = [swap_seq(half, 2)]
    half, grads = lax.optimization_barrier((half, grads))
    half = project_back(order, 2, grads, qkv, [far], (1, 2))
    across.append(swap_seq(half, 2))
    half, grads = lax.optimization_barrier((half, grads))
    (qkv_grad,) = products(zero, [normed_one_t] * 3, list(grads), (1, 1, 1), joined=True)
    qkv_state = scatter_start(qkv_grad, 0, None)
    across[0], qkv_grad, grads = lax.optimization_barrier((across[0], qkv_grad, grads))
    sums, across[0], near = settle(sums, across[0], near)
    sums = [exchange(g) for g in sums]
    (qkv_state, *sums), _, near = settle([qkv_state, *sums], (), near)
    while any(state[2] for state in sums):
        sums = settle([exchange(g) for g in sums], (), ())[0]
    qkv_state = exchange(qkv_state)
    joined = jnp.concatenate([last_rows(state) for state in sums], axis=1)
    lower = swap_seq(joined, upper[0])
    last = (tokens, gain_one, grad_residual)
    grad_tokens = project_back(order, 0, grads, qkv, [near, across[0]], (0, 2), last)
    (qkv_state,), grad_tokens, (hid, across[1]) = settle(
        [qkv_state], grad_tokens, (hid, across[1])
    )
    qkv_state = exchange(qkv_state)
    result = finish(residual, hid, big, 2)
    grad_tokens = project_back(
        order, 0, grads, qkv, [near, across[1]], (1, 2), last, grad_tokens
    )
    joined, grad_tokens = lax.optimization_barrier((joined, grad_tokens))
    joined = rows_whole(joined, lower)
    other = swap_seq(joined, 1)
    (qkv_state,), _, _ = settle([qkv_state], (result, grad_tokens), ())
    while qkv_state[2]:
        qkv_state = settle([exchange(qkv_state)], (), ())[0][0]
    qkv_pieces = by_distance([last_rows(qkv_state)] * seq_count)
    grad_gate, grad_up, grad_down, grad_out, grad_gain_two = feedforward_ends(
        own_half, joined, other, gate_weight, up_weight, feedforward_gain
    )
    qkv_pieces[0], grad_out = lax.optimization_barrier((qkv_pieces[0], grad_out))
    grad_q, grad_k, grad_v, grad_gain_one = projection_ends(
        order, qkv_pieces, (query_weight, key_weight, value_weight), attention_gain
    )
    return (
        result,
        grad_tokens,
        grad_q,
        grad_k,
        grad_v,
        grad_out,
        grad_gate,
        grad_up,
        grad_down,
        grad_gain_one,
        grad_gain_two,
    )


def solution(mesh):
    tok, row, col, one = P(("fsdp", "seq"), None), P("fsdp", None), P(None, "fsdp"), P("fsdp")
    cache = P("fsdp", "seq", None, None)
    return jax.shard_map(
        body,
        mesh=mesh,
        in_specs=(tok, tok) + (row,) * 6 + (col, one, one) + (cache,) * 4,
        out_specs=(tok, tok) + (row,) * 6 + (col, one, one),
        check_vma=False,
    )
```

```python
import functools

import jax
import jax.numpy as jnp
from jax import lax
from jax.experimental import pallas as pl
from jax.experimental.pallas import tpu as pltpu
from jax.sharding import PartitionSpec as P

epsilon = 1e-06
log2e = 1.4426950408889634
f32 = jnp.float32
bf16 = jnp.bfloat16
VMEM_LIMIT = 60 * 1024 * 1024
hint = 0.15


def dot(a, b):
    return jnp.dot(a, b, preferred_element_type=f32)


def dot_nt(a, b):
    return lax.dot_general(a, b, (((1,), (1,)), ((), ())), preferred_element_type=f32)


def dot_tn(a, b):
    return lax.dot_general(a, b, (((0,), (0,)), ((), ())), preferred_element_type=f32)


def call(
    kernel, grid, in_specs, out_specs, out_shape, flops, bytes_accessed, scratch=(), prefetch=0, aliases=None
):
    return pl.pallas_call(
        kernel,
        name=kernel.__qualname__.split(".")[0],
        grid_spec=pltpu.PrefetchScalarGridSpec(
            num_scalar_prefetch=prefetch,
            grid=grid,
            in_specs=in_specs,
            out_specs=out_specs,
            scratch_shapes=list(scratch),
        ),
        out_shape=out_shape,
        input_output_aliases=aliases or {},
        compiler_params=pltpu.CompilerParams(
            dimension_semantics=("arbitrary",) * len(grid), vmem_limit_bytes=VMEM_LIMIT
        ),
        cost_estimate=pl.CostEstimate(
            flops=int(flops * hint), bytes_accessed=int(bytes_accessed * hint), transcendentals=0
        ),
    )


def resident(shape, index):
    return pl.BlockSpec(shape, lambda *_: index, pipeline_mode=pl.Buffered(1))


def column_blocks(height, first, parts):
    return [resident((height, 256), (0, first // 256 + c)) for c in range(parts)]


def struct(shape, dtype):
    return jax.ShapeDtypeStruct(shape, dtype)


def swap_seq(array, bit):
    count = lax.axis_size("seq")
    return lax.ppermute(array, "seq", [(i, i ^ bit) for i in range(count)])


def spread(array, axis):
    count = lax.axis_size(axis)
    copies = jnp.broadcast_to(array[None], (count,) + array.shape)
    return lax.all_to_all(copies, axis, split_axis=0, concat_axis=0, tiled=True)


def project(order, pieces, weights, gain_row, cosine, sine, head_local, head_dim):
    rows, width = pieces[0].shape
    count = len(pieces)
    block = min(512, rows)
    steps = rows // block
    length = rows * count
    cols = weights.shape[1]
    group = head_local * head_dim

    def kernel(order_ref, *refs):
        xs = refs[:count]
        w_ref, g_ref, c_ref, s_ref, q_ref, k_ref, v_ref, vt_ref, nt_ref, x_block = refs[count:]
        slot = pl.program_id(0)

        def run(x_ref):
            x = x_ref[...].astype(f32)
            scale = lax.rsqrt(jnp.mean(x * x, axis=-1, keepdims=True) + epsilon)
            normed = (x * scale * g_ref[...]).astype(bf16)
            nt_ref[...] = normed.T
            lin = dot(normed, w_ref[...])
            cos, sin = c_ref[...], s_ref[...]
            for head in range(head_local):
                for part, out in ((0, q_ref), (1, k_ref)):
                    start = part * group + head * head_dim
                    u = lin[:, start : start + head_dim]
                    out[head] = (u * cos + pltpu.roll(u, head_dim // 2, 1) * sin).astype(bf16)
                start = 2 * group + head * head_dim
                v = lin[:, start : start + head_dim].astype(bf16)
                v_ref[head] = v
                vt_ref[head] = v.T

        for k in range(count):
            @pl.when(slot == k)
            def _():
                x_block[...] = xs[k][...]

        run(x_block)

    def piece_spec(k):
        return pl.BlockSpec(
            (block, width),
            lambda slot, i, order_ref: (
                jnp.where(slot == k, i, jnp.where(slot < k, 0, steps - 1)),
                0,
            ),
        )

    def at_rows(slot, i, order_ref):
        return order_ref[slot] * steps + i

    head_spec = pl.BlockSpec((head_local, block, head_dim), lambda *a: (0, at_rows(*a), 0))
    table_spec = pl.BlockSpec((block, head_dim), lambda *a: (at_rows(*a), 0))
    heads = struct((head_local, length, head_dim), bf16)
    return call(
        kernel,
        (count, steps),
        [piece_spec(k) for k in range(count)]
        + [resident((width, cols), (0, 0)), resident((1, width), (0, 0)), table_spec, table_spec],
        [
            head_spec,
            head_spec,
            head_spec,
            pl.BlockSpec((head_local, head_dim, block), lambda *a: (0, 0, at_rows(*a))),
            pl.BlockSpec((width, block), lambda *a: (0, at_rows(*a))),
        ],
        [heads, heads, heads, struct((head_local, head_dim, length), bf16)]
        + [struct((width, length), bf16)],
        2 * length * width * cols,
        4 * length * width + 2 * length * cols + 8 * length * head_dim,
        scratch=[pltpu.VMEM((block, width), bf16)],
        prefetch=1,
    )(order, *pieces, weights, gain_row, cosine, sine)


def retrieve(chosen, keys, values, base, before=None):
    head_local, rows_cache, head_dim = keys.shape
    blocks, slots = chosen.shape[1:]
    per = min(4, blocks)
    total = blocks * slots

    def kernel(c_ref, k_ref, v_ref, *refs):
        if before is not None:
            bk_ref, bv_ref = refs[:2]
        ok_ref, ov_ref, table, mask = refs[-4:]

        @pl.when(pl.program_id(1) == 0)
        def _():
            table[:, :head_dim] = k_ref[0]
            table[:, head_dim:] = v_ref[0]

        for b in range(per):
            row = c_ref[0, 0, b : b + 1, :] - base
            column = jnp.broadcast_to(row, (slots, slots)).T
            lane = lax.broadcasted_iota(jnp.int32, (slots, slots), 1)
            for start in range(0, rows_cache, slots):
                mask[b * slots : (b + 1) * slots, start : start + slots] = jnp.where(
                    column == lane + start, 1.0, 0.0
                ).astype(bf16)
        picked = dot(mask[...], table[...])
        if before is not None:
            picked_keys = picked[:, :head_dim] + bk_ref[0].astype(f32)
            picked_values = picked[:, head_dim:] + bv_ref[0].astype(f32)
        else:
            picked_keys, picked_values = picked[:, :head_dim], picked[:, head_dim:]
        ok_ref[0] = picked_keys.astype(bf16)
        ov_ref[0] = picked_values.astype(bf16)

    out_spec = pl.BlockSpec((1, per * slots, head_dim), lambda h, i: (h, i, 0))
    table_spec = pl.BlockSpec((1, rows_cache, head_dim), lambda h, i: (h, 0, 0))
    extra = () if before is None else before
    out = struct((head_local, total, head_dim), bf16)
    return call(
        kernel,
        (head_local, blocks // per),
        [pl.BlockSpec((1, 1, per, slots), lambda h, i: (h, i, 0, 0)), table_spec, table_spec]
        + [out_spec] * len(extra),
        [out_spec, out_spec],
        [out, out],
        4 * head_local * total * rows_cache * head_dim,
        8 * head_local * total * head_dim,
        scratch=[
            pltpu.VMEM((rows_cache, 2 * head_dim), bf16),
            pltpu.VMEM((per * slots, rows_cache), bf16),
        ],
    )(chosen.reshape(head_local, blocks // per, per, slots), keys, values, *extra)


def attend(order, query, key, value_t, memory_keys, memory_values, mem_block, mem_count, count):
    head_local, length, head_dim = query.shape
    block = length // count
    half = block // 2
    groups = block // mem_block
    factor = head_dim ** (-0.5) * log2e

    def kernel(order_ref, q_ref, k_ref, vt_ref, mk_ref, mv_ref, *refs):
        o_refs, lse_ref = refs[:count], refs[count]
        index = pl.program_id(0)

        def memory(head):
            parts = []
            for g in range(groups):
                q = q_ref[head, g * mem_block : (g + 1) * mem_block, :]
                parts.append(dot_nt(mk_ref[head, g * mem_count : (g + 1) * mem_count, :], q))
            scores = jnp.concatenate(parts, axis=1) * factor
            top = jnp.max(scores, axis=0, keepdims=True)
            weight = jnp.exp2(scores - top)
            total = jnp.sum(weight, axis=0, keepdims=True)
            weight = weight.astype(bf16)
            values_t = mv_ref[head].T
            mixed = jnp.concatenate(
                [
                    dot(
                        values_t[:, g * mem_count : (g + 1) * mem_count],
                        weight[:, g * mem_block : (g + 1) * mem_block],
                    )
                    for g in range(groups)
                ],
                axis=1,
            )
            return top, total, mixed

        def step(head, carry, start, size, queries, offset):
            top, total, mixed = carry
            keys = k_ref[head, pl.ds(start, size), :]
            scores = dot_nt(keys, q_ref[head, queries, :]) * factor
            if offset is not None:
                row = lax.broadcasted_iota(jnp.int32, scores.shape, 0) + offset
                col = lax.broadcasted_iota(jnp.int32, scores.shape, 1) + (queries.start or 0)
                scores = jnp.where(row <= col, scores, -jnp.inf)
            new_top = jnp.maximum(top, jnp.max(scores, axis=0, keepdims=True))
            decay = jnp.exp2(top - new_top)
            weight = jnp.exp2(scores - new_top)
            total = total * decay + jnp.sum(weight, axis=0, keepdims=True)
            mixed = mixed * decay + dot(vt_ref[head, :, pl.ds(start, size)], weight.astype(bf16))
            return new_top, total, mixed

        every, later = slice(0, block), slice(half, block)
        carries = tuple(memory(head) for head in range(head_local))
        carries = lax.fori_loop(
            0,
            index,
            lambda j, c: tuple(
                step(head, c[head], pl.multiple_of(j * block, block), block, every, None)
                for head in range(head_local)
            ),
            carries,
        )
        start = pl.multiple_of(index * block, block)
        for head in range(head_local):
            carry = step(head, carries[head], start, half, every, 0)
            last = tuple(part[:, half:] for part in carry)
            middle = pl.multiple_of(start + half, half)
            last = step(head, last, middle, half, later, half)
            top, total, mixed = (
                jnp.concatenate([part[:, :half], end], axis=1) for part, end in zip(carry, last)
            )
            columns = slice(head * head_dim, (head + 1) * head_dim)
            mixed = (mixed / total).T.astype(bf16)
            for k in range(count):
                @pl.when(index == order_ref[k])
                def _():
                    o_refs[k][:, columns] = mixed
            lse = top + jnp.log2(total)
            lse_ref[0, head : head + 1, :] = lse[:, :half]
            lse_ref[1, head : head + 1, :] = lse[:, half:]

    full = resident((head_local, length, head_dim), (0, 0, 0))
    full_t = resident((head_local, head_dim, length), (0, 0, 0))
    rows = pl.BlockSpec((head_local, block, head_dim), lambda i, order_ref: (0, i, 0))
    mem_rows = pl.BlockSpec(
        (head_local, groups * mem_count, head_dim), lambda i, order_ref: (0, i, 0)
    )
    return call(
        kernel,
        (count,),
        [rows, full, full_t, mem_rows, mem_rows],
        [pl.BlockSpec((block, head_local * head_dim), lambda i, order_ref: (0, 0))] * count
        + [pl.BlockSpec((2, 8, half), lambda i, order_ref: (i, 0, 0))],
        [struct((block, head_local * head_dim), bf16)] * count
        + [struct((2 * count, 8, half), f32)],
        4 * head_local * length * length * head_dim,
        12 * head_local * length * head_dim,
        prefetch=1,
    )(order, query, key, value_t, memory_keys, memory_values)


def attend_back(
    order, query, key, value, memory_keys, memory_values, mem_block, mem_count, grads, attended, lse,
    cosine, sine, first, last, carried=None,
):
    head_local, length, head_dim = query.shape
    count, _, block = lse.shape
    pieces = len(grads)
    piece = length // pieces
    per = piece // block
    groups = block // mem_block
    scale = head_dim ** (-0.5)
    factor = scale * log2e
    opening, closing = first == 0, last == count

    def kernel(order_ref, q_ref, k_ref, v_ref, mk_ref, mv_ref, *refs):
        g_refs, refs = refs[:pieces], refs[pieces:]
        if opening:
            o_refs, refs = refs[:pieces], refs[pieces:]
        else:
            (part_ref, delta), refs = refs[:2], refs[5:]
        (lse_ref, c_ref, s_ref, dq_ref, dk_ref, dv_ref), refs = refs[:6], refs[6:]
        if opening and not closing:
            (rest_ref, delta), refs = refs[:2], refs[2:]
        elif opening:
            delta, refs = refs[0], refs[1:]
        dq_acc, do_ref = refs
        index = pl.program_id(0) + first

        def cols(head):
            return slice(head * head_dim, (head + 1) * head_dim)

        @pl.when(index == first)
        def _():
            for k in range(pieces):
                start = pl.multiple_of(order_ref[k] * piece, piece)
                do_ref[pl.ds(start, piece), :] = g_refs[k][...]
            if not opening:
                dq_acc[:, :, first * block :] = part_ref[...]
            else:
                for k in range(pieces):
                    for p in range(per):
                        rows = slice(p * block, (p + 1) * block)
                        for head in range(head_local):
                            do = g_refs[k][rows, cols(head)].astype(f32)
                            o = o_refs[k][rows, cols(head)].astype(f32)
                            row = jnp.sum((do * o).T, axis=0, keepdims=True)
                            delta[order_ref[k] * per + p, head : head + 1, :] = row

        row_id = lax.broadcasted_iota(jnp.int32, (block, block), 0)
        col_id = lax.broadcasted_iota(jnp.int32, (block, block), 1)
        keys_t = [k_ref[head].T for head in range(head_local)]

        def memory(head):
            start = pl.multiple_of(index * block, block)
            q = q_ref[head, pl.ds(start, block), :]
            do = do_ref[pl.ds(start, block), cols(head)]
            scores = dot_nt(mk_ref[head], q)
            weight = jnp.exp2(scores * factor - lse_ref[index, head : head + 1, :])
            slot = lax.broadcasted_iota(jnp.int32, scores.shape, 0) // mem_count
            own = slot == lax.broadcasted_iota(jnp.int32, scores.shape, 1) // mem_block
            dp = dot_nt(mv_ref[head], do)
            ds = jnp.where(own, weight * (dp - delta[index, head : head + 1, :]), 0.0)
            return dot(mk_ref[head].T, ds.astype(bf16))

        def step(head, carry, i, masked):
            dk, dv = carry
            start = pl.multiple_of(i * block, block)
            q = q_ref[head, pl.ds(start, block), :]
            do = do_ref[pl.ds(start, block), cols(head)]
            k, v = k_ref[head], v_ref[head]
            weight = jnp.exp2(dot_nt(k, q) * factor - lse_ref[i, head : head + 1, :])
            if masked:
                weight = jnp.where(row_id <= col_id, weight, 0.0)
            dp = dot_nt(v, do)
            ds = (weight * (dp - delta[i, head : head + 1, :])).astype(bf16)
            dv = dv + dot(weight.astype(bf16), do)
            dk = dk + dot(ds, q)
            so_far = dq_acc[head, :, pl.ds(start, block)]
            if opening:
                so_far = jnp.where(index == 0, 0.0, so_far)
            total = so_far + dot(keys_t[head], ds)
            if masked:
                return dk, dv, total
            dq_acc[head, :, pl.ds(start, block)] = total
            return dk, dv

        cos, sin = c_ref[...], s_ref[...]

        def unrotate(grad_rows):
            u = (grad_rows * scale).astype(bf16).astype(f32)
            return (u * cos - pltpu.roll(u, head_dim // 2, 1) * sin).astype(bf16)

        zero = jnp.zeros((block, head_dim), f32)
        carries = []
        for head in range(head_local):
            dk, dv, dq = step(head, (zero, zero), index, True)
            dq_ref[:, cols(head)] = unrotate((dq + memory(head)).T)
            carries.append((dk, dv))
        carries = lax.fori_loop(
            index + 1,
            count,
            lambda i, c: tuple(step(head, c[head], i, False) for head in range(head_local)),
            tuple(carries),
        )
        for head, (dk, dv) in enumerate(carries):
            dk_ref[:, cols(head)] = unrotate(dk)
            dv_ref[:, cols(head)] = dv.astype(bf16)
        if opening and not closing:
            @pl.when(index == last - 1)
            def _():
                rest_ref[...] = dq_acc[:, :, last * block :]

    group = head_local * head_dim
    full = resident((head_local, length, head_dim), (0, 0, 0))
    flat = resident((piece, group), (0, 0))
    rows = pl.BlockSpec((head_local, block, head_dim), lambda i, o: (0, i + first, 0))
    mem_rows = pl.BlockSpec(
        (head_local, groups * mem_count, head_dim), lambda i, o: (0, i + first, 0)
    )
    table = pl.BlockSpec((block, head_dim), lambda i, o: (i + first, 0))
    out_rows = pl.BlockSpec((block, group), lambda i, o: (i + first, 0))
    out = struct((length, group), bf16)
    aliases = {}
    small = resident(lse.shape, (0, 0, 0))
    in_specs = [full, rows, rows, mem_rows, mem_rows] + [flat] * pieces
    inputs = [query, key, value, memory_keys, memory_values, *grads]
    out_specs, out_shape, scratch = [out_rows] * 3, [out] * 3, []
    if opening:
        in_specs += [flat] * pieces
        inputs += list(attended)
        if closing:
            scratch.append(pltpu.VMEM(lse.shape, f32))
        else:
            rest = (head_local, head_dim, length - last * block)
            out_specs += [pl.BlockSpec(rest, lambda i, o: (0, 0, 0)), pl.BlockSpec(lse.shape, lambda i, o: (0, 0, 0))]
            out_shape += [struct(rest, f32), struct(lse.shape, f32)]
    else:
        in_specs += [resident(carried[0].shape, (0, 0, 0)), small]
        in_specs += [pl.BlockSpec(memory_space=pl.ANY)] * 3
        aliases = {1 + len(inputs) + 2 + k: k for k in range(3)}
        inputs += list(carried)
    done = sum(count - j for j in range(first, last)) / (count * (count + 1) / 2)
    return call(
        kernel,
        (last - first,),
        in_specs + [small, table, table],
        out_specs,
        out_shape,
        done * 10 * head_local * length * length * head_dim // 2,
        24 * head_local * length * head_dim,
        scratch=scratch
        + [pltpu.VMEM((head_local, head_dim, length), f32), pltpu.VMEM((length, group), bf16)],
        prefetch=1,
        aliases=aliases,
    )(order, *inputs, lse, cosine, sine)


def mix(order, attended, weights, first, tokens, gain_row, places):
    count = len(attended)
    rows, group = attended[0].shape
    width = tokens.shape[1]
    block = min(256, rows)
    parts = width // 256

    def kernel(order_ref, *refs):
        a_refs = refs[:count]
        w_refs, refs = refs[count : count + parts], refs[count + parts :]
        x_ref, g_ref, res_ref, n_ref, nt_ref, at_ref = refs
        residual = x_ref[...].astype(f32)
        mixed = [None] * parts
        for k in range(count):
            start = pl.multiple_of(order_ref[k] * group, group)
            for c in range(parts):
                part = dot(a_refs[k][...], w_refs[c][pl.ds(start, group), :])
                mixed[c] = part if mixed[c] is None else mixed[c] + part
            at_ref[pl.ds(start, group), :] = a_refs[k][...].T
        residual = residual + jnp.concatenate(mixed, axis=1)
        scale = lax.rsqrt(jnp.mean(residual * residual, axis=-1, keepdims=True) + epsilon)
        normed = (residual * scale * g_ref[...]).astype(bf16)
        res_ref[...] = residual
        n_ref[...] = normed
        normed_t = normed.T
        size = width // len(places)
        for source, place in enumerate(places):
            nt_ref[place * size : (place + 1) * size, :] = normed_t[source * size : (source + 1) * size]

    rows_spec = pl.BlockSpec((block, width), lambda i, o: (i, 0))
    cols_spec = pl.BlockSpec((width, block), lambda i, o: (0, i))
    return call(
        kernel,
        (rows // block,),
        [pl.BlockSpec((block, group), lambda i, o: (i, 0))] * count
        + column_blocks(width, first, parts)
        + [rows_spec, resident((1, width), (0, 0))],
        [rows_spec, rows_spec, cols_spec, cols_spec],
        [struct((rows, width), f32), struct((rows, width), bf16)]
        + [struct((width, rows), bf16)] * 2,
        2 * rows * width * width,
        16 * rows * width,
        prefetch=1,
    )(order, *attended, *[weights] * parts, tokens, gain_row)


def gated(normed, cotangent, weights, first, hidden_cols):
    rows, width = normed.shape
    block = 256

    def kernel(n_ref, c_ref, wg_ref, wu_ref, wd_ref, h_ref, gg_ref, gu_ref):
        normed_block = n_ref[...]
        gate = dot(normed_block, wg_ref[...])
        up = dot(normed_block, wu_ref[...])
        grad = dot(c_ref[...], wd_ref[...])
        sg = 1.0 / (1.0 + jnp.exp(-gate))
        silu = gate * sg
        h_ref[...] = (silu * up).astype(bf16)
        gg_ref[...] = (grad * up * sg * (1.0 + gate * (1.0 - sg))).astype(bf16)
        gu_ref[...] = (grad * silu).astype(bf16)

    def weight_spec(k):
        offset = (first + k * hidden_cols) // block
        return pl.BlockSpec((width, block), lambda i: (0, i + offset))

    flat = resident((rows, width), (0, 0))
    out_spec = pl.BlockSpec((rows, block), lambda i: (0, i))
    return call(
        kernel,
        (hidden_cols // block,),
        [flat, flat] + [weight_spec(k) for k in range(3)],
        [out_spec] * 3,
        [struct((rows, hidden_cols), bf16)] * 3,
        6 * rows * width * hidden_cols,
        6 * (rows + width) * hidden_cols,
    )(normed, cotangent, weights, weights, weights)


def norm_back(order, grads, weights, first, residual, cotangent, gain_row):
    rows, width = residual.shape
    count = order.shape[0]
    block = min(256, rows)
    steps = width // block
    row_steps = rows // block
    group = width // count
    parts = width // 256
    n_grads = len(grads)

    def kernel(order_ref, *refs):
        g_refs, w_refs = refs[:n_grads], refs[n_grads : 2 * n_grads]
        wo_refs, refs = refs[2 * n_grads : 2 * n_grads + parts], refs[2 * n_grads + parts :]
        r_ref, c_ref, gain_ref, gres_ref, gb_ref = refs[:5]
        gm_refs, acc = refs[5 : 5 + count], refs[5 + count]
        step = pl.program_id(0)

        @pl.when(step < steps)
        def _():
            total = dot_nt(g_refs[0][...], w_refs[0][...])
            for k in range(1, n_grads):
                total = total + dot_nt(g_refs[k][...], w_refs[k][...])
            acc[:, pl.ds(pl.multiple_of(step * block, block), block)] = total

        @pl.when(step >= steps)
        def _():
            start = pl.multiple_of((step - steps) * block, block)
            grad = acc[pl.ds(start, block), :]
            res = r_ref[...]
            scale = lax.rsqrt(jnp.mean(res * res, axis=-1, keepdims=True) + epsilon)
            unit = res * scale
            scaled = grad * gain_ref[...]
            inner = jnp.mean(scaled * unit, axis=-1, keepdims=True)
            gres = c_ref[...].astype(f32) + scale * (scaled - unit * inner)
            gres_ref[...] = gres
            branch = gres.astype(bf16)
            gb_ref[...] = branch
            for k in range(count):
                start_k = pl.multiple_of(order_ref[k] * group, group)
                mixed = None
                for c in range(parts):
                    part = dot_nt(
                        branch[:, c * 256 : (c + 1) * 256], wo_refs[c][pl.ds(start_k, group), :]
                    )
                    mixed = part if mixed is None else mixed + part
                gm_refs[k][...] = mixed.astype(bf16)

    def row(i):
        return jnp.maximum(i - steps, 0)

    rows_spec = pl.BlockSpec((block, width), lambda i, o: (row(i), 0))
    weight_specs = [
        pl.BlockSpec(
            (block, grads[k].shape[1]),
            functools.partial(lambda c, i, o: (jnp.minimum(i, steps - 1), c), k),
        )
        for k in range(n_grads)
    ]
    hidden_cols = sum(g.shape[1] for g in grads)
    return call(
        kernel,
        (steps + row_steps,),
        [resident(g.shape, (0, 0)) for g in grads]
        + weight_specs
        + column_blocks(width, first, parts)
        + [rows_spec, rows_spec, resident((1, width), (0, 0))],
        [
            rows_spec,
            rows_spec,
        ]
        + [pl.BlockSpec((block, group), lambda i, o: (row(i), 0))] * count,
        [
            struct((rows, width), f32),
            struct((rows, width), bf16),
        ]
        + [struct((rows, group), bf16)] * count,
        2 * rows * width * hidden_cols + 2 * rows * width * width,
        2 * (rows + width) * hidden_cols + 16 * rows * width,
        scratch=[pltpu.VMEM((rows, width), f32)],
        prefetch=1,
    )(order, *grads, *[weights] * (n_grads + parts), residual, cotangent, gain_row)


def products(select, lefts, rights, parts, added=None, joined=False, halves=None):
    height = lefts[0].shape[0]
    block = min(256, height) if halves is None else height // 4
    n = len(rights)
    sizes = [r.shape[1] // p for r, p in zip(rights, parts)]
    added = added or []
    distinct = []
    for left in lefts:
        if not any(left is d for d in distinct):
            distinct.append(left)
    which = [next(i for i, d in enumerate(distinct) if d is left) for left in lefts]
    n_left, n_add = len(distinct), len(added)

    def kernel(select_ref, *refs):
        l_refs, r_refs, outs = refs[:n_left], refs[n_left : n_left + n], refs[n_left + n + n_add :]
        def product(k):
            total = dot(l_refs[which[k]][...], r_refs[k][...])
            if k < n_add:
                total = total + refs[n_left + n + k][...].astype(f32)
            return total.astype(bf16)

        for k in range(n):
            if halves is not None:
                step, mine = pl.program_id(0), select_ref[1 + k]
                keep = (step // 2 if halves[k] == 0 else step % 2) == mine
                for cond, out in ((keep, outs[k]), (jnp.logical_not(keep), outs[n + k])):
                    @pl.when(cond)
                    def _():
                        out[...] = product(k)
            elif joined:
                start = sum(sizes[:k])
                outs[0][:, start : start + sizes[k]] = product(k)
            else:
                outs[k][...] = product(k)

    def right_spec(k):
        return pl.BlockSpec(
            (rights[k].shape[0], sizes[k]),
            lambda i, s: (0, s[0] if parts[k] > 1 else 0),
            pipeline_mode=pl.Buffered(1),
        )

    out_sizes = [sum(sizes)] if joined else sizes
    out_specs = [pl.BlockSpec((block, size), lambda i, s: (i, 0)) for size in out_sizes]
    add_specs = out_specs[:n_add]
    out_shape = [struct((height, size), bf16) for size in out_sizes]
    if halves is not None:

        def half_spec(k, kept):
            def index(i, s):
                value = s[1 + k] if kept else 1 - s[1 + k]
                return (jnp.clip(i - 2 * value, 0, 1) if halves[k] == 0 else i // 2, 0)

            return pl.BlockSpec((block, sizes[k]), index)

        out_specs = [half_spec(k, kept) for kept in (True, False) for k in range(n)]
        out_shape = [struct((height // 2, size), bf16) for size in sizes] * 2
    return call(
        kernel,
        (height // block,),
        [pl.BlockSpec((block, d.shape[1]), lambda i, s: (i, 0)) for d in distinct]
        + [right_spec(k) for k in range(n)]
        + add_specs,
        out_specs,
        out_shape,
        sum(2 * height * r.shape[0] * size for r, size in zip(rights, sizes)),
        2 * height * sum(sizes) + sum(2 * r.shape[0] * size for r, size in zip(rights, sizes)),
        prefetch=1,
    )(select, *distinct, *rights, *added)


def finish(residual, hidden, weights, first):
    rows, width = residual.shape
    block = min(256, rows)
    hidden_cols = hidden.shape[1]

    def kernel(r_ref, h_ref, w_ref, out_ref):
        out_ref[...] = (r_ref[...] + dot_nt(h_ref[...], w_ref[...])).astype(bf16)

    rows_spec = pl.BlockSpec((block, width), lambda i: (i, 0))
    return call(
        kernel,
        (rows // block,),
        [
            rows_spec,
            pl.BlockSpec((block, hidden_cols), lambda i: (i, 0)),
            resident((width, hidden_cols), (0, first)),
        ],
        rows_spec,
        struct((rows, width), bf16),
        2 * rows * width * hidden_cols,
        6 * rows * width + 2 * (rows + width) * hidden_cols,
    )(residual, hidden, weights)


def project_back(order, slot, grads, weights, added=(), part=(0, 1), last=None, into=None):
    length, group = grads[0].shape
    width = weights.shape[0]
    piece = length // order.shape[0]
    rows = piece // part[1]
    block = min(512 if last is None else 256, rows)
    steps = rows // block
    before = part[0] * steps
    n = len(added)

    def kernel(order_ref, a_ref, b_ref, c_ref, w_ref, *refs):
        total = dot_nt(a_ref[...], w_ref[:, :group])
        total = total + dot_nt(b_ref[...], w_ref[:, group : 2 * group])
        total = total + dot_nt(c_ref[...], w_ref[:, 2 * group :])
        for ref in refs[:n]:
            total = total + ref[...].astype(f32)
        if last is not None:
            x_ref, gain_ref, g_ref = refs[n : n + 3]
            x = x_ref[...].astype(f32)
            scale = lax.rsqrt(jnp.mean(x * x, axis=-1, keepdims=True) + epsilon)
            unit = x * scale
            scaled = total * gain_ref[...]
            inner = jnp.mean(scaled * unit, axis=-1, keepdims=True)
            total = g_ref[...] + scale * (scaled - unit * inner)
        refs[-1][...] = total.astype(bf16)

    def rows_of(array):
        first = before if array.shape[0] == piece else 0
        return pl.BlockSpec((block, width), lambda i, order_ref: (i + first, 0))

    def grad_rows(i, order_ref):
        return (order_ref[slot] * (piece // block) + before + i, 0)

    inputs = [*grads, weights, *added]
    in_specs = [pl.BlockSpec((block, group), grad_rows)] * 3 + [resident(weights.shape, (0, 0))]
    in_specs += [rows_of(a) for a in added]
    aliases = {}
    out = struct((rows, width), bf16)
    if last is not None:
        out = struct((piece, width), bf16)
        inputs += last
        in_specs += [rows_of(last[0]), resident((1, width), (0, 0)), rows_of(last[2])]
        if into is not None:
            aliases = {1 + len(inputs): 0}
            inputs.append(into)
            in_specs.append(pl.BlockSpec(memory_space=pl.ANY))
    return call(
        kernel,
        (steps,),
        in_specs,
        rows_of(out),
        out,
        6 * rows * width * group,
        2 * rows * (2 * width + 3 * group),
        prefetch=1,
        aliases=aliases,
    )(order, *inputs)


def pair_add(a, b):
    return (a.astype(f32) + b.astype(f32)).astype(bf16)


def axis_bits(axis, first=1):
    bits = []
    while first < lax.axis_size(axis):
        bits.append(first)
        first *= 2
    return bits


def trade(array, dim, axis, bit):
    count = lax.axis_size(axis)
    mine = (lax.axis_index(axis) // bit) % 2
    keep = lax.dynamic_index_in_dim(array, mine, axis=dim, keepdims=False)
    give = lax.dynamic_index_in_dim(array, 1 - mine, axis=dim, keepdims=False)
    return keep, lax.ppermute(give, axis, [(i, i ^ bit) for i in range(count)])


def scatter_start(array, turn, halve_at):
    count = lax.axis_size("fsdp")
    bits = axis_bits("fsdp")
    bits = bits[turn % len(bits) :] + bits[: turn % len(bits)]
    left = axis_bits("fsdp")[::-1]
    array = array.reshape((2,) * len(bits) + (array.shape[0] // count, array.shape[1]))
    todo = [("fsdp", bit) for bit in bits]
    if halve_at is not None:
        todo[halve_at:halve_at] = [("seq", bit) for bit in axis_bits("seq", 2)]
    return exchange((array, None, todo, left))


def scatter_from(keep, give, axis, bit, left, todo, rows):
    count = lax.axis_size(axis)
    got = lax.ppermute(give, axis, [(i, i ^ bit) for i in range(count)])
    shape = (2,) * len(left) + (rows, keep.shape[1])
    return keep.reshape(shape), got.reshape(shape), todo, left


def exchange(state):
    array, _, todo, left = state
    if not todo:
        return state
    axis, bit = todo[0]
    if axis == "fsdp":
        pair = trade(array, left.index(bit), axis, bit)
        left = [b for b in left if b != bit]
    else:
        rows, n = array.shape[-2:]
        array = array.reshape(array.shape[:-2] + (2, rows // 2, n))
        pair = trade(array, array.ndim - 3, axis, bit)
    return (*pair, todo[1:], left)


def settle(states, done, ahead):
    keeps, done = lax.optimization_barrier(([state[0] for state in states], done))
    arrays = [
        keep if state[1] is None else pair_add(keep, state[1])
        for keep, state in zip(keeps, states)
    ]
    arrays, ahead = lax.optimization_barrier((arrays, ahead))
    return [(a, None) + state[2:] for a, state in zip(arrays, states)], done, ahead


def rows_whole(array, other):
    first = (lax.axis_index("seq") // 2) % 2 == 0
    return both_ways(array, other, first).reshape(-1, array.shape[1])


def last_rows(state):
    return state[0].reshape(state[0].shape[-2:])


def both_ways(own, other, first):
    return jnp.stack([jnp.where(first, own, other), jnp.where(first, other, own)])


def feedforward_ends(half, joined, other, gate_weight, up_weight, gain):
    rows, hidden_cols = gate_weight.shape
    width = joined.shape[1] - 3 * (hidden_cols // 2)
    size = hidden_cols // 2

    def kernel(half_ref, j_ref, o_ref, wg_ref, wu_ref, gain_ref, g_ref, u_ref, d_ref, out_ref, gg_ref):
        def both(k):
            columns = slice(k * size, (k + 1) * size)
            own, far = j_ref[:, columns].astype(f32), o_ref[:, columns].astype(f32)
            lower = half_ref[0] == 0
            return jnp.concatenate(
                [jnp.where(lower, own, far), jnp.where(lower, far, own)], axis=1
            )

        down, gate, up = both(0), both(1), both(2)
        g_ref[...] = gate
        u_ref[...] = up
        d_ref[...] = down.T
        out_ref[...] = j_ref[:, 3 * size :].astype(f32) + o_ref[:, 3 * size :].astype(f32)
        total = jnp.sum(
            wg_ref[...].astype(f32) * gate + wu_ref[...].astype(f32) * up, axis=1, keepdims=True
        )
        gg_ref[...] = jnp.broadcast_to(total / gain_ref[...], (rows, 128)).T[0:1, :]

    whole = lambda shape: pl.BlockSpec(shape, lambda i, h: (0, 0))
    shapes = [(rows, hidden_cols)] * 2 + [(hidden_cols, rows), (rows, width), (1, rows)]
    *ends, gain_grad = call(
        kernel,
        (1,),
        [whole(joined.shape)] * 2 + [whole(gate_weight.shape)] * 2 + [whole((rows, 1))],
        [whole(shape) for shape in shapes],
        [struct(shape, f32) for shape in shapes],
        4 * rows * hidden_cols,
        20 * rows * hidden_cols,
        prefetch=1,
    )(half, joined, other, gate_weight, up_weight, gain.astype(f32)[:, None])
    return *ends, gain_grad[0]


def projection_ends(order, pieces, weights, gain):
    rows, width = weights[0].shape
    count = len(pieces)
    group = width // count

    def kernel(order_ref, *refs):
        p_refs, refs = refs[:count], refs[count:]
        w_refs, gain_ref, outs, gg_ref = refs[:3], refs[3], refs[4:7], refs[7]
        for k in range(count):
            start = pl.multiple_of(order_ref[k] * group, group)
            for j in range(3):
                outs[j][:, pl.ds(start, group)] = p_refs[k][
                    :, j * group : (j + 1) * group
                ].astype(f32)
        total = None
        for j in range(3):
            part = jnp.sum(w_refs[j][...].astype(f32) * outs[j][...], axis=1, keepdims=True)
            total = part if total is None else total + part
        gg_ref[...] = jnp.broadcast_to(total / gain_ref[...], (rows, 128)).T[0:1, :]

    whole = lambda shape: pl.BlockSpec(shape, lambda i, o: (0, 0))
    shapes = [(rows, width)] * 3 + [(1, rows)]
    *ends, gain_grad = call(
        kernel,
        (1,),
        [whole(pieces[0].shape)] * count + [whole((rows, width))] * 3 + [whole((rows, 1))],
        [whole(shape) for shape in shapes],
        [struct(shape, f32) for shape in shapes],
        6 * rows * width,
        24 * rows * width,
        prefetch=1,
    )(order, *pieces, *weights, gain.astype(f32)[:, None])
    return *ends, gain_grad[0]


def body(
    tokens, cotangent, query_weight, key_weight, value_weight, output_weight, gate_weight, up_weight,
    down_weight, attention_gain, feedforward_gain, cache_keys, cache_values, memory_rows, memory_docs,
):
    seq_count, fsdp_count = lax.axis_size("seq"), lax.axis_size("fsdp")
    here = lax.axis_index("seq")
    tok_rows, width = tokens.shape
    head_local, rows_cache, head_dim = cache_keys.shape[1:]
    group = head_local * head_dim
    length = tok_rows * seq_count
    mem_block = length // memory_rows.shape[2]
    mem_count = memory_rows.shape[3]
    shard = query_weight.shape[0]
    hidden_cols = gate_weight.shape[1]
    order = here ^ jnp.arange(seq_count, dtype=jnp.int32)

    gains = spread(jnp.stack([attention_gain, feedforward_gain]), "fsdp")
    gains = gains.transpose(1, 0, 2).reshape(2, width).astype(f32)
    gain_one, gain_two = gains[0:1], gains[1:2]
    own_cols = [
        lax.dynamic_slice_in_dim(w, here * group, group, axis=1)
        for w in (query_weight, key_weight, value_weight)
    ]
    qkv = spread(jnp.concatenate(own_cols, axis=1), "fsdp").reshape(width, 3 * group)

    pieces = [tokens, swap_seq(tokens, 1), swap_seq(tokens, 2)]
    pieces.append(swap_seq(pieces[2], 1))

    ring = [(i, (i + 1) % fsdp_count) for i in range(fsdp_count)]
    partner_keys = lax.ppermute(cache_keys[0], "fsdp", ring)
    partner_values = lax.ppermute(cache_values[0], "fsdp", ring)

    part = shard // seq_count

    def own_rows(w):
        return lax.dynamic_slice_in_dim(w, here * part, part, axis=0)

    own_wd = lax.dynamic_slice_in_dim(down_weight, here * part, part, axis=1).T
    own_part = jnp.concatenate(
        [own_rows(gate_weight), own_rows(up_weight), own_wd, own_rows(output_weight)], axis=1
    )
    big = lax.all_gather(own_part, ("fsdp", "seq"), axis=0, tiled=True)

    half = head_dim // 2
    frequency = 10000.0 ** (-2.0 * jnp.arange(half, dtype=f32) / head_dim)
    near_count = 64
    near_angles = jnp.arange(near_count, dtype=f32)[:, None] * frequency[None, :]
    far_angles = jnp.arange(0, length, near_count).astype(f32)[:, None] * frequency[None, :]
    near_angles, far_angles = near_angles[None], far_angles[:, None]
    near_cos, near_sin, far_cos, far_sin = lax.optimization_barrier(
        (jnp.cos(near_angles), jnp.sin(near_angles), jnp.cos(far_angles), jnp.sin(far_angles))
    )
    cos_half = (far_cos * near_cos - far_sin * near_sin).reshape(length, half)
    sin_half = (far_sin * near_cos + far_cos * near_sin).reshape(length, half)
    cosine = jnp.concatenate([cos_half, cos_half], axis=1)
    sine = jnp.concatenate([-sin_half, sin_half], axis=1)
    cotangent_t = cotangent.T.reshape(fsdp_count, 2, shard // 2, tok_rows)
    cotangent_t = cotangent_t.swapaxes(0, 1).reshape(width, tok_rows)
    places = [
        (f % 4 // 2 + f % 2 * 2) * (fsdp_count // 4) + f // 4 for f in range(fsdp_count)
    ]

    chosen = memory_docs[0] * rows_cache + memory_rows[0]
    picked = retrieve(chosen, cache_keys[0], cache_values[0], 0)
    query, key, value, value_t, normed_one_t = project(
        order, pieces, qkv, gain_one, cosine, sine, head_local, head_dim
    )
    picked_keys, picked_values = retrieve(chosen, partner_keys, partner_values, rows_cache, picked)
    *attended_heads, lse = attend(
        order, query, key, value_t, picked_keys, picked_values, mem_block, mem_count, seq_count
    )

    def by_distance(stack):
        return [stack[0]] + [swap_seq(stack[k], k) for k in range(1, seq_count)]

    attended = by_distance(attended_heads)
    residual, normed_two, normed_two_t, attended_t = mix(
        order, attended, big, 3 * hidden_cols, tokens, gain_two, places
    )
    hid, gg, gu = gated(normed_two, cotangent, big, 0, hidden_cols)
    own_half, other_half = (here % 2)[None].astype(jnp.int32), (1 - here % 2)[None].astype(jnp.int32)
    lefts, rights = [cotangent_t, normed_two_t, normed_two_t], [hid, gg, gu]
    given = products(other_half, lefts, rights, (2, 2, 2))
    given, gg_later = lax.optimization_barrier((given, gg))
    got = [swap_seq(g, 1) for g in given]
    grad_residual, grad_branch, *grad_mixed = norm_back(
        order, [gg_later, gu], big, 3 * hidden_cols, residual, cotangent, gain_two
    )
    grad_heads = by_distance(grad_mixed)
    bits, upper = axis_bits("fsdp"), axis_bits("seq", 2)
    firsts = (("seq", upper[0]), ("fsdp", bits[0]), ("fsdp", bits[1]), ("fsdp", bits[-1]))
    mine = [(lax.axis_index(axis) // bit) % 2 for axis, bit in firsts]
    select = jnp.stack([here % 2, *mine]).astype(jnp.int32)
    own = products(
        select, [*lefts, attended_t], [*rights, grad_branch], (2, 2, 2, 1), got, halves=(0, 0, 1, 0)
    )
    grad_heads, own = lax.optimization_barrier((grad_heads, own))
    down = bits[::-1]
    over = lambda *picks: [("fsdp", b) if b else ("seq", upper[0]) for b in picks]
    sums = [
        scatter_from(keep, give, axis, bit, left, todo, rows)
        for keep, give, (axis, bit), left, todo, rows in zip(
            own[:4],
            own[4:],
            firsts,
            (down, [bits[1], *down[: -2]], [bits[0], *down[: -2]], down[1:]),
            (
                over(*bits),
                over(0, *bits[1:]),
                over(0, *bits[2:], bits[0]),
                over(bits[0], 0, *bits[1:-1]),
            ),
            (shard // 2, shard, shard, shard),
        )
    ]

    blocks = lse.shape[0]
    middle = 3 * blocks // 8
    attention = (order, query, key, value, picked_keys, picked_values, mem_block, mem_count)
    *grads, rest, delta = attend_back(
        *attention, grad_heads, attended_heads, lse, cosine, sine, 0, middle
    )
    sums, _, (rest, delta) = settle(sums, (), (rest, delta))
    sums = [exchange(g) for g in sums]
    grads = attend_back(
        *attention, grad_heads, None, lse, cosine, sine, middle, blocks, (rest, delta, *grads)
    )

    zero = jnp.zeros((1,), jnp.int32)
    sums, _, grads = settle(sums, (), grads)
    sums = [exchange(g) for g in sums]
    far_part = project_back(order, 3, grads, qkv)
    far = swap_seq(far_part, 1)
    far_part, grads = lax.optimization_barrier((far_part, grads))
    near_part = project_back(order, 1, grads, qkv)
    near = swap_seq(near_part, 1)
    far, near_part, grads = lax.optimization_barrier((far, near_part, grads))
    half = project_back(order, 2, grads, qkv, [far], (0, 2))
    across = [swap_seq(half, 2)]
    half, grads = lax.optimization_barrier((half, grads))
    (qkv_grad,) = products(zero, [normed_one_t] * 3, list(grads), (1, 1, 1), joined=True)
    qkv_state = scatter_start(qkv_grad, 0, None)
    qkv_grad, grads = lax.optimization_barrier((qkv_grad, grads))
    half = project_back(order, 2, grads, qkv, [far], (1, 2))
    across.append(swap_seq(half, 2))
    across[0], half, grads = lax.optimization_barrier((across[0], half, grads))
    sums, across[0], near = settle(sums, across[0], near)
    sums = [exchange(g) for g in sums]
    (qkv_state, *sums), _, near = settle([qkv_state, *sums], (), near)
    while any(state[2] for state in sums):
        sums = settle([exchange(g) for g in sums], (), ())[0]
    qkv_state = exchange(qkv_state)
    joined = jnp.concatenate([last_rows(state) for state in sums], axis=1)
    lower = swap_seq(joined, upper[0])
    last = (tokens, gain_one, grad_residual)
    grad_tokens = project_back(order, 0, grads, qkv, [near, across[0]], (0, 2), last)
    (qkv_state,), grad_tokens, (hid, across[1]) = settle(
        [qkv_state], grad_tokens, (hid, across[1])
    )
    qkv_state = exchange(qkv_state)
    result = finish(residual, hid, big, 2)
    grad_tokens = project_back(
        order, 0, grads, qkv, [near, across[1]], (1, 2), last, grad_tokens
    )
    joined, grad_tokens = lax.optimization_barrier((joined, grad_tokens))
    joined = rows_whole(joined, lower)
    other = swap_seq(joined, 1)
    (qkv_state,), _, _ = settle([qkv_state], (result, grad_tokens), ())
    while qkv_state[2]:
        qkv_state = settle([exchange(qkv_state)], (), ())[0][0]
    qkv_pieces = by_distance([last_rows(qkv_state)] * seq_count)
    grad_gate, grad_up, grad_down, grad_out, grad_gain_two = feedforward_ends(
        own_half, joined, other, gate_weight, up_weight, feedforward_gain
    )
    qkv_pieces[0], grad_out = lax.optimization_barrier((qkv_pieces[0], grad_out))
    grad_q, grad_k, grad_v, grad_gain_one = projection_ends(
        order, qkv_pieces, (query_weight, key_weight, value_weight), attention_gain
    )
    return (
        result,
        grad_tokens,
        grad_q,
        grad_k,
        grad_v,
        grad_out,
        grad_gate,
        grad_up,
        grad_down,
        grad_gain_one,
        grad_gain_two,
    )


def solution(mesh):
    tok, row, col, one = P(("fsdp", "seq"), None), P("fsdp", None), P(None, "fsdp"), P("fsdp")
    cache = P("fsdp", "seq", None, None)
    return jax.shard_map(
        body,
        mesh=mesh,
        in_specs=(tok, tok) + (row,) * 6 + (col, one, one) + (cache,) * 4,
        out_specs=(tok, tok) + (row,) * 6 + (col, one, one),
        check_vma=False,
    )
```
